256 devices in a mesh: gx: 32 (over y_hi, z, core), gy: 8 (over x, y_lo).
Axes of the slice: x: 4, y: 4 (y_hi: 2, y_lo: 2; y = y_hi * 2 + y_lo), z: 8, core: 2. Of those that a mesh axis runs over, the one named last changes fastest.
Arguments:
- charge: float32 [1024, 8192], P('gx', 'gy'), may hold values from -8 to 8
Outputs:
- potential: float32 [1024, 8192], P('gx', 'gy')
The draws below stay inside these ranges and needn't reach their ends.
All inputs are finite; a program needn't handle non-finite values.
Results may differ from the reference program's by a relative error of at most 0.0003.
Values sent between devices are 32-bit elements; how exact they have to be, the bound alone decides.
No kernel may reach another device: no remote copies, remote signals or barrier semaphores. Data moves between devices by JAX's collectives and lax.ppermute only.
A program may use at most 128 MiB of HBM per device.

```python
import jax
import jax.numpy as jnp
from jax import lax

P_SIZE = 32
W = 16
Q = 4
NL = 16
NX = 1024
NY = 256
N_GX = 32
N_GY = 8


def draw_charge(key, part):
    key_values = jax.random.fold_in(key, 0)
    extent = (NX, NY * P_SIZE)
    return jnp.clip(jax.random.normal(key_values, extent, jnp.float32), -8.0, 8.0)


def setup_inputs(seed: int = 0) -> dict:
    streams_of = jax.random.split(jax.random.key(seed), 2)
    return {
        "charge": draw_charge(jax.random.fold_in(streams_of[1], 71), 0),
    }


highest = lax.Precision.HIGHEST

def product(left, right):
    return jnp.matmul(left, right, precision=highest)

def sine_table(length):
    counter = jnp.arange(length, dtype=jnp.int32) + 1
    multiple = counter[:, None] * counter[None, :] % (2 * (length + 1))
    return jnp.sin(jnp.pi * multiple.astype(jnp.float32) / (length + 1))

def eigen_values(length):
    counter = (jnp.arange(length, dtype=jnp.int32) + 1).astype(jnp.float32)
    return 2.0 - 2.0 * jnp.cos(jnp.pi * counter / (length + 1))

def interp_table(fine_start, fine_count, coarse_start, coarse_count, ratio):
    fine_pos = jnp.arange(fine_count, dtype=jnp.int32) + fine_start
    coarse_pos = jnp.arange(coarse_count, dtype=jnp.int32) + coarse_start
    numerator = 2 * fine_pos - (ratio - 1)
    lower_index = numerator // (2 * ratio)
    weight = ((numerator - 2 * ratio * lower_index).astype(jnp.float32) / (2 * ratio))[:, None]
    below = (coarse_pos[None, :] == lower_index[:, None]).astype(jnp.float32)
    above = (coarse_pos[None, :] == lower_index[:, None] + 1).astype(jnp.float32)
    return below * (1.0 - weight) + above * weight

def legendre_basis(length, count):
    points = (2.0 * jnp.arange(length, dtype=jnp.int32).astype(jnp.float32) + 1.0) / length - 1.0
    columns = [jnp.ones_like(points), points]
    for degree in range(2, count):
        columns.append(((2 * degree - 1) * points * columns[-1] - (degree - 1) * columns[-2]) / degree)
    columns = columns[:count]
    result = []
    for column in columns:
        vector = column
        for passes in range(2):
            for earlier in result:
                vector = vector - jnp.sum(earlier * vector) * earlier
        vector = vector / jnp.sqrt(jnp.sum(vector * vector))
        result.append(vector)
    return jnp.stack(result, axis=1)

def along_three(volume, first_table, second_table, third_table):
    volume = jnp.einsum('ai,ijk->ajk', first_table, volume, precision=highest)
    volume = jnp.einsum('bj,ijk->ibk', second_table, volume, precision=highest)
    return jnp.einsum('ck,ijk->ijc', third_table, volume, precision=highest)

def box_solve(patch):
    length = patch.shape[0] + 2 * W
    padded = jnp.pad(patch, W)
    table = sine_table(length)
    values = eigen_values(length)
    spectrum = along_three(padded, table, table, table)
    spectrum = spectrum / (values[:, None, None] + values[None, :, None] + values[None, None, :])
    return along_three(spectrum, table, table, table) * (2.0 / (length + 1)) ** 3

def coarse_charge(local):
    blocks = local.shape[0] // Q
    samples = local.reshape(blocks, Q, blocks, Q, blocks, Q).mean(axis=(1, 3, 5))
    padded = jnp.pad(samples, 1)
    beside = padded[2:, 1:-1, 1:-1] + padded[:-2, 1:-1, 1:-1]
    beside = beside + padded[1:-1, 2:, 1:-1] + padded[1:-1, :-2, 1:-1]
    beside = beside + padded[1:-1, 1:-1, 2:] + padded[1:-1, 1:-1, :-2]
    return (samples, (6.0 * samples - beside) / (Q * Q))

def face_planes(local, samples):
    length = local.shape[0]
    inner = length - 2 * W
    fine_table = interp_table(0, length, 0, samples.shape[0], Q)
    middle = fine_table[W:W + inner]

    def across_x(index):
        coarse_plane = jnp.einsum('j,jkl->kl', fine_table[index], samples, precision=highest)
        return local[index, W:W + inner, W:W + inner] - product(product(middle, coarse_plane), middle.T)

    def across_y(index):
        coarse_plane = jnp.einsum('k,jkl->jl', fine_table[index], samples, precision=highest)
        return local[W:W + inner, index, W:W + inner] - product(product(middle, coarse_plane), middle.T)
    own = jnp.stack([across_x(W - 1), across_x(W + inner), across_y(W - 1), across_y(W + inner)])
    outgoing = jnp.stack([across_x(W), across_x(W + inner - 1), across_y(W), across_y(W + inner - 1)])
    return (own, outgoing)

def coefficients(planes, basis):
    return jnp.einsum('ia,nij,jb->nab', basis, planes, basis, precision=highest)

def expand(coefs, basis):
    return jnp.einsum('ia,nab,jb->nij', basis, coefs, basis, precision=highest)

def coarse_faces(block, inner):
    cells = block.shape[2]
    edge = interp_table(-1, inner + 2, -1, cells + 2, Q)
    depth = interp_table(0, inner, 0, cells, Q)
    lateral = edge[1:inner + 1]

    def spread(plane):
        return product(product(lateral, plane), depth.T)
    return jnp.stack([spread(jnp.einsum('e,efk->fk', edge[0], block, precision=highest)), spread(jnp.einsum('e,efk->fk', edge[inner + 1], block, precision=highest)), spread(jnp.einsum('f,efk->ek', edge[0], block, precision=highest)), spread(jnp.einsum('f,efk->ek', edge[inner + 1], block, precision=highest))])

def dirichlet_solve(patch, faces):
    inner = patch.shape[0]
    source = patch.at[0].add(faces[0]).at[inner - 1].add(faces[1])
    source = source.at[:, 0].add(faces[2]).at[:, inner - 1].add(faces[3])
    table = sine_table(inner)
    values = eigen_values(inner)
    spectrum = along_three(source, table, table, table)
    spectrum = spectrum / (values[:, None, None] + values[None, :, None] + values[None, None, :])
    return along_three(spectrum, table, table, table) * (2.0 / (inner + 1)) ** 3

def coarse_solve(source):
    size_x, size_y, size_z = source.shape
    table_x = sine_table(size_x)
    table_y = sine_table(size_y)
    table_z = sine_table(size_z)
    values_x = eigen_values(size_x)
    values_y = eigen_values(size_y)
    values_z = eigen_values(size_z)
    spectrum = along_three(source, table_x, table_y, table_z)
    spectrum = spectrum * (Q * Q) / (values_x[:, None, None] + values_y[None, :, None] + values_z[None, None, :])
    scale = 2.0 / (size_x + 1) * (2.0 / (size_y + 1)) * (2.0 / (size_z + 1))
    return along_three(spectrum, table_x, table_y, table_z) * scale

def reference(charge):
    inner = P_SIZE
    cells = inner // Q
    margin_coarse = W // Q
    count = N_GX * N_GY
    patches = charge.reshape(N_GX, inner, N_GY, inner, inner).transpose(0, 2, 1, 3, 4).reshape(count, inner, inner, inner)
    basis = legendre_basis(inner, NL)

    def first_pass(patch):
        local = box_solve(patch)
        samples, spill = coarse_charge(local)
        own, outgoing = face_planes(local, samples)
        return (spill[:, :, margin_coarse:margin_coarse + cells], coefficients(own, basis), coefficients(outgoing, basis))
    spills, own_coefs, sent_coefs = lax.map(first_pass, patches)
    span = spills.shape[1]
    total = jnp.zeros((N_GX * cells + 2 * margin_coarse, N_GY * cells + 2 * margin_coarse, cells), jnp.float32)

    def deposit(index, total):
        index = index.astype(jnp.int32)
        start_x = (index // N_GY * cells).astype(jnp.int32)
        start_y = (index % N_GY * cells).astype(jnp.int32)
        anchor = jnp.zeros((), jnp.int32)
        current = lax.dynamic_slice(total, (start_x, start_y, anchor), (span, span, cells))
        return lax.dynamic_update_slice(total, current + spills[index], (start_x, start_y, anchor))
    total = lax.fori_loop(0, count, deposit, total)
    source = total[margin_coarse:margin_coarse + N_GX * cells, margin_coarse:margin_coarse + N_GY * cells]
    coarse = coarse_solve(source)
    rimmed = jnp.pad(coarse, ((1, 1), (1, 1), (0, 0)))
    grid_sent = sent_coefs.reshape(N_GX, N_GY, 4, NL, NL)
    no_pad = (0, 0)
    from_left = jnp.pad(grid_sent[:, :, 1], ((1, 0), no_pad, no_pad, no_pad))[:-1]
    from_right = jnp.pad(grid_sent[:, :, 0], ((0, 1), no_pad, no_pad, no_pad))[1:]
    from_below = jnp.pad(grid_sent[:, :, 3], (no_pad, (1, 0), no_pad, no_pad))[:, :-1]
    from_above = jnp.pad(grid_sent[:, :, 2], (no_pad, (0, 1), no_pad, no_pad))[:, 1:]
    received = jnp.stack([from_left, from_right, from_below, from_above], axis=2).reshape(count, 4, NL, NL)

    def second_pass(items):
        patch, own, incoming, index = items
        start_x = (index // N_GY * cells).astype(jnp.int32)
        start_y = (index % N_GY * cells).astype(jnp.int32)
        anchor = jnp.zeros((), jnp.int32)
        block = lax.dynamic_slice(rimmed, (start_x, start_y, anchor), (cells + 2, cells + 2, cells))
        faces = coarse_faces(block, inner) + expand(own + incoming, basis)
        return dirichlet_solve(patch, faces)
    solved = lax.map(second_pass, (patches, own_coefs, received, jnp.arange(count, dtype=jnp.int32)))
    return solved.reshape(N_GX, N_GY, inner, inner, inner).transpose(0, 2, 1, 3, 4).reshape(charge.shape)
```

```python
import jax
import jax.numpy as jnp
import numpy as np
from jax import lax
from jax.sharding import PartitionSpec as P

P_SIZE = 32
W = 16
Q = 4
NL = 16


highest = lax.Precision.HIGHEST


def extended(shard, sides, width):
    for axis, dim in sides:
        peers, length = (lax.axis_size(axis), shard.shape[dim])
        up = [(i, (i + 1) % peers) for i in range(peers - 1)]
        down = [(j, i) for i, j in up]
        last = lax.slice_in_dim(shard, length - width, length, axis=dim)
        first = lax.slice_in_dim(shard, 0, width, axis=dim)
        before = lax.ppermute(last, axis, up)
        after = lax.ppermute(first, axis, down)
        shard = jnp.concatenate([before, shard, after], axis=dim)
    return shard


def extended_2(shard, sides, width):
    edges = {}
    for axis, dim in sides:
        peers, length = (lax.axis_size(axis), shard.shape[dim])
        up = [(i, (i + 1) % peers) for i in range(peers - 1)]
        last = lax.slice_in_dim(shard, length - width, length, axis=dim)
        first = lax.slice_in_dim(shard, 0, width, axis=dim)
        edges[dim] = (
            lax.ppermute(last, axis, up),
            lax.ppermute(first, axis, [(b, a) for a, b in up]),
        )
    done = []
    for _, dim in sides:
        low, high = edges[dim]
        around = [(width, width) if d in done else (0, 0) for d in range(shard.ndim)]
        shard = jnp.concatenate([jnp.pad(low, around), shard, jnp.pad(high, around)], axis=dim)
        done.append(dim)
    return shard


def product(left, right):
    return jnp.matmul(left, right, precision=highest)


def sine_table(length):
    counter = np.arange(length) + 1
    multiple = counter[:, None] * counter[None, :] % (2 * (length + 1))
    return jnp.asarray(np.sin(np.pi * multiple / (length + 1)), jnp.float32)


def eigen_values(length):
    counter = np.arange(length) + 1
    return jnp.asarray(2.0 - 2.0 * np.cos(np.pi * counter / (length + 1)), jnp.float32)


def interp_table(fine_start, fine_count, coarse_start, coarse_count, ratio):
    fine_pos = np.arange(fine_count) + fine_start
    coarse_pos = np.arange(coarse_count) + coarse_start
    numerator = 2 * fine_pos - (ratio - 1)
    lower_index = numerator // (2 * ratio)
    weight = ((numerator - 2 * ratio * lower_index) / (2.0 * ratio))[:, None]
    below = (coarse_pos[None, :] == lower_index[:, None]).astype(np.float64)
    above = (coarse_pos[None, :] == lower_index[:, None] + 1).astype(np.float64)
    return jnp.asarray(below * (1.0 - weight) + above * weight, jnp.float32)


def legendre_basis(length, count):
    points = (2.0 * np.arange(length) + 1.0) / length - 1.0
    columns = [np.ones_like(points), points]
    for degree in range(2, count):
        columns.append(
            ((2 * degree - 1) * points * columns[-1] - (degree - 1) * columns[-2]) / degree
        )
    columns = columns[:count]
    result = []
    for column in columns:
        vector = column
        for passes in range(2):
            for earlier in result:
                vector = vector - np.sum(earlier * vector) * earlier
        vector = vector / np.sqrt(np.sum(vector * vector))
        result.append(vector)
    return jnp.asarray(np.stack(result, axis=1), jnp.float32)


def along_three(volume, first_table, second_table, third_table):
    volume = jnp.einsum("ai,ijk->ajk", first_table, volume, precision=highest)
    volume = jnp.einsum("bj,ijk->ibk", second_table, volume, precision=highest)
    return jnp.einsum("ck,ijk->ijc", third_table, volume, precision=highest)


def box_solve(patch):
    length = patch.shape[0] + 2 * W
    padded = jnp.pad(patch, W)
    table = sine_table(length)
    values = eigen_values(length)
    spectrum = along_three(padded, table, table, table)
    spectrum = spectrum / (values[:, None, None] + values[None, :, None] + values[None, None, :])
    return along_three(spectrum, table, table, table) * (2.0 / (length + 1)) ** 3


def coarse_charge(local):
    blocks = local.shape[0] // Q
    samples = local.reshape(blocks, Q, blocks, Q, blocks, Q).mean(axis=(1, 3, 5))
    padded = jnp.pad(samples, 1)
    beside = padded[2:, 1:-1, 1:-1] + padded[:-2, 1:-1, 1:-1]
    beside = beside + padded[1:-1, 2:, 1:-1] + padded[1:-1, :-2, 1:-1]
    beside = beside + padded[1:-1, 1:-1, 2:] + padded[1:-1, 1:-1, :-2]
    return (samples, (6.0 * samples - beside) / (Q * Q))


def face_planes(local, samples):
    length = local.shape[0]
    inner = length - 2 * W
    fine_table = interp_table(0, length, 0, samples.shape[0], Q)
    middle = fine_table[W : W + inner]

    def across_x(index):
        coarse_plane = jnp.einsum("j,jkl->kl", fine_table[index], samples, precision=highest)
        return local[index, W : W + inner, W : W + inner] - product(
            product(middle, coarse_plane), middle.T
        )

    def across_y(index):
        coarse_plane = jnp.einsum("k,jkl->jl", fine_table[index], samples, precision=highest)
        return local[W : W + inner, index, W : W + inner] - product(
            product(middle, coarse_plane), middle.T
        )

    own = jnp.stack([across_x(W - 1), across_x(W + inner), across_y(W - 1), across_y(W + inner)])
    outgoing = jnp.stack(
        [across_x(W), across_x(W + inner - 1), across_y(W), across_y(W + inner - 1)]
    )
    return (own, outgoing)


def coefficients(planes, basis):
    return jnp.einsum("ia,nij,jb->nab", basis, planes, basis, precision=highest)


def expand(coefs, basis):
    return jnp.einsum("ia,nab,jb->nij", basis, coefs, basis, precision=highest)


def coarse_faces(block, inner):
    cells = block.shape[2]
    edge = interp_table(-1, inner + 2, -1, cells + 2, Q)
    depth = interp_table(0, inner, 0, cells, Q)
    lateral = edge[1 : inner + 1]

    def spread(plane):
        return product(product(lateral, plane), depth.T)

    return jnp.stack(
        [
            spread(jnp.einsum("e,efk->fk", edge[0], block, precision=highest)),
            spread(jnp.einsum("e,efk->fk", edge[inner + 1], block, precision=highest)),
            spread(jnp.einsum("f,efk->ek", edge[0], block, precision=highest)),
            spread(jnp.einsum("f,efk->ek", edge[inner + 1], block, precision=highest)),
        ]
    )


def dirichlet_solve(patch, faces):
    inner = patch.shape[0]
    source = patch.at[0].add(faces[0]).at[inner - 1].add(faces[1])
    source = source.at[:, 0].add(faces[2]).at[:, inner - 1].add(faces[3])
    table = sine_table(inner)
    values = eigen_values(inner)
    spectrum = along_three(source, table, table, table)
    spectrum = spectrum / (values[:, None, None] + values[None, :, None] + values[None, None, :])
    return along_three(spectrum, table, table, table) * (2.0 / (inner + 1)) ** 3


def fold_table(cells, span, margin):
    row_index = jnp.arange(cells, dtype=jnp.int32)[:, None]
    col_index = jnp.arange(span + 2 * margin, dtype=jnp.int32)[None, :]
    centre = (col_index == row_index + 2 * margin).astype(jnp.float32)
    left_part = ((col_index == row_index) & (row_index < margin)).astype(jnp.float32)
    right_part = ((col_index == row_index + 4 * margin) & (row_index >= cells - margin)).astype(
        jnp.float32
    )
    return centre + left_part + right_part


def arrange(items):
    return jnp.stack([jnp.stack([items[2], items[0]]), jnp.stack([items[1], items[3]])])


def pick(arrived):
    return jnp.stack([arrived[0, 1], arrived[3, 2], arrived[2, 0], arrived[1, 3]])


def body(charge):
    inner = P_SIZE
    patch = charge.reshape(inner, inner, inner)
    cells = inner // Q
    margin_coarse = W // Q
    count_x = lax.axis_size("gx")
    count_y = lax.axis_size("gy")
    basis = legendre_basis(inner, NL)
    local = box_solve(patch)
    samples, spill = coarse_charge(local)
    spill = spill[:, :, margin_coarse : margin_coarse + cells]
    span = spill.shape[0]
    widened = extended(spill, (("gx", 0), ("gy", 1)), margin_coarse)
    fold = fold_table(cells, span, margin_coarse)
    source = jnp.einsum("ai,bj,ijk->abk", fold, fold, widened, precision=highest)
    slab_depth = cells // count_y
    total_x = cells * count_x
    total_y = cells * count_y
    width_y = total_y // count_x
    table_x = sine_table(total_x)
    table_y = sine_table(total_y)
    table_z = sine_table(cells)
    section = jnp.einsum("ck,ijk->ijc", table_z, source, precision=highest)
    slab = lax.all_to_all(section, "gy", split_axis=2, concat_axis=1, tiled=True)
    slab = jnp.einsum("bj,ijk->ibk", table_y, slab, precision=highest)
    pencil = lax.all_to_all(slab, "gx", split_axis=1, concat_axis=0, tiled=True)
    pencil = jnp.einsum("ai,ijk->ajk", table_x, pencil, precision=highest)
    values_x = eigen_values(total_x)
    values_y = lax.dynamic_slice_in_dim(
        eigen_values(total_y), lax.axis_index("gx") * width_y, width_y, 0
    )
    values_z = lax.dynamic_slice_in_dim(
        eigen_values(cells), lax.axis_index("gy") * slab_depth, slab_depth, 0
    )
    pencil = (
        pencil
        * (Q * Q)
        / (values_x[:, None, None] + values_y[None, :, None] + values_z[None, None, :])
    )
    pencil = jnp.einsum("ai,ijk->ajk", table_x, pencil, precision=highest) * (2.0 / (total_x + 1))
    returned = lax.all_to_all(pencil, "gx", split_axis=0, concat_axis=1, tiled=True)
    returned = jnp.einsum("bj,ijk->ibk", table_y, returned, precision=highest) * (
        2.0 / (total_y + 1)
    )
    block = lax.all_to_all(returned, "gy", split_axis=1, concat_axis=2, tiled=True)
    coarse = jnp.einsum("ck,ijk->ijc", table_z, block, precision=highest) * (2.0 / (cells + 1))
    rimmed = extended(coarse, (("gx", 0), ("gy", 1)), 1)
    own_planes, outgoing = face_planes(local, samples)
    own_coefs = coefficients(own_planes, basis)
    faces = coarse_faces(rimmed, inner)
    sent_coefs = coefficients(outgoing, basis)
    arrived = extended_2(arrange(sent_coefs.reshape(4, NL * NL)), (("gx", 0), ("gy", 1)), 1)
    faces = faces + expand(own_coefs + pick(arrived).reshape(4, NL, NL), basis)
    return dirichlet_solve(patch, faces).reshape(inner, inner * inner)


def solution(mesh):
    in_specs = (P("gx", "gy"),)
    out_specs = P("gx", "gy")
    return jax.shard_map(body, mesh=mesh, in_specs=in_specs, out_specs=out_specs, check_vma=False)
```

```python
import functools

import jax
import jax.numpy as jnp
import ml_dtypes
import numpy as np
from jax import lax
from jax.experimental import pallas as pl
from jax.experimental.pallas import tpu as pltpu
from jax.sharding import PartitionSpec as P

P_SIZE = 32
W = 16
Q = 4
NL = 16
N_GX = 32
N_GY = 8
CELLS = P_SIZE // Q
VMEM_LIMIT = 56 * 1024 * 1024
BF16 = jnp.bfloat16
F32 = jnp.float32


def sine(length):
    counter = np.arange(length) + 1
    multiple = counter[:, None] * counter[None, :] % (2 * (length + 1))
    return np.sin(np.pi * multiple / (length + 1))


def eigen(length):
    return 2.0 - 2.0 * np.cos(np.pi * (np.arange(length) + 1) / (length + 1))


def interp(fine_start, fine_count, coarse_start, coarse_count, ratio):
    fine_pos = np.arange(fine_count) + fine_start
    coarse_pos = np.arange(coarse_count) + coarse_start
    numerator = 2 * fine_pos - (ratio - 1)
    lower_index = numerator // (2 * ratio)
    weight = ((numerator - 2 * ratio * lower_index) / (2.0 * ratio))[:, None]
    below = (coarse_pos[None, :] == lower_index[:, None]).astype(np.float64)
    above = (coarse_pos[None, :] == lower_index[:, None] + 1).astype(np.float64)
    return below * (1.0 - weight) + above * weight


def legendre(length, count):
    points = (2.0 * np.arange(length) + 1.0) / length - 1.0
    columns = [np.ones_like(points), points]
    for degree in range(2, count):
        columns.append(
            ((2 * degree - 1) * points * columns[-1] - (degree - 1) * columns[-2]) / degree
        )
    result = []
    for column in columns[:count]:
        vector = column
        for _ in range(2):
            for earlier in result:
                vector = vector - np.sum(earlier * vector) * earlier
        result.append(vector / np.sqrt(np.sum(vector * vector)))
    return np.stack(result, axis=1)


def columns_at(table, positions):
    positions = np.asarray(positions)
    inside = (positions >= 0) & (positions < table.shape[1])
    return table[:, np.clip(positions, 0, table.shape[1] - 1)] * inside


def pair(table):
    table = np.asarray(table, np.float64)
    high = table.astype(np.float32).astype(ml_dtypes.bfloat16)
    low = (table - high.astype(np.float64)).astype(np.float32).astype(ml_dtypes.bfloat16)
    return np.stack([high, low], axis=-3)


@functools.lru_cache(None)
def tables():
    t = {}
    n = P_SIZE + 2 * W
    s64, m64 = sine(n), eigen(n)
    s32, m32 = sine(P_SIZE), eigen(P_SIZE)
    s8, m8 = sine(CELLS), eigen(CELLS)
    nx, ny = CELLS * N_GX, CELLS * N_GY
    sx, mx = sine(nx), eigen(nx)
    sy, my = sine(ny), eigen(ny)
    eye = np.eye
    basis = legendre(P_SIZE, NL)
    fine = interp(0, n, 0, n // Q, Q)
    mean = np.kron(eye(n // Q), np.full((1, Q), 1.0 / Q))
    inside = slice(W, W + P_SIZE)
    places = [W - 1, W + P_SIZE, W, W + P_SIZE - 1]
    r = mean @ s64
    bs = basis.T @ s64[inside]
    st = s64[places]
    bl = basis.T @ fine[inside]
    lt = fine[places]
    slot_x, slot_y = [0, 1, 4, 5], [2, 3, 6, 7]
    sc = s64[:, inside]
    t["sc"] = pair(sc)
    t["bd"] = pair(np.kron(eye(4), sc.T))
    kx = m64.reshape(16, 1, 4, 1)
    rm = (2.0 / (n + 1)) ** 3 / (kx + m64.reshape(1, n, 1, 1) + m64.reshape(1, 1, 1, n))
    t["rm"] = rm.reshape(16 * n, 4 * n).astype(np.float32)
    ty = np.zeros((4, n, 256))
    for i in range(4):
        ty[i, :, i * 16 : i * 16 + 16] = r.T
        ty[i, :, 64 + i * 16 : 64 + i * 16 + 16] = bs.T
        ty[i, :, 128 + i * 4 : 128 + i * 4 + 4] = st.T
    t["ty"] = pair(ty.reshape(4 * n, 256))
    t["tz"] = pair(np.kron(eye(4), np.concatenate([r, bs], axis=0)))
    t["tx1"] = pair(np.kron(r.T, eye(16)))
    tx2 = np.zeros((n, NL, 8, NL))
    tx3 = np.zeros((n, 4, 8, NL))
    kl = np.zeros((16, 16, 8, NL))
    for i in range(4):
        tx2[:, :, slot_x[i], :] = st[i][:, None, None] * eye(NL)
        tx3[:, i, slot_y[i], :] = bs.T
        kl[:, :, slot_x[i], :] = lt[i][:, None, None] * bl.T[None]
        kl[:, :, slot_y[i], :] = bl.T[:, None, :] * lt[i][None, :, None]
    t["tx2"] = pair(tx2.reshape(n * NL, 128))
    t["tx3"] = pair(tx3.reshape(n * 4, 128))
    t["kl"] = pair(kl.reshape(256, 128))
    first = W // Q
    u1 = np.zeros((CELLS, 16))
    u2 = np.zeros((CELLS, 16))
    for k in range(CELLS):
        u1[:, k + first] += s8[:, k]
        u2[:, k + first - 1] -= s8[:, k] / (Q * Q)
        u2[:, k + first + 1] -= s8[:, k] / (Q * Q)
    t["u"] = pair(np.concatenate([u1, u2, bl], axis=0))
    beside = eye(16, k=1) + eye(16, k=-1)
    k1 = 6.0 * eye(256) - np.kron(beside, eye(16)) - np.kron(eye(16), beside)
    t["k1"] = pair(k1 / (Q * Q))
    tb = [np.tile(columns_at(sy, np.arange(16) + b * CELLS - first).T, (1, CELLS)) for b in range(N_GY)]
    t["tb"] = pair(np.stack(tb))
    ta = [np.repeat(columns_at(sx, np.arange(16) + a * CELLS - first), CELLS, axis=1) for a in range(N_GX)]
    t["ta"] = pair(np.stack(ta))
    scale = Q * Q * (2.0 / (nx + 1)) * (2.0 / (ny + 1)) * (2.0 / (CELLS + 1))
    wc = scale / (mx.reshape(nx, 1, 1) + m8.reshape(1, CELLS, 1) + my.reshape(1, 1, ny))
    t["wc"] = wc.reshape(nx, CELLS * ny).astype(np.float32)
    edge = interp(-1, P_SIZE + 2, -1, CELLS + 2, Q)
    ends = edge[[0, P_SIZE + 1]]
    lateral = edge[1 : P_SIZE + 1]
    depth = interp(0, P_SIZE, 0, CELLS, Q)
    around = np.arange(CELLS + 2) - 1
    y_near = np.stack([columns_at(sy, around + b * CELLS) for b in range(N_GY)], axis=1)
    x_near = np.stack([columns_at(sx, around + a * CELLS) for a in range(N_GX)], axis=1)
    tf = np.zeros((CELLS, ny, N_GY, 2, CELLS))
    tc = np.zeros((4, ny, N_GY, 16, 4))
    y_ends = np.einsum("fe,ybe->ybf", ends, y_near)
    for k in range(CELLS):
        tf[k, :, :, :, k] = y_ends
    for k in range(4):
        tc[k, :, :, : CELLS + 2, k] = y_near
    t["tf"] = pair(tf.reshape(CELLS * ny, 128))
    t["tc"] = pair(tc.reshape(4 * ny, 512))
    t["ec"] = pair(x_near.transpose(2, 1, 0).reshape((CELLS + 2) * N_GX, nx))
    t["ef"] = pair(np.einsum("fe,xae->fax", ends, x_near).reshape(2 * N_GX, nx))
    t["s32"] = pair(s32)
    t["bd32"] = pair(np.kron(eye(4), s32))
    rm32 = m32.reshape(8, 1, 4, 1) + m32.reshape(1, 32, 1, 1) + m32.reshape(1, 1, 1, 32)
    t["rm32"] = ((2.0 / (P_SIZE + 1)) ** 3 / rm32).reshape(256, 128).astype(np.float32)
    t["sbz"] = pair(s32 @ basis)
    lz = s32 @ depth @ s8
    lane = np.arange(128)
    t["lz"] = np.stack([lz[:, lane // 64 * 4 + lane % 4], lz[:, lane % 8]]).astype(np.float32)
    sel = np.zeros((N_GY, 4, 128, 128), np.float32)
    for b in range(N_GY):
        for f in range(2):
            for i in range(128):
                where_x = i % 64 // 4
                where_y = (i // 8 - 2 * b - f) % 16
                if where_x < CELLS + 2:
                    sel[b, f, i, 64 + f * 16 + where_x] = 1.0
                if where_y < CELLS + 2:
                    sel[b, 2 + f, i, 96 + f * 16 + where_y] = 1.0
    t["sel"] = sel.reshape(N_GY, 512, 128).astype(ml_dtypes.bfloat16)
    tz2 = np.zeros((128, 32, 32))
    sb, sl = s32 @ basis, s32 @ lateral
    for f, layer in enumerate([0, P_SIZE - 1]):
        near = s32[:, layer]
        for i in range(NL):
            tz2[f * 16 + i] = near[:, None] * sb[None, :, i]
            tz2[32 + f * 16 + i] = near[None, :] * sb[:, None, i]
        for i in range(CELLS + 2):
            tz2[64 + f * 16 + i] = near[:, None] * sl[None, :, i]
            tz2[96 + f * 16 + i] = near[None, :] * sl[:, None, i]
    t["tz2"] = pair(tz2.reshape(128, 1024))
    return t


def split(x):
    high = x.astype(BF16)
    return high, (x - high.astype(F32)).astype(BF16)


def dot(x, y):
    return lax.dot_general(x, y, (((1,), (0,)), ((), ())), preferred_element_type=F32)


def dot_nt(x, y):
    return lax.dot_general(x, y, (((1,), (1,)), ((), ())), preferred_element_type=F32)


def times_table(x, table):
    high, low = split(x)
    return dot(high, table[0]) + dot(low, table[0]) + dot(high, table[1])


def table_times(table, x, product=dot):
    high, low = split(x)
    return product(table[0], high) + product(table[1], high) + product(table[0], low)


def stacked(x, width):
    return jnp.concatenate([x[:, i : i + width] for i in range(0, x.shape[1], width)], axis=0)


def unstacked(x, rows):
    return jnp.concatenate([x[i : i + rows] for i in range(0, x.shape[0], rows)], axis=1)


def lanes(rows):
    return lax.broadcasted_iota(jnp.int32, (rows, 128), 1)


A_TABLES = ("sc", "bd", "rm", "ty", "tz", "tx1", "tx2", "tx3", "u", "k1", "kl", "wc", "tf", "tc", "ec", "ef")


def first_kernel(q_ref, *refs):
    t = dict(zip(A_TABLES, refs))
    refs = refs[len(A_TABLES) :]
    tb_hbm, ta_hbm, m_ref, own_ref, down_ref, up_ref, rows, ls, lp, ly, g, tb, ta, sem = refs
    a, b = lax.axis_index("gx"), lax.axis_index("gy")
    copy_a = pltpu.make_async_copy(ta_hbm.at[a], ta, sem.at[0])
    copy_b = pltpu.make_async_copy(tb_hbm.at[b], tb, sem.at[1])
    copy_a.start()
    copy_b.start()
    x = table_times(t["sc"], q_ref[...])
    for y in range(P_SIZE):
        rows[pl.ds(y, 64, stride=P_SIZE), :] = x[:, y * 32 : y * 32 + 32]
    x = table_times(t["sc"], rows[...], dot_nt)
    x = times_table(stacked(x, 128), t["bd"]) * t["rm"][...]
    x = times_table(x, t["ty"])
    for i in range(4):
        z = table_times(t["tz"], x[i * 256 : i * 256 + 256])
        for j in range(4):
            k = i * 4 + j
            ls[:, k * 64 : k * 64 + 64] = z[j * 32 : j * 32 + 16, 0:64]
            lp[:, k * 64 : k * 64 + 64] = z[j * 32 + 16 : j * 32 + 32, 64:128]
            ly[:, k * 16 : k * 16 + 16] = z[j * 32 + 16 : j * 32 + 32, 128:144]
    samples = times_table(ls[...], t["tx1"])
    coefs = times_table(lp[...], t["tx2"]) + times_table(ly[...], t["tx3"])
    x = table_times(t["u"], samples)
    coefs = coefs - times_table(x[16:32], t["kl"])
    own_ref[...] = coefs
    down_ref[...] = pltpu.roll(coefs, 128 - 48, 1)
    up_ref[...] = pltpu.roll(coefs, 128 - 80, 1)
    x = times_table(x[0:8], t["k1"]) + x[8:16]
    for i in range(16):
        g[i * 8 : i * 8 + 8, :] = x[:, i * 16 : i * 16 + 16]
    copy_b.wait()
    x = times_table(g[...], tb)
    row = lax.broadcasted_iota(jnp.int32, (128, 512), 0)
    lane = lax.broadcasted_iota(jnp.int32, (128, 512), 1)
    x = jnp.where(row % 8 == lane // 64, x, 0.0)
    copy_a.wait()
    x = table_times(ta, x) * t["wc"][...]
    y_faces = table_times(t["ec"], times_table(x, t["tf"]))
    x_faces = times_table(stacked(table_times(t["ef"], x), 256), t["tc"])
    lane = lanes(N_GX)
    for f in range(2):
        for i in range(N_GY):
            col = i // 2 * 128
            low = x_faces[f * 32 : f * 32 + 32, col : col + 128]
            high = x_faces[64 + f * 32 : 96 + f * 32, col : col + 128]
            if i % 2:
                low = pltpu.roll(low, 64, 1)
            else:
                high = pltpu.roll(high, 64, 1)
            m_ref[pl.ds(i * 4 + f, N_GX, stride=32), :] = jnp.where(lane < 64, low, high)
    turned = [y_faces[i * 32 : i * 32 + 32] for i in range(CELLS + 2)]
    turned = [v if i == 0 else pltpu.roll(v, 8 * i, 1) for i, v in enumerate(turned)]
    group = lane // 8
    for i in range(N_GY):
        for f in range(2):
            value = jnp.zeros((N_GX, 128), F32)
            for k in range(CELLS + 2):
                value = jnp.where(group == (2 * i + f + k) % 16, turned[k], value)
            m_ref[pl.ds(i * 4 + 2 + f, N_GX, stride=32), :] = value


def charge_kernel(q_ref, s_ref, bd_ref, out_ref, rows):
    x = table_times(s_ref, q_ref[...])
    for y in range(P_SIZE):
        rows[pl.ds(y, 32, stride=P_SIZE), :] = x[:, y * 32 : y * 32 + 32]
    x = table_times(s_ref, rows[...], dot_nt)
    out_ref[...] = times_table(stacked(x, 128), bd_ref)


def last_kernel(m_ref, own_ref, right_ref, left_ref, above_ref, below_ref, spec_ref, s_ref, bd_ref, rm_ref,
                sbz_ref, lz_ref, tz_ref, sel_hbm, out_ref, rows, flat, sel, sem):
    copy = pltpu.make_async_copy(sel_hbm.at[lax.axis_index("gy")], sel, sem)
    copy.start()
    got = jnp.sum(m_ref[...].reshape(128, 8, 128), axis=0)
    got = got[0:4] + got[4:8]
    lane = lanes(NL)
    coefs = jnp.where(lane < 64, own_ref[...], 0.0)
    for i, ref in enumerate((left_ref, right_ref, below_ref, above_ref)):
        coefs = coefs + jnp.where(lane // 16 == i, ref[...], 0.0)
    copy.wait()
    high, low = split(jnp.concatenate([lz_ref[i // 2] * got[i : i + 1] for i in range(4)], axis=1))
    x = dot(high, sel[...]) + dot(low, sel[...]) + table_times(sbz_ref, coefs)
    x = times_table(x, tz_ref)
    x = (stacked(x, 128) + spec_ref[...]) * rm_ref[...]
    x = table_times(s_ref, unstacked(x, 32))
    x = times_table(stacked(x, 128), bd_ref)
    for i in range(8):
        rows[i * 128 : i * 128 + 128, :] = x[i * 32 : i * 32 + 32].T
    for y in range(P_SIZE):
        flat[:, y * 32 : y * 32 + 32] = rows[pl.ds(y, 32, stride=P_SIZE), :]
    out_ref[...] = table_times(s_ref, flat[...])


def vmem(count):
    return [pl.BlockSpec(memory_space=pltpu.VMEM)] * count


def hbm(count):
    return [pl.BlockSpec(memory_space=pl.ANY)] * count


def shape(*dims):
    return jax.ShapeDtypeStruct(dims, F32)


PARAMS = pltpu.CompilerParams(vmem_limit_bytes=VMEM_LIMIT)


def body(charge):
    t = {k: jnp.asarray(v) for k, v in tables().items()}
    message, own, down, up = pl.pallas_call(
        first_kernel,
        out_shape=(shape(1024, 128), shape(NL, 128), shape(NL, 128), shape(NL, 128)),
        in_specs=vmem(1 + len(A_TABLES)) + hbm(2),
        out_specs=tuple(vmem(4)),
        scratch_shapes=[
            pltpu.VMEM((2048, 32), F32),
            pltpu.VMEM((16, 1024), F32),
            pltpu.VMEM((16, 1024), F32),
            pltpu.VMEM((16, 256), F32),
            pltpu.VMEM((128, 16), F32),
            pltpu.VMEM((2, 16, 512), BF16),
            pltpu.VMEM((2, 256, 128), BF16),
            pltpu.SemaphoreType.DMA((2,)),
        ],
        compiler_params=PARAMS,
        name="first",
    )(charge, *[t[k] for k in A_TABLES], t["tb"], t["ta"])
    arrived = lax.all_to_all(message.reshape(256, 4, 128), ("gx", "gy"), 0, 0).reshape(1024, 128)
    around = []
    for axis, count in (("gx", N_GX), ("gy", N_GY)):
        forward = [(i, i + 1) for i in range(count - 1)]
        around.append(lax.ppermute(down, axis, [(j, i) for i, j in forward]))
        around.append(lax.ppermute(up, axis, forward))
    spec = pl.pallas_call(
        charge_kernel,
        out_shape=shape(256, 128),
        in_specs=vmem(3),
        out_specs=vmem(1)[0],
        scratch_shapes=[pltpu.VMEM((1024, 32), F32)],
        compiler_params=PARAMS,
        name="charge",
    )(charge, t["s32"], t["bd32"])
    return pl.pallas_call(
        last_kernel,
        out_shape=shape(32, 1024),
        in_specs=vmem(13) + hbm(1),
        out_specs=vmem(1)[0],
        scratch_shapes=[
            pltpu.VMEM((1024, 32), F32),
            pltpu.VMEM((32, 1024), F32),
            pltpu.VMEM((512, 128), BF16),
            pltpu.SemaphoreType.DMA,
        ],
        compiler_params=PARAMS,
        name="last",
    )(arrived, own, *around, spec, t["s32"], t["bd32"], t["rm32"], t["sbz"], t["lz"], t["tz2"], t["sel"])


def solution(mesh):
    spec = P("gx", "gy")
    return jax.shard_map(body, mesh=mesh, in_specs=(spec,), out_specs=spec, check_vma=False)
```

```python
import functools

import jax
import jax.numpy as jnp
import ml_dtypes
import numpy as np
from jax import lax
from jax.experimental import pallas as pl
from jax.experimental.pallas import tpu as pltpu
from jax.sharding import PartitionSpec as P

P_SIZE = 32
W = 16
Q = 4
NL = 16
N_GX = 32
N_GY = 8
CELLS = P_SIZE // Q
BF16 = jnp.bfloat16
F32 = jnp.float32


def sine(length):
    counter = np.arange(length) + 1
    multiple = counter[:, None] * counter[None, :] % (2 * (length + 1))
    return np.sin(np.pi * multiple / (length + 1))


def eigen(length):
    return 2.0 - 2.0 * np.cos(np.pi * (np.arange(length) + 1) / (length + 1))


def interp(fine_start, fine_count, coarse_start, coarse_count, ratio):
    fine_pos = np.arange(fine_count) + fine_start
    coarse_pos = np.arange(coarse_count) + coarse_start
    numerator = 2 * fine_pos - (ratio - 1)
    lower_index = numerator // (2 * ratio)
    weight = ((numerator - 2 * ratio * lower_index) / (2.0 * ratio))[:, None]
    below = (coarse_pos[None, :] == lower_index[:, None]).astype(np.float64)
    above = (coarse_pos[None, :] == lower_index[:, None] + 1).astype(np.float64)
    return below * (1.0 - weight) + above * weight


def legendre(length, count):
    points = (2.0 * np.arange(length) + 1.0) / length - 1.0
    columns = [np.ones_like(points), points]
    for degree in range(2, count):
        columns.append(
            ((2 * degree - 1) * points * columns[-1] - (degree - 1) * columns[-2]) / degree
        )
    result = []
    for column in columns[:count]:
        vector = column
        for _ in range(2):
            for earlier in result:
                vector = vector - np.sum(earlier * vector) * earlier
        result.append(vector / np.sqrt(np.sum(vector * vector)))
    return np.stack(result, axis=1)


def columns_at(table, positions):
    positions = np.asarray(positions)
    inside = (positions >= 0) & (positions < table.shape[1])
    return table[:, np.clip(positions, 0, table.shape[1] - 1)] * inside


def pair(table):
    table = np.asarray(table, np.float64)
    high = table.astype(np.float32).astype(ml_dtypes.bfloat16)
    low = (table - high.astype(np.float64)).astype(np.float32).astype(ml_dtypes.bfloat16)
    return np.stack([high, low], axis=-3)


@functools.lru_cache(None)
def tables():
    t = {}
    n = P_SIZE + 2 * W
    s64, m64 = sine(n), eigen(n)
    s32, m32 = sine(P_SIZE), eigen(P_SIZE)
    s8, m8 = sine(CELLS), eigen(CELLS)
    nx, ny = CELLS * N_GX, CELLS * N_GY
    sx, mx = sine(nx), eigen(nx)
    sy, my = sine(ny), eigen(ny)
    eye = np.eye
    basis = legendre(P_SIZE, NL)
    fine = interp(0, n, 0, n // Q, Q)
    mean = np.kron(eye(n // Q), np.full((1, Q), 1.0 / Q))
    inside = slice(W, W + P_SIZE)
    places = [W - 1, W + P_SIZE, W, W + P_SIZE - 1]
    r = mean @ s64
    bs = basis.T @ s64[inside]
    st = s64[places]
    bl = basis.T @ fine[inside]
    lt = fine[places]
    lanes_x, lanes_y = [[0], [16], [128, 144], [160, 176]], [[32], [48], [192, 208], [224, 240]]
    sc = s64[:, inside]
    t["sc"] = pair(sc)
    t["bd"] = pair(np.kron(eye(4), sc.T))
    kx = m64.reshape(16, 1, 4, 1)
    rm = (2.0 / (n + 1)) ** 3 / (kx + m64.reshape(1, n, 1, 1) + m64.reshape(1, 1, 1, n))
    t["rm"] = rm.reshape(16 * n, 4 * n).astype(np.float32)
    ty = np.zeros((4, n, 256))
    for i in range(4):
        ty[i, :, i * 16 : i * 16 + 16] = r.T
        ty[i, :, 64 + i * 16 : 64 + i * 16 + 16] = bs.T
        ty[i, :, 128 + i * 4 : 128 + i * 4 + 4] = st.T
    t["ty"] = pair(ty.reshape(4 * n, 256))
    t["tz"] = pair(np.kron(eye(4), np.concatenate([r, bs], axis=0)))
    t["tx1"] = pair(np.kron(r.T, eye(16)))
    tx2 = np.zeros((n, NL, 256))
    tx3 = np.zeros((n, 4, 256))
    kl = np.zeros((16, 16, 256))
    for i in range(4):
        for lane in lanes_x[i]:
            tx2[:, :, lane : lane + NL] = st[i][:, None, None] * eye(NL)
            kl[:, :, lane : lane + NL] = lt[i][:, None, None] * bl.T[None]
        for lane in lanes_y[i]:
            tx3[:, i, lane : lane + NL] = bs.T
            kl[:, :, lane : lane + NL] = bl.T[:, None, :] * lt[i][None, :, None]
    t["tx2"] = pair(tx2.reshape(n * NL, 256))
    t["tx3"] = pair(tx3.reshape(n * 4, 256))
    t["kl"] = pair(kl.reshape(256, 256))
    first = W // Q
    u1 = np.zeros((CELLS, 16))
    u2 = np.zeros((CELLS, 16))
    for k in range(CELLS):
        u1[:, k + first] += s8[:, k]
        u2[:, k + first - 1] -= s8[:, k] / (Q * Q)
        u2[:, k + first + 1] -= s8[:, k] / (Q * Q)
    t["u"] = pair(np.concatenate([u1, u2, bl], axis=0))
    beside = eye(16, k=1) + eye(16, k=-1)
    k1 = 6.0 * eye(256) - np.kron(beside, eye(16)) - np.kron(eye(16), beside)
    t["k1"] = pair(k1 / (Q * Q))
    t["yb"] = pair(np.concatenate([columns_at(sy, np.arange(16) + b * CELLS - first) for b in range(N_GY)], axis=1))
    xa = [columns_at(sx, np.arange(16) + a * CELLS - first) for a in range(N_GX)]
    xa = [np.concatenate(xa[2 * i : 2 * i + 2], axis=1).T for i in range(N_GX // 2)]
    t["xa"] = pair(np.stack([np.repeat(v, CELLS, axis=0) for v in xa]))
    scale = Q * Q * (2.0 / (nx + 1)) * (2.0 / (ny + 1)) * (2.0 / (CELLS + 1))
    wc = scale / (m8.reshape(CELLS, 1, 1) + my.reshape(1, ny, 1) + mx.reshape(1, 1, nx))
    t["wc"] = wc.reshape(CELLS * ny, nx).astype(np.float32)
    edge = interp(-1, P_SIZE + 2, -1, CELLS + 2, Q)
    ends = edge[[0, P_SIZE + 1]]
    lateral = edge[1 : P_SIZE + 1]
    depth = interp(0, P_SIZE, 0, CELLS, Q)
    around = np.arange(CELLS + 2) - 1
    near = [columns_at(sy, around + b * CELLS).T for b in range(N_GY)]
    near = [np.concatenate([v, ends @ v, np.zeros((4, ny))], axis=0) for v in near]
    ey = np.zeros((N_GY, 16, CELLS, CELLS, ny))
    for k in range(CELLS):
        ey[:, :, k, k, :] = np.stack(near)
    t["ey"] = pair(ey.reshape(N_GY, 128, CELLS * ny))
    near = [columns_at(sx, around + a * CELLS).T for a in range(N_GX)]
    near = np.stack([np.concatenate([v, ends @ v], axis=0) for v in near]).reshape(N_GX // 2, 2, 12, nx)
    t["ex"] = pair(near.transpose(1, 2, 0, 3).reshape(2, 12 * (N_GX // 2), nx))
    t["s32"] = pair(s32)
    t["bd32"] = pair(np.kron(eye(4), s32))
    rm32 = m32.reshape(8, 1, 4, 1) + m32.reshape(1, 32, 1, 1) + m32.reshape(1, 1, 1, 32)
    t["rm32"] = ((2.0 / (P_SIZE + 1)) ** 3 / rm32).reshape(256, 128).astype(np.float32)
    t["sbz"] = pair(s32 @ basis)
    lz = s32 @ depth @ s8
    lane = np.arange(128)
    t["lz"] = lz[:, lane % 8].astype(np.float32)
    sel = np.zeros((4, 128, 128), np.float32)
    for f in range(4):
        for i in range((CELLS + 2) * CELLS):
            sel[f, i, 64 + f * 16 + i // 8] = 1.0
    t["sel"] = sel.reshape(512, 128).astype(ml_dtypes.bfloat16)
    tz2 = np.zeros((128, 32, 32))
    sb, sl = s32 @ basis, s32 @ lateral
    for f, layer in enumerate([0, P_SIZE - 1]):
        near = s32[:, layer]
        for i in range(NL):
            tz2[f * 16 + i] = near[:, None] * sb[None, :, i]
            tz2[32 + f * 16 + i] = near[None, :] * sb[:, None, i]
        for i in range(CELLS + 2):
            tz2[64 + f * 16 + i] = near[:, None] * sl[None, :, i]
            tz2[96 + f * 16 + i] = near[None, :] * sl[:, None, i]
    t["tz2"] = pair(tz2.reshape(128, 1024))
    return t


def split(x):
    high = x.astype(BF16)
    return high, (x - high.astype(F32)).astype(BF16)


def dot(x, y):
    return lax.dot_general(x, y, (((1,), (0,)), ((), ())), preferred_element_type=F32)


def dot_nt(x, y):
    return lax.dot_general(x, y, (((1,), (1,)), ((), ())), preferred_element_type=F32)


def times_table(x, table):
    high, low = split(x)
    return dot(high, table[0]) + dot(low, table[0]) + dot(high, table[1])


def table_times(table, x, product=dot):
    high, low = split(x)
    return product(table[0], high) + product(table[1], high) + product(table[0], low)


def stacked(x, width):
    return jnp.concatenate([x[:, i : i + width] for i in range(0, x.shape[1], width)], axis=0)


def unstacked(x, rows):
    return jnp.concatenate([x[i : i + rows] for i in range(0, x.shape[0], rows)], axis=1)


def lanes(rows):
    return lax.broadcasted_iota(jnp.int32, (rows, 128), 1)


class Loaded:
    def __init__(self, names, sources, targets, sem):
        self.refs = dict(zip(names, targets))
        self.copies = {
            name: pltpu.make_async_copy(source, target, sem.at[i])
            for i, (name, source, target) in enumerate(zip(names, sources, targets))
        }
        for name in names:
            self.copies[name].start()

    def __getitem__(self, name):
        if name in self.copies:
            self.copies.pop(name).wait()
        return self.refs[name]


def kind(name):
    table = tables()[name]
    dims = table.shape[1:] if name in ("xa", "ey", "ex") else table.shape
    return dims, F32 if table.dtype == np.float32 else BF16


A_TABLES = ("sc", "bd", "rm", "ty", "tz", "tx1", "u", "k1", "tx2", "tx3", "kl", "s32", "bd32")
B_TABLES = ("yb", "xa", "wc", "ey", "ex")
C_TABLES = ("lz", "sel", "sbz", "tz2", "rm32", "s32", "bd32")
LATER = B_TABLES + C_TABLES


def first_kernel(q_ref, *refs):
    n, later = len(A_TABLES), len(LATER)
    own_tables, later_tables, refs = refs[:n], refs[n : n + later], refs[n + later :]
    m_ref, own_ref, spec_ref = refs[:3]
    fetched, refs = refs[3 : 3 + later], refs[3 + later :]
    rows, rows32, ls, lp, ly, spill = refs[:6]
    t = Loaded(A_TABLES, own_tables, refs[6 : 6 + n], refs[6 + n])
    place = {"xa": lax.axis_index("gs"), "ey": lax.axis_index("gy"), "ex": lax.axis_index("gc")}
    sources = [ref.at[place[k]] if k in place else ref for k, ref in zip(LATER, later_tables)]
    ahead = Loaded(LATER, sources, fetched, refs[7 + n])
    x = table_times(t["sc"], q_ref[...])
    for y in range(P_SIZE):
        rows[pl.ds(y, 64, stride=P_SIZE), :] = x[:, y * 32 : y * 32 + 32]
    x = table_times(t["sc"], rows[...], dot_nt)
    x = times_table(stacked(x, 128), t["bd"]) * t["rm"][...]
    x = times_table(x, t["ty"])
    for i in range(4):
        z = table_times(t["tz"], x[i * 256 : i * 256 + 256])
        for j in range(4):
            k = i * 4 + j
            ls[:, k * 64 : k * 64 + 64] = z[j * 32 : j * 32 + 16, 0:64]
            lp[:, k * 64 : k * 64 + 64] = z[j * 32 + 16 : j * 32 + 32, 64:128]
            ly[:, k * 16 : k * 16 + 16] = z[j * 32 + 16 : j * 32 + 32, 128:144]
    samples = times_table(ls[...], t["tx1"])
    coefs = times_table(lp[...], t["tx2"]) + times_table(ly[...], t["tx3"])
    x = table_times(t["u"], samples)
    coefs = coefs - times_table(x[16:32], t["kl"])
    own_ref[...] = coefs[:, 0:128]
    y = table_times(t["s32"], q_ref[...])
    for i in range(P_SIZE):
        rows32[pl.ds(i, 32, stride=P_SIZE), :] = y[:, i * 32 : i * 32 + 32]
    y = table_times(t["s32"], rows32[...], dot_nt)
    spec_ref[...] = times_table(stacked(y, 128), t["bd32"])
    x = (times_table(x[0:8], t["k1"]) + x[8:16]).T
    for i in range(16):
        spill[:, i * 8 : i * 8 + 8] = x[i * 16 : i * 16 + 16]
    spilled = spill[...]
    tile = jnp.where(lanes(8) // 16 % 2 == 0, coefs[0:8, 128:256], coefs[8:16, 128:256])
    for i in range(16):
        m_ref[i * 24 : i * 24 + 16, :] = spilled
        m_ref[i * 24 + 16 : i * 24 + 24, :] = tile
    for name in LATER:
        ahead[name]


def unpacked(tile, source, slot):
    parts = []
    for half in range(2):
        shift = (16 * slot - source - 16 * half) % 128
        parts.append(pltpu.roll(tile, shift, 1) if shift else tile)
    return jnp.where(lanes(NL) // 16 == slot, jnp.concatenate(parts, axis=0), 0.0)


def strip_kernel(got_ref, own_ref, *refs):
    t = dict(zip(B_TABLES, refs))
    m_ref, coefs_ref = refs[len(B_TABLES) :]
    s, c, b = lax.axis_index("gs"), lax.axis_index("gc"), lax.axis_index("gy")
    source = [
        jnp.concatenate([got_ref[(i * 8 + j) * 24 : (i * 8 + j) * 24 + 16, :] for j in range(N_GY)], axis=0)
        for i in range(2)
    ]
    x = table_times(t["yb"], jnp.concatenate(source, axis=1))
    lane = lax.broadcasted_iota(jnp.int32, (64, 256), 1)
    x = jnp.concatenate([jnp.where(lane % 8 == k, x, 0.0) for k in range(CELLS)], axis=0)
    x = times_table(x, t["xa"]) * t["wc"][...]
    x = table_times(t["ey"], x)
    x = table_times(t["ex"], x, dot_nt)
    m_ref[...] = jnp.zeros((128, 128), F32)
    lane = lanes(16)
    for f in range(2):
        m_ref[pl.ds(f, 16, stride=8), :] = jnp.where(lane < 80, x[160 + f * 16 : 176 + f * 16], 0.0)
        value = jnp.zeros((16, 128), F32)
        for k in range(CELLS + 2):
            part = pltpu.roll(x[k * 16 : k * 16 + 16], (8 * (k - 10 - f)) % 128, 1)
            value = jnp.where(lane // 8 == k, part, value)
        m_ref[pl.ds(2 + f, 16, stride=8), :] = value

    def tile_of(i, j):
        return got_ref[pl.ds(pl.multiple_of((i * 8 + j) * 24 + 16, 8), 8), :]

    partner = tile_of(1 - c, b)
    outside = jnp.where(c == 0, pltpu.roll(partner, 64, 1), pltpu.roll(partner, 96, 1))
    outside = jnp.where(lanes(8) >= 96, outside, 0.0)
    target = s + 1 - 2 * c

    @pl.when((target >= 0) & (target < 16))
    def _():
        where = pl.ds(pl.multiple_of(target * 8, 8), 8)
        m_ref[where, :] = m_ref[where, :] + outside

    coefs = jnp.where(lane < 64, own_ref[...], 0.0)
    coefs = coefs + jnp.where(c == 0, unpacked(partner, 0, 1), unpacked(partner, 32, 0))
    above = unpacked(tile_of(c, jnp.minimum(b + 1, N_GY - 1)), 64, 3)
    below = unpacked(tile_of(c, jnp.maximum(b - 1, 0)), 96, 2)
    coefs = coefs + jnp.where(b < N_GY - 1, above, 0.0) + jnp.where(b > 0, below, 0.0)
    coefs_ref[...] = coefs


def last_kernel(m_ref, coefs_ref, spec_ref, *refs):
    t = dict(zip(C_TABLES, refs))
    out_ref, rows, flat = refs[len(C_TABLES) :]
    got = jnp.sum(m_ref[...].reshape(16, 8, 128), axis=0)
    coefs = coefs_ref[...] + jnp.where(lax.axis_index("gc") == 0, unpacked(got, 96, 0), unpacked(got, 96, 1))
    lz = t["lz"][...]
    sel = t["sel"][...]
    high, low = split(jnp.concatenate([lz * got[i : i + 1] for i in range(4)], axis=1))
    x = dot(high, sel) + dot(low, sel) + table_times(t["sbz"], coefs)
    x = times_table(x, t["tz2"])
    x = (stacked(x, 128) + spec_ref[...]) * t["rm32"][...]
    x = table_times(t["s32"], unstacked(x, 32))
    x = times_table(stacked(x, 128), t["bd32"])
    for i in range(8):
        rows[i * 128 : i * 128 + 128, :] = x[i * 32 : i * 32 + 32].T
    for y in range(P_SIZE):
        flat[:, y * 32 : y * 32 + 32] = rows[pl.ds(y, 32, stride=P_SIZE), :]
    out_ref[...] = table_times(t["s32"], flat[...])


def vmem(count):
    return [pl.BlockSpec(memory_space=pltpu.VMEM)] * count


def hbm(count):
    return [pl.BlockSpec(memory_space=pltpu.HBM)] * count


def shape(*dims):
    return jax.ShapeDtypeStruct(dims, F32)


def params(mib):
    return pltpu.CompilerParams(vmem_limit_bytes=mib * 1024 * 1024)


def body(charge):
    t = {k: jnp.asarray(v) for k, v in tables().items()}
    message, own, spec, *fetched = pl.pallas_call(
        first_kernel,
        out_shape=[shape(384, 128), shape(NL, 128), shape(256, 128)] + [jax.ShapeDtypeStruct(*kind(k)) for k in LATER],
        in_specs=vmem(1) + hbm(len(A_TABLES) + len(LATER)),
        out_specs=vmem(3 + len(LATER)),
        scratch_shapes=[
            pltpu.VMEM((2048, 32), F32),
            pltpu.VMEM((1024, 32), F32),
            pltpu.VMEM((16, 1024), F32),
            pltpu.VMEM((16, 1024), F32),
            pltpu.VMEM((16, 256), F32),
            pltpu.VMEM((16, 128), F32),
        ]
        + [pltpu.VMEM(*kind(k)) for k in A_TABLES]
        + [pltpu.SemaphoreType.DMA((len(A_TABLES),)), pltpu.SemaphoreType.DMA((len(LATER),))],
        compiler_params=params(24),
        name="first",
    )(*[pltpu.with_memory_space_constraint(v, pltpu.HBM) for v in (charge, *[t[k] for k in A_TABLES + LATER])])
    fetched = dict(zip(LATER, fetched))
    strip = lax.all_to_all(message.reshape(16, 24, 128), ("gc", "gy"), 0, 0).reshape(384, 128)
    message, coefs = pl.pallas_call(
        strip_kernel,
        out_shape=(shape(128, 128), shape(NL, 128)),
        in_specs=vmem(2 + len(B_TABLES)),
        out_specs=tuple(vmem(2)),
        compiler_params=params(12),
        name="strip",
    )(strip, own, *[fetched[k] for k in B_TABLES])
    arrived = lax.all_to_all(message.reshape(16, 8, 128), "gs", 0, 0).reshape(128, 128)
    return pl.pallas_call(
        last_kernel,
        out_shape=shape(32, 1024),
        in_specs=vmem(3 + len(C_TABLES)),
        out_specs=vmem(1)[0],
        scratch_shapes=[pltpu.VMEM((1024, 32), F32), pltpu.VMEM((32, 1024), F32)],
        compiler_params=params(12),
        name="last",
    )(arrived, coefs, spec, *[fetched[k] for k in C_TABLES])


def solution(mesh):
    strips = jax.sharding.Mesh(mesh.devices.reshape(N_GX // 2, 2, N_GY), ("gs", "gc", "gy"))
    spec = P(("gs", "gc"), "gy")
    return jax.shard_map(body, mesh=strips, in_specs=(spec,), out_specs=spec, check_vma=False)
```

```python
import functools

import jax
import jax.numpy as jnp
import ml_dtypes
import numpy as np
from jax import lax
from jax.experimental import pallas as pl
from jax.experimental.pallas import tpu as pltpu
from jax.sharding import PartitionSpec as P

P_SIZE = 32
W = 16
Q = 4
NL = 16
N_GX = 32
N_GY = 8
CELLS = P_SIZE // Q
BF16 = jnp.bfloat16
F32 = jnp.float32


def sine(length):
    counter = np.arange(length) + 1
    multiple = counter[:, None] * counter[None, :] % (2 * (length + 1))
    return np.sin(np.pi * multiple / (length + 1))


def eigen(length):
    return 2.0 - 2.0 * np.cos(np.pi * (np.arange(length) + 1) / (length + 1))


def interp(fine_start, fine_count, coarse_start, coarse_count, ratio):
    fine_pos = np.arange(fine_count) + fine_start
    coarse_pos = np.arange(coarse_count) + coarse_start
    numerator = 2 * fine_pos - (ratio - 1)
    lower_index = numerator // (2 * ratio)
    weight = ((numerator - 2 * ratio * lower_index) / (2.0 * ratio))[:, None]
    below = (coarse_pos[None, :] == lower_index[:, None]).astype(np.float64)
    above = (coarse_pos[None, :] == lower_index[:, None] + 1).astype(np.float64)
    return below * (1.0 - weight) + above * weight


def legendre(length, count):
    points = (2.0 * np.arange(length) + 1.0) / length - 1.0
    columns = [np.ones_like(points), points]
    for degree in range(2, count):
        columns.append(
            ((2 * degree - 1) * points * columns[-1] - (degree - 1) * columns[-2]) / degree
        )
    result = []
    for column in columns[:count]:
        vector = column
        for _ in range(2):
            for earlier in result:
                vector = vector - np.sum(earlier * vector) * earlier
        result.append(vector / np.sqrt(np.sum(vector * vector)))
    return np.stack(result, axis=1)


def columns_at(table, positions):
    positions = np.asarray(positions)
    inside = (positions >= 0) & (positions < table.shape[1])
    return table[:, np.clip(positions, 0, table.shape[1] - 1)] * inside


def pair(table):
    table = np.asarray(table, np.float64)
    high = table.astype(np.float32).astype(ml_dtypes.bfloat16)
    low = (table - high.astype(np.float64)).astype(np.float32).astype(ml_dtypes.bfloat16)
    return np.stack([high, low], axis=-3)


@functools.lru_cache(None)
def tables():
    t = {}
    n = P_SIZE + 2 * W
    s64, m64 = sine(n), eigen(n)
    s32, m32 = sine(P_SIZE), eigen(P_SIZE)
    s8, m8 = sine(CELLS), eigen(CELLS)
    nx, ny = CELLS * N_GX, CELLS * N_GY
    sx, mx = sine(nx), eigen(nx)
    sy, my = sine(ny), eigen(ny)
    eye = np.eye
    basis = legendre(P_SIZE, NL)
    fine = interp(0, n, 0, n // Q, Q)
    mean = np.kron(eye(n // Q), np.full((1, Q), 1.0 / Q))
    inside = slice(W, W + P_SIZE)
    places = [W - 1, W + P_SIZE, W, W + P_SIZE - 1]
    r = mean @ s64
    bs = basis.T @ s64[inside]
    st = s64[places]
    bl = basis.T @ fine[inside]
    lt = fine[places]
    lanes_x, lanes_y = [[0], [16], [128, 144], [160, 176]], [[32], [48], [192, 208], [224, 240]]
    sc = s64[:, inside]
    t["sc"] = pair(sc)
    t["bd"] = pair(np.kron(eye(4), sc.T))
    kx = m64.reshape(16, 1, 4, 1)
    rm = (2.0 / (n + 1)) ** 3 / (kx + m64.reshape(1, n, 1, 1) + m64.reshape(1, 1, 1, n))
    t["rm"] = rm.reshape(16 * n, 4 * n).astype(np.float32)
    ty = np.zeros((4, n, 256))
    for i in range(4):
        ty[i, :, i * 16 : i * 16 + 16] = r.T
        ty[i, :, 64 + i * 16 : 64 + i * 16 + 16] = bs.T
        ty[i, :, 128 + i * 4 : 128 + i * 4 + 4] = st.T
    t["ty"] = pair(ty.reshape(4 * n, 256))
    t["tz"] = pair(np.kron(eye(4), np.concatenate([r, bs], axis=0)))
    t["tx1"] = pair(np.kron(r.T, eye(16)))
    tx2 = np.zeros((n, NL, 256))
    tx3 = np.zeros((n, 4, 256))
    kl = np.zeros((16, 16, 256))
    for i in range(4):
        for lane in lanes_x[i]:
            tx2[:, :, lane : lane + NL] = st[i][:, None, None] * eye(NL)
            kl[:, :, lane : lane + NL] = lt[i][:, None, None] * bl.T[None]
        for lane in lanes_y[i]:
            tx3[:, i, lane : lane + NL] = bs.T
            kl[:, :, lane : lane + NL] = bl.T[:, None, :] * lt[i][None, :, None]
    t["tx2"] = pair(tx2.reshape(n * NL, 256))
    t["tx3"] = pair(tx3.reshape(n * 4, 256))
    t["kl"] = pair(kl.reshape(256, 256))
    first = W // Q
    u1 = np.zeros((CELLS, 16))
    u2 = np.zeros((CELLS, 16))
    for k in range(CELLS):
        u1[:, k + first] += s8[:, k]
        u2[:, k + first - 1] -= s8[:, k] / (Q * Q)
        u2[:, k + first + 1] -= s8[:, k] / (Q * Q)
    t["u"] = pair(np.concatenate([u1, u2, bl], axis=0))
    beside = eye(16, k=1) + eye(16, k=-1)
    k1 = 6.0 * eye(256) - np.kron(beside, eye(16)) - np.kron(eye(16), beside)
    t["k1"] = pair(k1 / (Q * Q))
    t["yb"] = pair(np.concatenate([columns_at(sy, np.arange(16) + b * CELLS - first) for b in range(N_GY)], axis=1))
    xa = [columns_at(sx, np.arange(16) + a * CELLS - first) for a in range(N_GX)]
    xa = [np.concatenate(xa[2 * i : 2 * i + 2], axis=1).T for i in range(N_GX // 2)]
    t["xa"] = pair(np.stack([np.repeat(v, CELLS, axis=0) for v in xa]))
    scale = Q * Q * (2.0 / (nx + 1)) * (2.0 / (ny + 1)) * (2.0 / (CELLS + 1))
    wc = scale / (m8.reshape(CELLS, 1, 1) + my.reshape(1, ny, 1) + mx.reshape(1, 1, nx))
    t["wc"] = wc.reshape(CELLS * ny, nx).astype(np.float32)
    edge = interp(-1, P_SIZE + 2, -1, CELLS + 2, Q)
    ends = edge[[0, P_SIZE + 1]]
    lateral = edge[1 : P_SIZE + 1]
    depth = interp(0, P_SIZE, 0, CELLS, Q)
    around = np.arange(CELLS + 2) - 1
    near = [columns_at(sy, around + b * CELLS).T for b in range(N_GY)]
    near = [np.concatenate([v, ends @ v, np.zeros((4, ny))], axis=0) for v in near]
    ey = np.zeros((N_GY, 16, CELLS, CELLS, ny))
    for k in range(CELLS):
        ey[:, :, k, k, :] = np.stack(near)
    t["ey"] = pair(ey.reshape(N_GY, 128, CELLS * ny))
    near = [columns_at(sx, around + a * CELLS).T for a in range(N_GX)]
    near = np.stack([np.concatenate([v, ends @ v], axis=0) for v in near]).reshape(N_GX // 2, 2, 12, nx)
    t["ex"] = pair(near.transpose(1, 2, 0, 3).reshape(2, 12 * (N_GX // 2), nx))
    t["s32"] = pair(s32)
    t["bd32"] = pair(np.kron(eye(4), s32))
    rm32 = m32.reshape(8, 1, 4, 1) + m32.reshape(1, 32, 1, 1) + m32.reshape(1, 1, 1, 32)
    t["rm32"] = ((2.0 / (P_SIZE + 1)) ** 3 / rm32).reshape(256, 128).astype(np.float32)
    t["sbz"] = pair(s32 @ basis)
    lz = s32 @ depth @ s8
    lane = np.arange(128)
    t["lz"] = lz[:, lane % 8].astype(np.float32)
    sel = np.zeros((4, 128, 128), np.float32)
    for f in range(4):
        for i in range((CELLS + 2) * CELLS):
            sel[f, i, 64 + f * 16 + i // 8] = 1.0
    t["sel"] = sel.reshape(512, 128).astype(ml_dtypes.bfloat16)
    tz2 = np.zeros((128, 32, 32))
    sb, sl = s32 @ basis, s32 @ lateral
    for f, layer in enumerate([0, P_SIZE - 1]):
        near = s32[:, layer]
        for i in range(NL):
            tz2[f * 16 + i] = near[:, None] * sb[None, :, i]
            tz2[32 + f * 16 + i] = near[None, :] * sb[:, None, i]
        for i in range(CELLS + 2):
            tz2[64 + f * 16 + i] = near[:, None] * sl[None, :, i]
            tz2[96 + f * 16 + i] = near[None, :] * sl[:, None, i]
    t["tz2"] = pair(tz2.reshape(128, 1024))
    return t


WIDE = {"bd": (0, 128), "ty": (128, 256), "tz": (384, 128), "tx1": (512, 1024), "k1": (1536, 256), "tx2": (1792, 1024), "tx3": (2816, 256), "kl": (3072, 256)}
SMALL = {"sc|": (0, 0, 64, 0, 96), "s32|": (0, 64, 32, 0, 96), "u|": (0, 96, 32, 0, 48), "sc=": (1, 0, 128, 0, 64), "s32=": (1, 0, 64, 64, 64)}


def in_row(table):
    return np.concatenate([table[0], table[1], table[0]], axis=1)


def in_block(table):
    return np.block([[table[0], table[0]], [table[1], np.zeros_like(table[1])]])


@functools.lru_cache(None)
def packs():
    t = tables()
    small = np.zeros((2, 256, 128), ml_dtypes.bfloat16)
    for name, (which, row, rows, lane, width) in SMALL.items():
        form = in_row if name[-1] == "|" else in_block
        small[which, row : row + rows, lane : lane + width] = form(t[name[:-1]])
    small[:, 128:256] = t["bd32"]
    later = np.zeros((2, 128, 1408), ml_dtypes.bfloat16)
    later[:, :, :1024] = t["tz2"]
    later[:, :64, 1024:1152] = t["yb"]
    later[0, 64:96, 1024:1072] = in_row(t["sbz"])
    later[:, :, 1152:] = t["sel"].reshape(2, 2, 128, 128).transpose(0, 2, 1, 3).reshape(2, 128, 256)
    scales = np.zeros((768, 256), np.float32)
    scales[:512] = t["wc"]
    scales[512:, :128] = t["rm32"]
    scales[512:544, 128:] = t["lz"]
    return {
        "small": small,
        "wide": np.concatenate([t[name] for name in WIDE], axis=1),
        "rm": t["rm"],
        "xa": t["xa"],
        "ey": t["ey"],
        "ex": t["ex"],
        "later": later,
        "scales": scales,
    }


class View:
    def __init__(self, ref, row, rows, lane, width):
        self.ref, self.rows, self.lanes = ref, slice(row, row + rows), slice(lane, lane + width)
        self.shape = (2, rows, width)

    def __getitem__(self, part):
        return self.ref[slice(None) if part is Ellipsis else part, self.rows, self.lanes]


def small_table(ref, name):
    which, row, rows, lane, width = SMALL[name]
    return ref[which, row : row + rows, lane : lane + width]


def split(x):
    high = x.astype(BF16)
    return high, (x - high.astype(F32)).astype(BF16)


def dot(x, y):
    return lax.dot_general(x, y, (((1,), (0,)), ((), ())), preferred_element_type=F32)


def dot_nt(x, y):
    return lax.dot_general(x, y, (((1,), (1,)), ((), ())), preferred_element_type=F32)


def times_table(x, table):
    high, low = split(x)
    rows = x.shape[0]
    if rows > 128:
        return dot(jnp.concatenate([high, low, high], axis=1), jnp.concatenate([table[0], table[0], table[1]], axis=0))
    if rows % 16:
        return dot(high, table[0]) + dot(low, table[0]) + dot(high, table[1])
    both = dot(jnp.concatenate([high, low], axis=0), table[0])
    return both[:rows] + both[rows:] + dot(high, table[1])


def table_times(table, x, product=dot):
    high, low = split(x)
    rows = table.shape[1]
    both = product(table[...].reshape(2 * rows, table.shape[2]), high)
    return both[:rows] + both[rows:] + product(table[0], low)


def row_times(table, x):
    high, low = split(x)
    return dot(table, jnp.concatenate([high, high, low], axis=0))


def block_times_nt(table, x):
    both = dot_nt(table, x)
    rows = table.shape[0] // 2
    return both[:rows] + both[rows:]


def spread(x, rows):
    high, low = split(x)
    high, low = high.astype(F32), low.astype(F32)
    for y in range(P_SIZE):
        part = slice(y * 32, y * 32 + 32)
        rows[pl.ds(y, x.shape[0], stride=P_SIZE), :] = jnp.concatenate([high[:, part], low[:, part]], axis=1)
    return rows[...].astype(BF16)


def stacked(x, width):
    return jnp.concatenate([x[:, i : i + width] for i in range(0, x.shape[1], width)], axis=0)


def unstacked(x, rows):
    return jnp.concatenate([x[i : i + rows] for i in range(0, x.shape[0], rows)], axis=1)


def lanes(rows):
    return lax.broadcasted_iota(jnp.int32, (rows, 128), 1)


SOURCES = ("rm", "wide", "small", "xa", "ey", "ex", "later", "scales")
KEPT = (((2, 256, 128), BF16), ((2, 256, 256), BF16), ((2, 128, 512), BF16), ((2, 192, 256), BF16), ((2, 128, 1408), BF16), ((768, 256), F32))


def first_kernel(q_hbm, rm_hbm, wide_hbm, small_hbm, xa_hbm, ey_hbm, ex_hbm, later_hbm, scales_hbm,
                 m_ref, own_ref, spec_ref, small, xa, ey, ex, later, scales,
                 q, rm, wide, rows, rows32, ls, lp, ly, spill, sem):
    started = []

    def start(source, target):
        copy = pltpu.make_async_copy(source, target, sem.at[len(started)])
        started.append(copy)
        copy.start()
        return copy

    def part(first, last):
        return start(wide_hbm.at[:, first:last, :], wide.at[:, first:last, :])

    now = [start(q_hbm, q), start(small_hbm, small), part(0, 512)]
    soon = [start(rm_hbm, rm)]
    for copy in now:
        copy.wait()
    soon += [part(512, 1792), part(1792, 3328)]
    t = {name: View(wide, row, count, 0, 256) for name, (row, count) in WIDE.items()}
    x = row_times(small_table(small, "sc|"), q[...])
    x = block_times_nt(small_table(small, "sc="), spread(x, rows))
    x = times_table(stacked(x, 128), t["bd"])
    bd32 = View(small, 128, 128, 0, 128)
    y = row_times(small_table(small, "s32|"), q[...])
    y = block_times_nt(small_table(small, "s32="), spread(y, rows32))
    spec_ref[...] = times_table(stacked(y, 128), bd32)
    for copy in soon:
        copy.wait()
    ahead = [
        start(xa_hbm.at[lax.axis_index("gs")], xa),
        start(ey_hbm.at[lax.axis_index("gy")], ey),
        start(ex_hbm.at[lax.axis_index("gc")], ex),
        start(scales_hbm, scales),
        start(later_hbm, later),
    ]
    x = x * rm[...]
    x = times_table(x, t["ty"])
    for i in range(4):
        z = table_times(t["tz"], x[i * 256 : i * 256 + 256])
        for j in range(4):
            k = i * 4 + j
            ls[:, k * 64 : k * 64 + 64] = z[j * 32 : j * 32 + 16, 0:64]
            lp[:, k * 64 : k * 64 + 64] = z[j * 32 + 16 : j * 32 + 32, 64:128]
            ly[:, k * 16 : k * 16 + 16] = z[j * 32 + 16 : j * 32 + 32, 128:144]
    samples = times_table(ls[...], t["tx1"])
    coefs = times_table(lp[...], t["tx2"]) + times_table(ly[...], t["tx3"])
    x = row_times(small_table(small, "u|"), samples)
    coefs = coefs - times_table(x[16:32], t["kl"])
    own_ref[...] = coefs[:, 0:128]
    x = (times_table(x[0:8], t["k1"]) + x[8:16]).T
    for i in range(16):
        spill[:, i * 8 : i * 8 + 8] = x[i * 16 : i * 16 + 16]
    spilled = spill[...]
    tile = jnp.where(lanes(8) // 16 % 2 == 0, coefs[0:8, 128:256], coefs[8:16, 128:256])
    for i in range(16):
        m_ref[i * 24 : i * 24 + 16, :] = spilled
        m_ref[i * 24 + 16 : i * 24 + 24, :] = tile
    for copy in ahead:
        copy.wait()


def unpacked(tile, source, slot):
    parts = []
    for half in range(2):
        shift = (16 * slot - source - 16 * half) % 128
        parts.append(pltpu.roll(tile, shift, 1) if shift else tile)
    return jnp.where(lanes(NL) // 16 == slot, jnp.concatenate(parts, axis=0), 0.0)


def strip_kernel(got_ref, own_ref, xa, ey, ex, later, scales, m_ref, coefs_ref):
    s, c, b = lax.axis_index("gs"), lax.axis_index("gc"), lax.axis_index("gy")
    source = [
        jnp.concatenate([got_ref[(i * 8 + j) * 24 : (i * 8 + j) * 24 + 16, :] for j in range(N_GY)], axis=0)
        for i in range(2)
    ]
    x = table_times(View(later, 0, 64, 1024, 128), jnp.concatenate(source, axis=1))
    lane = lax.broadcasted_iota(jnp.int32, (64, 256), 1)
    x = jnp.concatenate([jnp.where(lane % 8 == k, x, 0.0) for k in range(CELLS)], axis=0)
    x = times_table(x, xa) * scales[0:512, :]
    x = table_times(ey, x)
    x = table_times(ex, x, dot_nt)
    m_ref[...] = jnp.zeros((128, 128), F32)
    lane = lanes(16)
    for f in range(2):
        m_ref[pl.ds(f, 16, stride=8), :] = jnp.where(lane < 80, x[160 + f * 16 : 176 + f * 16], 0.0)
        value = jnp.zeros((16, 128), F32)
        for k in range(CELLS + 2):
            part = pltpu.roll(x[k * 16 : k * 16 + 16], (8 * (k - 10 - f)) % 128, 1)
            value = jnp.where(lane // 8 == k, part, value)
        m_ref[pl.ds(2 + f, 16, stride=8), :] = value

    def tile_of(i, j):
        return got_ref[pl.ds(pl.multiple_of((i * 8 + j) * 24 + 16, 8), 8), :]

    partner = tile_of(1 - c, b)
    outside = jnp.where(c == 0, pltpu.roll(partner, 64, 1), pltpu.roll(partner, 96, 1))
    outside = jnp.where(lanes(8) >= 96, outside, 0.0)
    target = s + 1 - 2 * c

    @pl.when((target >= 0) & (target < 16))
    def _():
        where = pl.ds(pl.multiple_of(target * 8, 8), 8)
        m_ref[where, :] = m_ref[where, :] + outside

    coefs = jnp.where(lane < 64, own_ref[...], 0.0)
    coefs = coefs + jnp.where(c == 0, unpacked(partner, 0, 1), unpacked(partner, 32, 0))
    above = unpacked(tile_of(c, jnp.minimum(b + 1, N_GY - 1)), 64, 3)
    below = unpacked(tile_of(c, jnp.maximum(b - 1, 0)), 96, 2)
    coefs = coefs + jnp.where(b < N_GY - 1, above, 0.0) + jnp.where(b > 0, below, 0.0)
    coefs_ref[...] = coefs


def last_kernel(m_ref, coefs_ref, spec_ref, small, later, scales, out_ref, rows, flat):
    s32, bd32 = small_table(small, "s32|"), View(small, 128, 128, 0, 128)
    got = jnp.sum(m_ref[...].reshape(16, 8, 128), axis=0)
    coefs = coefs_ref[...] + jnp.where(lax.axis_index("gc") == 0, unpacked(got, 96, 0), unpacked(got, 96, 1))
    lz = scales[512:544, 128:256]
    high, low = split(jnp.concatenate([lz * got[i : i + 1] for i in range(4)], axis=1))
    x = row_times(later[0, 64:96, 1024:1072], coefs)
    for i in range(4):
        part = jnp.concatenate([high[:, i * 128 : i * 128 + 128], low[:, i * 128 : i * 128 + 128]], axis=0)
        part = dot(part, later[i // 2, :, 1152 + i % 2 * 128 : 1280 + i % 2 * 128])
        x = x + part[:32] + part[32:]
    x = times_table(x, View(later, 0, 128, 0, 1024))
    x = (stacked(x, 128) + spec_ref[...]) * scales[512:768, 0:128]
    x = row_times(s32, unstacked(x, 32))
    x = times_table(stacked(x, 128), bd32)
    for i in range(8):
        rows[i * 128 : i * 128 + 128, :] = x[i * 32 : i * 32 + 32].T
    for y in range(P_SIZE):
        flat[:, y * 32 : y * 32 + 32] = rows[pl.ds(y, 32, stride=P_SIZE), :]
    out_ref[...] = row_times(s32, flat[...])


def vmem(count):
    return [pl.BlockSpec(memory_space=pltpu.VMEM)] * count


def hbm(count):
    return [pl.BlockSpec(memory_space=pltpu.HBM)] * count


def shape(*dims):
    return jax.ShapeDtypeStruct(dims, F32)


def params(mib):
    return pltpu.CompilerParams(vmem_limit_bytes=mib * 1024 * 1024)


def body(charge):
    t = packs()
    sources = [charge] + [jnp.asarray(t[k]) for k in SOURCES]
    message, own, spec, small, xa, ey, ex, later, scales = pl.pallas_call(
        first_kernel,
        out_shape=[shape(384, 128), shape(NL, 128), shape(256, 128)] + [jax.ShapeDtypeStruct(*k) for k in KEPT],
        in_specs=hbm(len(sources)),
        out_specs=vmem(3 + len(KEPT)),
        scratch_shapes=[
            pltpu.VMEM((32, 1024), F32),
            pltpu.VMEM((1024, 256), F32),
            pltpu.VMEM((2, 3328, 256), BF16),
            pltpu.VMEM((2048, 64), F32),
            pltpu.VMEM((1024, 64), F32),
            pltpu.VMEM((16, 1024), F32),
            pltpu.VMEM((16, 1024), F32),
            pltpu.VMEM((16, 256), F32),
            pltpu.VMEM((16, 128), F32),
            pltpu.SemaphoreType.DMA((11,)),
        ],
        compiler_params=params(24),
        name="first",
    )(*[pltpu.with_memory_space_constraint(v, pltpu.HBM) for v in sources])
    strip = lax.all_to_all(message.reshape(16, 24, 128), ("gc", "gy"), 0, 0).reshape(384, 128)
    message, coefs = pl.pallas_call(
        strip_kernel,
        out_shape=(shape(128, 128), shape(NL, 128)),
        in_specs=vmem(7),
        out_specs=tuple(vmem(2)),
        compiler_params=params(12),
        name="strip",
    )(strip, own, xa, ey, ex, later, scales)
    arrived = lax.all_to_all(message.reshape(16, 8, 128), "gs", 0, 0).reshape(128, 128)
    return pl.pallas_call(
        last_kernel,
        out_shape=shape(32, 1024),
        in_specs=vmem(6),
        out_specs=vmem(1)[0],
        scratch_shapes=[pltpu.VMEM((1024, 32), F32), pltpu.VMEM((32, 1024), F32)],
        compiler_params=params(12),
        name="last",
    )(arrived, coefs, spec, small, later, scales)


def solution(mesh):
    strips = jax.sharding.Mesh(mesh.devices.reshape(N_GX // 2, 2, N_GY), ("gs", "gc", "gy"))
    spec = P(("gs", "gc"), "gy")
    return jax.shard_map(body, mesh=strips, in_specs=(spec,), out_specs=spec, check_vma=False)
```

```python
import functools

import jax
import jax.numpy as jnp
import ml_dtypes
import numpy as np
from jax import lax
from jax.experimental import pallas as pl
from jax.experimental.pallas import tpu as pltpu
from jax.sharding import PartitionSpec as P

P_SIZE = 32
W = 16
Q = 4
NL = 16
N_GX = 32
N_GY = 8
CELLS = P_SIZE // Q
BF16 = jnp.bfloat16
F32 = jnp.float32


def sine(length):
    counter = np.arange(length) + 1
    multiple = counter[:, None] * counter[None, :] % (2 * (length + 1))
    return np.sin(np.pi * multiple / (length + 1))


def eigen(length):
    return 2.0 - 2.0 * np.cos(np.pi * (np.arange(length) + 1) / (length + 1))


def interp(fine_start, fine_count, coarse_start, coarse_count, ratio):
    fine_pos = np.arange(fine_count) + fine_start
    coarse_pos = np.arange(coarse_count) + coarse_start
    numerator = 2 * fine_pos - (ratio - 1)
    lower_index = numerator // (2 * ratio)
    weight = ((numerator - 2 * ratio * lower_index) / (2.0 * ratio))[:, None]
    below = (coarse_pos[None, :] == lower_index[:, None]).astype(np.float64)
    above = (coarse_pos[None, :] == lower_index[:, None] + 1).astype(np.float64)
    return below * (1.0 - weight) + above * weight


def legendre(length, count):
    points = (2.0 * np.arange(length) + 1.0) / length - 1.0
    columns = [np.ones_like(points), points]
    for degree in range(2, count):
        columns.append(
            ((2 * degree - 1) * points * columns[-1] - (degree - 1) * columns[-2]) / degree
        )
    result = []
    for column in columns[:count]:
        vector = column
        for _ in range(2):
            for earlier in result:
                vector = vector - np.sum(earlier * vector) * earlier
        result.append(vector / np.sqrt(np.sum(vector * vector)))
    return np.stack(result, axis=1)


def columns_at(table, positions):
    positions = np.asarray(positions)
    inside = (positions >= 0) & (positions < table.shape[1])
    return table[:, np.clip(positions, 0, table.shape[1] - 1)] * inside


def pair(table):
    table = np.asarray(table, np.float64)
    high = table.astype(np.float32).astype(ml_dtypes.bfloat16)
    low = (table - high.astype(np.float64)).astype(np.float32).astype(ml_dtypes.bfloat16)
    return np.stack([high, low], axis=-3)


@functools.lru_cache(None)
def tables():
    t = {}
    n = P_SIZE + 2 * W
    s64, m64 = sine(n), eigen(n)
    s32, m32 = sine(P_SIZE), eigen(P_SIZE)
    s8, m8 = sine(CELLS), eigen(CELLS)
    nx, ny = CELLS * N_GX, CELLS * N_GY
    sx, mx = sine(nx), eigen(nx)
    sy, my = sine(ny), eigen(ny)
    eye = np.eye
    basis = legendre(P_SIZE, NL)
    fine = interp(0, n, 0, n // Q, Q)
    mean = np.kron(eye(n // Q), np.full((1, Q), 1.0 / Q))
    inside = slice(W, W + P_SIZE)
    places = [W - 1, W + P_SIZE, W, W + P_SIZE - 1]
    r = mean @ s64
    bs = basis.T @ s64[inside]
    st = s64[places]
    bl = basis.T @ fine[inside]
    lt = fine[places]
    lanes_x, lanes_y = [0, 16, 64, 80], [32, 48, 96, 112]
    sc = s64[:, inside]
    t["sc"] = pair(sc)
    t["bd"] = pair(np.kron(eye(4), sc.T))
    mu = np.zeros((16 + n, 256))
    mu[:16] = (m64.reshape(16, 4, 1) + m64).reshape(16, 256)
    mu[16:] = m64[:, None]
    t["mu"] = (mu * ((n + 1) / 2.0) ** 3).astype(np.float32)
    ty = np.zeros((4, n, 256))
    for i in range(4):
        ty[i, :, i * 16 : i * 16 + 16] = r.T
        ty[i, :, 64 + i * 16 : 64 + i * 16 + 16] = bs.T
        ty[i, :, 128 + i * 4 : 128 + i * 4 + 4] = st.T
    t["ty"] = pair(ty.reshape(4 * n, 256))
    t["tz"] = pair(np.kron(eye(4), np.concatenate([r, bs], axis=0)))
    t["tx1"] = pair(np.kron(r.T, eye(16)))
    tx2 = np.zeros((n, NL, 128))
    tx3 = np.zeros((n, 4, 128))
    kl = np.zeros((16, 16, 128))
    for i in range(4):
        at_x, at_y = slice(lanes_x[i], lanes_x[i] + NL), slice(lanes_y[i], lanes_y[i] + NL)
        tx2[:, :, at_x] = st[i][:, None, None] * eye(NL)
        kl[:, :, at_x] = lt[i][:, None, None] * bl.T[None]
        tx3[:, i, at_y] = bs.T
        kl[:, :, at_y] = bl.T[:, None, :] * lt[i][None, :, None]
    t["tx2"] = pair(tx2.reshape(n * NL, 128))
    t["tx3"] = pair(tx3.reshape(n * 4, 128))
    t["kl"] = pair(kl.reshape(256, 128))
    first = W // Q
    u1 = np.zeros((CELLS, 16))
    u2 = np.zeros((CELLS, 16))
    for k in range(CELLS):
        u1[:, k + first] += s8[:, k]
        u2[:, k + first - 1] -= s8[:, k] / (Q * Q)
        u2[:, k + first + 1] -= s8[:, k] / (Q * Q)
    t["u"] = pair(np.concatenate([u1, u2, bl], axis=0))
    beside = eye(16, k=1) + eye(16, k=-1)
    k1 = 6.0 * eye(256) - np.kron(beside, eye(16)) - np.kron(eye(16), beside)
    t["k1"] = pair(k1 / (Q * Q))
    t["yb"] = pair(np.concatenate([columns_at(sy, np.arange(16) + b * CELLS - first) for b in range(N_GY)], axis=1))
    xa = [columns_at(sx, np.arange(16) + a * CELLS - first) for a in range(N_GX)]
    xa = [np.concatenate(xa[2 * i : 2 * i + 2], axis=1).T for i in range(N_GX // 2)]
    t["xa"] = pair(np.stack([np.repeat(v, CELLS, axis=0) for v in xa]))
    scale = Q * Q * (2.0 / (nx + 1)) * (2.0 / (ny + 1)) * (2.0 / (CELLS + 1))
    wc = scale / (m8.reshape(CELLS, 1, 1) + my.reshape(1, ny, 1) + mx.reshape(1, 1, nx))
    t["wc"] = wc.reshape(CELLS * ny, nx).astype(np.float32)
    edge = interp(-1, P_SIZE + 2, -1, CELLS + 2, Q)
    ends = edge[[0, P_SIZE + 1]]
    lateral = edge[1 : P_SIZE + 1]
    depth = interp(0, P_SIZE, 0, CELLS, Q)
    around = np.arange(CELLS + 2) - 1
    near = [columns_at(sy, around + b * CELLS).T for b in range(N_GY)]
    near = [np.concatenate([v, ends @ v, np.zeros((4, ny))], axis=0) for v in near]
    ey = np.zeros((N_GY, 16, CELLS, CELLS, ny))
    for k in range(CELLS):
        ey[:, :, k, k, :] = np.stack(near)
    t["ey"] = pair(ey.reshape(N_GY, 128, CELLS * ny))
    near = [columns_at(sx, around + a * CELLS).T for a in range(N_GX)]
    near = np.stack([np.concatenate([v, ends @ v], axis=0) for v in near]).reshape(N_GX // 2, 2, 12, nx)
    t["ex"] = pair(near.transpose(1, 2, 0, 3).reshape(2, 12 * (N_GX // 2), nx))
    t["s32"] = pair(s32)
    t["bd32"] = pair(np.kron(eye(4), s32))
    rm32 = m32.reshape(8, 1, 4, 1) + m32.reshape(1, 32, 1, 1) + m32.reshape(1, 1, 1, 32)
    t["rm32"] = ((2.0 / (P_SIZE + 1)) ** 3 / rm32).reshape(256, 128).astype(np.float32)
    t["sbz"] = pair(s32 @ basis)
    lz = s32 @ depth @ s8
    lane = np.arange(128)
    t["lz"] = lz[:, lane % 8].astype(np.float32)
    sel = np.zeros((4, 128, 128), np.float32)
    for f in range(4):
        for i in range((CELLS + 2) * CELLS):
            sel[f, i, 64 + f * 16 + i // 8] = 1.0
    t["sel"] = sel.reshape(512, 128).astype(ml_dtypes.bfloat16)
    tz2 = np.zeros((128, 32, 32))
    sb, sl = s32 @ basis, s32 @ lateral
    for f, layer in enumerate([0, P_SIZE - 1]):
        near = s32[:, layer]
        for i in range(NL):
            tz2[f * 16 + i] = near[:, None] * sb[None, :, i]
            tz2[32 + f * 16 + i] = near[None, :] * sb[:, None, i]
        for i in range(CELLS + 2):
            tz2[64 + f * 16 + i] = near[:, None] * sl[None, :, i]
            tz2[96 + f * 16 + i] = near[None, :] * sl[:, None, i]
    t["tz2"] = pair(tz2.reshape(128, 1024))
    return t


WIDE = {
    "bd": (0, 128, 0, 256),
    "ty": (128, 256, 0, 256),
    "tz": (384, 128, 0, 256),
    "tx1": (512, 1024, 0, 256),
    "k1": (1536, 256, 0, 256),
    "tx2a": (1792, 512, 0, 128),
    "tx2b": (1792, 512, 128, 128),
    "tx3": (2304, 256, 0, 128),
    "kl": (2304, 256, 128, 128),
}
SMALL = {"sc|": (0, 0, 64, 0, 96), "s32|": (0, 64, 32, 0, 96), "u|": (0, 96, 32, 0, 48), "sc=": (1, 0, 128, 0, 64), "s32=": (1, 0, 64, 64, 64)}


def in_row(table):
    return np.concatenate([table[0], table[1], table[0]], axis=1)


def in_block(table):
    return np.block([[table[0], table[0]], [table[1], np.zeros_like(table[1])]])


@functools.lru_cache(None)
def packs():
    t = tables()
    small = np.zeros((2, 256, 128), ml_dtypes.bfloat16)
    for name, (which, row, rows, lane, width) in SMALL.items():
        form = in_row if name[-1] == "|" else in_block
        small[which, row : row + rows, lane : lane + width] = form(t[name[:-1]])
    small[:, 128:256] = t["bd32"]
    parts = {**t, "tx2a": t["tx2"][:, :512], "tx2b": t["tx2"][:, 512:]}
    wide = np.zeros((2, 2560, 256), ml_dtypes.bfloat16)
    for name, (row, rows, lane, width) in WIDE.items():
        wide[:, row : row + rows, lane : lane + width] = parts[name]
    later = np.zeros((2, 128, 1408), ml_dtypes.bfloat16)
    later[:, :, :1024] = t["tz2"]
    later[:, :64, 1024:1152] = t["yb"]
    later[0, 64:96, 1024:1072] = in_row(t["sbz"])
    later[:, :, 1152:] = t["sel"].reshape(2, 2, 128, 128).transpose(0, 2, 1, 3).reshape(2, 128, 256)
    scales = np.zeros((768, 256), np.float32)
    scales[:512] = t["wc"]
    scales[512:, :128] = t["rm32"]
    scales[512:544, 128:] = t["lz"]
    return {
        "small": small,
        "wide": wide,
        "mu": t["mu"],
        "xa": t["xa"],
        "ey": t["ey"],
        "ex": t["ex"],
        "later": later,
        "scales": scales,
    }


class View:
    def __init__(self, ref, row, rows, lane, width):
        self.ref, self.rows, self.lanes = ref, slice(row, row + rows), slice(lane, lane + width)
        self.shape = (2, rows, width)

    def __getitem__(self, part):
        return self.ref[slice(None) if part is Ellipsis else part, self.rows, self.lanes]


def small_table(ref, name):
    which, row, rows, lane, width = SMALL[name]
    return ref[which, row : row + rows, lane : lane + width]


def split(x):
    high = x.astype(BF16)
    return high, (x - high.astype(F32)).astype(BF16)


def dot(x, y):
    return lax.dot_general(x, y, (((1,), (0,)), ((), ())), preferred_element_type=F32)


def dot_nt(x, y):
    return lax.dot_general(x, y, (((1,), (1,)), ((), ())), preferred_element_type=F32)


def times_table(x, table):
    high, low = split(x)
    rows = x.shape[0]
    if rows > 128:
        return dot(jnp.concatenate([high, low, high], axis=1), jnp.concatenate([table[0], table[0], table[1]], axis=0))
    if rows % 16:
        return dot(high, table[0]) + dot(low, table[0]) + dot(high, table[1])
    both = dot(jnp.concatenate([high, low], axis=0), table[0])
    return both[:rows] + both[rows:] + dot(high, table[1])


def table_times(table, x, product=dot):
    high, low = split(x)
    rows = table.shape[1]
    both = product(table[...].reshape(2 * rows, table.shape[2]), high)
    return both[:rows] + both[rows:] + product(table[0], low)


def row_times(table, x):
    high, low = split(x)
    return dot(table, jnp.concatenate([high, high, low], axis=0))


def block_times_nt(table, x):
    both = dot_nt(table, x)
    rows = table.shape[0] // 2
    return both[:rows] + both[rows:]


def spread(x, rows):
    high, low = split(x)
    high, low = high.astype(F32), low.astype(F32)
    for y in range(P_SIZE):
        part = slice(y * 32, y * 32 + 32)
        rows[pl.ds(y, x.shape[0], stride=P_SIZE), :] = jnp.concatenate([high[:, part], low[:, part]], axis=1)
    return rows[...].astype(BF16)


def stacked(x, width):
    return jnp.concatenate([x[:, i : i + width] for i in range(0, x.shape[1], width)], axis=0)


def unstacked(x, rows):
    return jnp.concatenate([x[i : i + rows] for i in range(0, x.shape[0], rows)], axis=1)


def lanes(rows):
    return lax.broadcasted_iota(jnp.int32, (rows, 128), 1)


FIRST = ("mu", "wide", "small")
NEXT = ("small", "xa", "ey", "ex", "later", "scales")
KEPT = (((2, 256, 128), BF16), ((2, 256, 256), BF16), ((2, 128, 512), BF16), ((2, 192, 256), BF16), ((2, 128, 1408), BF16), ((768, 256), F32))


def fetch_kernel(after_ref, *refs):
    places = {1: lax.axis_index("gs"), 2: lax.axis_index("gy"), 3: lax.axis_index("gc")}
    n = len(NEXT)
    copies = [
        pltpu.make_async_copy(source.at[places[i]] if i in places else source, target, refs[-1].at[i])
        for i, (source, target) in enumerate(zip(refs[:n], refs[n : 2 * n]))
    ]
    for copy in copies:
        copy.start()
    for copy in copies:
        copy.wait()


def first_kernel(q_hbm, mu_hbm, wide_hbm, small_hbm, m_ref, own_ref, spec_ref,
                 q, mu, wide, small, rows, rows32, ls, lp, ly, spill, sem):
    started = []

    def start(source, target):
        copy = pltpu.make_async_copy(source, target, sem.at[len(started)])
        started.append(copy)
        copy.start()
        return copy

    def part(first, last):
        return start(wide_hbm.at[:, first:last, :], wide.at[:, first:last, :])

    now = [start(q_hbm, q), start(small_hbm, small), part(0, 512), start(mu_hbm, mu)]
    for copy in now:
        copy.wait()
    soon = [part(512, 1536), part(1536, 2560)]
    t = {name: View(wide, *place) for name, place in WIDE.items()}
    x = row_times(small_table(small, "sc|"), q[...])
    x = block_times_nt(small_table(small, "sc="), spread(x, rows))
    x = times_table(stacked(x, 128), t["bd"])
    bd32 = View(small, 128, 128, 0, 128)
    y = row_times(small_table(small, "s32|"), q[...])
    y = block_times_nt(small_table(small, "s32="), spread(y, rows32))
    spec_ref[...] = times_table(stacked(y, 128), bd32)
    x = jnp.concatenate([x[i * 64 : i * 64 + 64] / (mu[16:80, :] + mu[i : i + 1, :]) for i in range(16)], axis=0)
    x = times_table(x, t["ty"])
    for i in range(4):
        z = table_times(t["tz"], x[i * 256 : i * 256 + 256])
        for j in range(4):
            k = i * 4 + j
            ls[:, k * 64 : k * 64 + 64] = z[j * 32 : j * 32 + 16, 0:64]
            lp[:, k * 64 : k * 64 + 64] = z[j * 32 + 16 : j * 32 + 32, 64:128]
            ly[:, k * 16 : k * 16 + 16] = z[j * 32 + 16 : j * 32 + 32, 128:144]
    for copy in soon:
        copy.wait()
    samples = times_table(ls[...], t["tx1"])
    coefs = times_table(lp[:, 0:512], t["tx2a"]) + times_table(lp[:, 512:1024], t["tx2b"]) + times_table(ly[...], t["tx3"])
    x = row_times(small_table(small, "u|"), samples)
    coefs = coefs - times_table(x[16:32], t["kl"])
    own_ref[...] = coefs
    x = (times_table(x[0:8], t["k1"]) + x[8:16]).T
    for i in range(16):
        spill[:, i * 8 : i * 8 + 8] = x[i * 16 : i * 16 + 16]
    spilled = spill[...]
    tile = jnp.zeros((8, 128), F32)
    for i in range(8):
        value = coefs[i % 2 * 8 : i % 2 * 8 + 8]
        shift = (16 * i - 64 - i // 2 * 16) % 128
        tile = jnp.where(lanes(8) // 16 == i, pltpu.roll(value, shift, 1) if shift else value, tile)
    for i in range(16):
        m_ref[i * 24 : i * 24 + 16, :] = spilled
        m_ref[i * 24 + 16 : i * 24 + 24, :] = tile


def unpacked(tile, source, slot):
    parts = []
    for half in range(2):
        shift = (16 * slot - source - 16 * half) % 128
        parts.append(pltpu.roll(tile, shift, 1) if shift else tile)
    return jnp.where(lanes(NL) // 16 == slot, jnp.concatenate(parts, axis=0), 0.0)


def strip_kernel(got_ref, own_ref, xa, ey, ex, later, scales, m_ref, coefs_ref):
    s, c, b = lax.axis_index("gs"), lax.axis_index("gc"), lax.axis_index("gy")
    source = [
        jnp.concatenate([got_ref[(i * 8 + j) * 24 : (i * 8 + j) * 24 + 16, :] for j in range(N_GY)], axis=0)
        for i in range(2)
    ]
    x = table_times(View(later, 0, 64, 1024, 128), jnp.concatenate(source, axis=1))
    lane = lax.broadcasted_iota(jnp.int32, (64, 256), 1)
    x = jnp.concatenate([jnp.where(lane % 8 == k, x, 0.0) for k in range(CELLS)], axis=0)
    x = times_table(x, xa) * scales[0:512, :]
    x = table_times(ey, x)
    x = table_times(ex, x, dot_nt)
    m_ref[...] = jnp.zeros((128, 128), F32)
    lane = lanes(16)
    for f in range(2):
        m_ref[pl.ds(f, 16, stride=8), :] = jnp.where(lane < 80, x[160 + f * 16 : 176 + f * 16], 0.0)
        value = jnp.zeros((16, 128), F32)
        for k in range(CELLS + 2):
            part = pltpu.roll(x[k * 16 : k * 16 + 16], (8 * (k - 10 - f)) % 128, 1)
            value = jnp.where(lane // 8 == k, part, value)
        m_ref[pl.ds(2 + f, 16, stride=8), :] = value

    def tile_of(i, j):
        return got_ref[pl.ds(pl.multiple_of((i * 8 + j) * 24 + 16, 8), 8), :]

    partner = tile_of(1 - c, b)
    outside = jnp.where(c == 0, pltpu.roll(partner, 64, 1), pltpu.roll(partner, 96, 1))
    outside = jnp.where(lanes(8) >= 96, outside, 0.0)
    target = s + 1 - 2 * c

    @pl.when((target >= 0) & (target < 16))
    def _():
        where = pl.ds(pl.multiple_of(target * 8, 8), 8)
        m_ref[where, :] = m_ref[where, :] + outside

    coefs = jnp.where(lane < 64, own_ref[...], 0.0)
    coefs = coefs + jnp.where(c == 0, unpacked(partner, 0, 1), unpacked(partner, 32, 0))
    above = unpacked(tile_of(c, jnp.minimum(b + 1, N_GY - 1)), 64, 3)
    below = unpacked(tile_of(c, jnp.maximum(b - 1, 0)), 96, 2)
    coefs = coefs + jnp.where(b < N_GY - 1, above, 0.0) + jnp.where(b > 0, below, 0.0)
    coefs_ref[...] = coefs


def last_kernel(m_ref, coefs_ref, spec_ref, small, later, scales, out_ref, rows, flat):
    s32, bd32 = small_table(small, "s32|"), View(small, 128, 128, 0, 128)
    got = jnp.sum(m_ref[...].reshape(16, 8, 128), axis=0)
    coefs = coefs_ref[...] + jnp.where(lax.axis_index("gc") == 0, unpacked(got, 96, 0), unpacked(got, 96, 1))
    lz = scales[512:544, 128:256]
    high, low = split(jnp.concatenate([lz * got[i : i + 1] for i in range(4)], axis=1))
    x = row_times(later[0, 64:96, 1024:1072], coefs)
    for i in range(4):
        part = jnp.concatenate([high[:, i * 128 : i * 128 + 128], low[:, i * 128 : i * 128 + 128]], axis=0)
        part = dot(part, later[i // 2, :, 1152 + i % 2 * 128 : 1280 + i % 2 * 128])
        x = x + part[:32] + part[32:]
    x = times_table(x, View(later, 0, 128, 0, 1024))
    x = (stacked(x, 128) + spec_ref[...]) * scales[512:768, 0:128]
    x = row_times(s32, unstacked(x, 32))
    x = times_table(stacked(x, 128), bd32)
    for i in range(8):
        rows[i * 128 : i * 128 + 128, :] = x[i * 32 : i * 32 + 32].T
    for y in range(P_SIZE):
        flat[:, y * 32 : y * 32 + 32] = rows[pl.ds(y, 32, stride=P_SIZE), :]
    out_ref[...] = row_times(s32, flat[...])


def vmem(count):
    return [pl.BlockSpec(memory_space=pltpu.VMEM)] * count


def hbm(count):
    return [pl.BlockSpec(memory_space=pltpu.HBM)] * count


def shape(*dims):
    return jax.ShapeDtypeStruct(dims, F32)


def params(mib):
    return pltpu.CompilerParams(vmem_limit_bytes=mib * 1024 * 1024)


def body(charge):
    t = {k: pltpu.with_memory_space_constraint(jnp.asarray(v), pltpu.HBM) for k, v in packs().items()}
    message, own, spec = pl.pallas_call(
        first_kernel,
        out_shape=[shape(384, 128), shape(NL, 128), shape(256, 128)],
        in_specs=hbm(4),
        out_specs=vmem(3),
        scratch_shapes=[
            pltpu.VMEM((32, 1024), F32),
            pltpu.VMEM((80, 256), F32),
            pltpu.VMEM((2, 2560, 256), BF16),
            pltpu.VMEM((2, 256, 128), BF16),
            pltpu.VMEM((2048, 64), F32),
            pltpu.VMEM((1024, 64), F32),
            pltpu.VMEM((16, 1024), F32),
            pltpu.VMEM((16, 1024), F32),
            pltpu.VMEM((16, 256), F32),
            pltpu.VMEM((16, 128), F32),
            pltpu.SemaphoreType.DMA((6,)),
        ],
        compiler_params=params(24),
        name="first",
    )(pltpu.with_memory_space_constraint(charge, pltpu.HBM), *[t[k] for k in FIRST])
    small, xa, ey, ex, later, scales = pl.pallas_call(
        fetch_kernel,
        out_shape=[jax.ShapeDtypeStruct(*k) for k in KEPT],
        in_specs=hbm(1 + len(NEXT)),
        out_specs=vmem(len(KEPT)),
        scratch_shapes=[pltpu.SemaphoreType.DMA((len(NEXT),))],
        compiler_params=params(12),
        name="fetch",
    )(own, *[t[k] for k in NEXT])
    strip = lax.all_to_all(message.reshape(16, 24, 128), ("gc", "gy"), 0, 0).reshape(384, 128)
    message, coefs = pl.pallas_call(
        strip_kernel,
        out_shape=(shape(128, 128), shape(NL, 128)),
        in_specs=vmem(7),
        out_specs=tuple(vmem(2)),
        compiler_params=params(12),
        name="strip",
    )(strip, own, xa, ey, ex, later, scales)
    arrived = lax.all_to_all(message.reshape(16, 8, 128), "gs", 0, 0).reshape(128, 128)
    return pl.pallas_call(
        last_kernel,
        out_shape=shape(32, 1024),
        in_specs=vmem(6),
        out_specs=vmem(1)[0],
        scratch_shapes=[pltpu.VMEM((1024, 32), F32), pltpu.VMEM((32, 1024), F32)],
        compiler_params=params(12),
        name="last",
    )(arrived, coefs, spec, small, later, scales)


def solution(mesh):
    strips = jax.sharding.Mesh(mesh.devices.reshape(N_GX // 2, 2, N_GY), ("gs", "gc", "gy"))
    spec = P(("gs", "gc"), "gy")
    return jax.shard_map(body, mesh=strips, in_specs=(spec,), out_specs=spec, check_vma=False)
```

```python
import functools

import jax
import jax.numpy as jnp
import ml_dtypes
import numpy as np
from jax import lax
from jax.experimental import pallas as pl
from jax.experimental.pallas import tpu as pltpu
from jax.sharding import PartitionSpec as P

P_SIZE = 32
W = 16
Q = 4
NL = 16
N_GX = 32
N_GY = 8
CELLS = P_SIZE // Q
BF16 = jnp.bfloat16
F32 = jnp.float32


def sine(length):
    counter = np.arange(length) + 1
    multiple = counter[:, None] * counter[None, :] % (2 * (length + 1))
    return np.sin(np.pi * multiple / (length + 1))


def eigen(length):
    return 2.0 - 2.0 * np.cos(np.pi * (np.arange(length) + 1) / (length + 1))


def interp(fine_start, fine_count, coarse_start, coarse_count, ratio):
    fine_pos = np.arange(fine_count) + fine_start
    coarse_pos = np.arange(coarse_count) + coarse_start
    numerator = 2 * fine_pos - (ratio - 1)
    lower_index = numerator // (2 * ratio)
    weight = ((numerator - 2 * ratio * lower_index) / (2.0 * ratio))[:, None]
    below = (coarse_pos[None, :] == lower_index[:, None]).astype(np.float64)
    above = (coarse_pos[None, :] == lower_index[:, None] + 1).astype(np.float64)
    return below * (1.0 - weight) + above * weight


def legendre(length, count):
    points = (2.0 * np.arange(length) + 1.0) / length - 1.0
    columns = [np.ones_like(points), points]
    for degree in range(2, count):
        columns.append(
            ((2 * degree - 1) * points * columns[-1] - (degree - 1) * columns[-2]) / degree
        )
    result = []
    for column in columns[:count]:
        vector = column
        for _ in range(2):
            for earlier in result:
                vector = vector - np.sum(earlier * vector) * earlier
        result.append(vector / np.sqrt(np.sum(vector * vector)))
    return np.stack(result, axis=1)


def columns_at(table, positions):
    positions = np.asarray(positions)
    inside = (positions >= 0) & (positions < table.shape[1])
    return table[:, np.clip(positions, 0, table.shape[1] - 1)] * inside


def pair(table):
    table = np.asarray(table, np.float64)
    high = table.astype(np.float32).astype(ml_dtypes.bfloat16)
    low = (table - high.astype(np.float64)).astype(np.float32).astype(ml_dtypes.bfloat16)
    return np.stack([high, low], axis=-3)


@functools.lru_cache(None)
def tables():
    t = {}
    n = P_SIZE + 2 * W
    s64, m64 = sine(n), eigen(n)
    s32, m32 = sine(P_SIZE), eigen(P_SIZE)
    s8, m8 = sine(CELLS), eigen(CELLS)
    nx, ny = CELLS * N_GX, CELLS * N_GY
    sx, mx = sine(nx), eigen(nx)
    sy, my = sine(ny), eigen(ny)
    eye = np.eye
    basis = legendre(P_SIZE, NL)
    fine = interp(0, n, 0, n // Q, Q)
    mean = np.kron(eye(n // Q), np.full((1, Q), 1.0 / Q))
    inside = slice(W, W + P_SIZE)
    places = [W - 1, W + P_SIZE, W, W + P_SIZE - 1]
    r = mean @ s64
    bs = basis.T @ s64[inside]
    st = s64[places]
    bl = basis.T @ fine[inside]
    lt = fine[places]
    lanes_x, lanes_y = [0, 16, 64, 80], [32, 48, 96, 112]
    sc = s64[:, inside]
    t["sc"] = pair(sc)
    t["bd"] = pair(np.kron(eye(4), sc.T))
    mu = np.zeros((16 + n, 256))
    mu[:16] = (m64.reshape(16, 4, 1) + m64).reshape(16, 256)
    mu[16:] = m64[:, None]
    t["mu"] = (mu * ((n + 1) / 2.0) ** 3).astype(np.float32)
    ty = np.zeros((4, n, 256))
    for i in range(4):
        ty[i, :, i * 16 : i * 16 + 16] = r.T
        ty[i, :, 64 + i * 16 : 64 + i * 16 + 16] = bs.T
        ty[i, :, 128 + i * 4 : 128 + i * 4 + 4] = st.T
    t["ty"] = pair(ty.reshape(4 * n, 256))
    t["tz"] = pair(np.kron(eye(4), np.concatenate([r, bs], axis=0)))
    t["tx1"] = pair(np.kron(r.T, eye(16)))
    tx2 = np.zeros((n, NL, 128))
    tx3 = np.zeros((n, 4, 128))
    kl = np.zeros((16, 16, 128))
    for i in range(4):
        at_x, at_y = slice(lanes_x[i], lanes_x[i] + NL), slice(lanes_y[i], lanes_y[i] + NL)
        tx2[:, :, at_x] = st[i][:, None, None] * eye(NL)
        kl[:, :, at_x] = lt[i][:, None, None] * bl.T[None]
        tx3[:, i, at_y] = bs.T
        kl[:, :, at_y] = bl.T[:, None, :] * lt[i][None, :, None]
    t["tx2"] = pair(tx2.reshape(n * NL, 128))
    t["tx3"] = pair(tx3.reshape(n * 4, 128))
    t["kl"] = pair(kl.reshape(256, 128))
    first = W // Q
    u1 = np.zeros((CELLS, 16))
    u2 = np.zeros((CELLS, 16))
    for k in range(CELLS):
        u1[:, k + first] += s8[:, k]
        u2[:, k + first - 1] -= s8[:, k] / (Q * Q)
        u2[:, k + first + 1] -= s8[:, k] / (Q * Q)
    t["u"] = pair(np.concatenate([u1, u2, bl], axis=0))
    beside = eye(16, k=1) + eye(16, k=-1)
    k1 = 6.0 * eye(256) - np.kron(beside, eye(16)) - np.kron(eye(16), beside)
    t["k1"] = pair(k1 / (Q * Q))
    t["yb"] = pair(np.concatenate([columns_at(sy, np.arange(16) + b * CELLS - first) for b in range(N_GY)], axis=1))
    xa = [columns_at(sx, np.arange(16) + a * CELLS - first) for a in range(N_GX)]
    xa = [np.concatenate(xa[2 * i : 2 * i + 2], axis=1).T for i in range(N_GX // 2)]
    t["xa"] = pair(np.stack([np.repeat(v, CELLS, axis=0) for v in xa]))
    scale = Q * Q * (2.0 / (nx + 1)) * (2.0 / (ny + 1)) * (2.0 / (CELLS + 1))
    wc = scale / (m8.reshape(CELLS, 1, 1) + my.reshape(1, ny, 1) + mx.reshape(1, 1, nx))
    t["wc"] = wc.reshape(CELLS * ny, nx).astype(np.float32)
    edge = interp(-1, P_SIZE + 2, -1, CELLS + 2, Q)
    ends = edge[[0, P_SIZE + 1]]
    lateral = edge[1 : P_SIZE + 1]
    depth = interp(0, P_SIZE, 0, CELLS, Q)
    around = np.arange(CELLS + 2) - 1
    near = [columns_at(sy, around + b * CELLS).T for b in range(N_GY)]
    near = [np.concatenate([v, ends @ v, np.zeros((4, ny))], axis=0) for v in near]
    ey = np.zeros((N_GY, 16, CELLS, CELLS, ny))
    for k in range(CELLS):
        ey[:, :, k, k, :] = np.stack(near)
    t["ey"] = pair(ey.reshape(N_GY, 128, CELLS * ny))
    near = [columns_at(sx, around + a * CELLS).T for a in range(N_GX)]
    near = np.stack([np.concatenate([v, ends @ v], axis=0) for v in near]).reshape(N_GX // 2, 2, 12, nx)
    t["ex"] = pair(near.transpose(1, 2, 0, 3).reshape(2, 12 * (N_GX // 2), nx))
    t["s32"] = pair(s32)
    t["bd32"] = pair(np.kron(eye(4), s32))
    rm32 = m32.reshape(8, 1, 4, 1) + m32.reshape(1, 32, 1, 1) + m32.reshape(1, 1, 1, 32)
    t["rm32"] = ((2.0 / (P_SIZE + 1)) ** 3 / rm32).reshape(256, 128).astype(np.float32)
    t["sbz"] = pair(s32 @ basis)
    lz = s32 @ depth @ s8
    lane = np.arange(128)
    t["lz"] = lz[:, lane % 8].astype(np.float32)
    sel = np.zeros((4, 128, 128), np.float32)
    for f in range(4):
        for i in range((CELLS + 2) * CELLS):
            sel[f, i, 64 + f * 16 + i // 8] = 1.0
    t["sel"] = sel.reshape(512, 128).astype(ml_dtypes.bfloat16)
    tz2 = np.zeros((128, 32, 32))
    sb, sl = s32 @ basis, s32 @ lateral
    for f, layer in enumerate([0, P_SIZE - 1]):
        near = s32[:, layer]
        for i in range(NL):
            tz2[f * 16 + i] = near[:, None] * sb[None, :, i]
            tz2[32 + f * 16 + i] = near[None, :] * sb[:, None, i]
        for i in range(CELLS + 2):
            tz2[64 + f * 16 + i] = near[:, None] * sl[None, :, i]
            tz2[96 + f * 16 + i] = near[None, :] * sl[:, None, i]
    t["tz2"] = pair(tz2.reshape(128, 1024))
    return t


WIDE = {
    "bd": (0, 128, 0, 256),
    "ty": (128, 256, 0, 256),
    "tz": (384, 128, 0, 256),
    "tx1": (512, 1024, 0, 256),
    "k1": (1536, 256, 0, 256),
    "tx2a": (1792, 512, 0, 128),
    "tx2b": (1792, 512, 128, 128),
    "tx3": (2304, 256, 0, 128),
    "kl": (2304, 256, 128, 128),
}
SMALL = {"sc|": (0, 0, 64, 0, 96), "s32|": (0, 64, 32, 0, 96), "u|": (0, 96, 32, 0, 48), "sc=": (1, 0, 128, 0, 64), "s32=": (1, 0, 64, 64, 64)}


def in_row(table):
    return np.concatenate([table[0], table[1], table[0]], axis=1)


def in_block(table):
    return np.block([[table[0], table[0]], [table[1], np.zeros_like(table[1])]])


@functools.lru_cache(None)
def packs():
    t = tables()
    small = np.zeros((2, 256, 128), ml_dtypes.bfloat16)
    for name, (which, row, rows, lane, width) in SMALL.items():
        form = in_row if name[-1] == "|" else in_block
        small[which, row : row + rows, lane : lane + width] = form(t[name[:-1]])
    small[:, 128:256] = t["bd32"]
    parts = {**t, "tx2a": t["tx2"][:, :512], "tx2b": t["tx2"][:, 512:]}
    wide = np.zeros((2, 2560, 256), ml_dtypes.bfloat16)
    for name, (row, rows, lane, width) in WIDE.items():
        wide[:, row : row + rows, lane : lane + width] = parts[name]
    later = np.zeros((2, 128, 1408), ml_dtypes.bfloat16)
    later[:, :, :1024] = t["tz2"]
    later[:, :64, 1024:1152] = t["yb"]
    later[0, 64:96, 1024:1072] = in_row(t["sbz"])
    later[:, :, 1152:] = t["sel"].reshape(2, 2, 128, 128).transpose(0, 2, 1, 3).reshape(2, 128, 256)
    scales = np.zeros((768, 256), np.float32)
    scales[:512] = t["wc"]
    scales[512:, :128] = t["rm32"]
    scales[512:544, 128:] = t["lz"]
    return {
        "small": small,
        "wide": wide,
        "mu": t["mu"],
        "xa": t["xa"],
        "ey": t["ey"],
        "ex": t["ex"],
        "later": later,
        "scales": scales,
    }


class View:
    def __init__(self, ref, row, rows, lane, width):
        self.ref, self.rows, self.lanes = ref, slice(row, row + rows), slice(lane, lane + width)
        self.shape = (2, rows, width)

    def __getitem__(self, part):
        return self.ref[slice(None) if part is Ellipsis else part, self.rows, self.lanes]


def small_table(ref, name):
    which, row, rows, lane, width = SMALL[name]
    return ref[which, row : row + rows, lane : lane + width]


def split(x):
    high = x.astype(BF16)
    return high, (x - high.astype(F32)).astype(BF16)


def dot(x, y):
    return lax.dot_general(x, y, (((1,), (0,)), ((), ())), preferred_element_type=F32)


def dot_nt(x, y):
    return lax.dot_general(x, y, (((1,), (1,)), ((), ())), preferred_element_type=F32)


def times_table(x, table):
    high, low = split(x)
    rows = x.shape[0]
    if rows > 128:
        return dot(jnp.concatenate([high, low, high], axis=1), jnp.concatenate([table[0], table[0], table[1]], axis=0))
    if rows % 16:
        return dot(high, table[0]) + dot(low, table[0]) + dot(high, table[1])
    both = dot(jnp.concatenate([high, low], axis=0), table[0])
    return both[:rows] + both[rows:] + dot(high, table[1])


def table_times(table, x, product=dot):
    high, low = split(x)
    rows = table.shape[1]
    both = product(table[...].reshape(2 * rows, table.shape[2]), high)
    return both[:rows] + both[rows:] + product(table[0], low)


def row_times(table, x):
    high, low = split(x)
    return dot(table, jnp.concatenate([high, high, low], axis=0))


def block_times_nt(table, x):
    both = dot_nt(table, x)
    rows = table.shape[0] // 2
    return both[:rows] + both[rows:]


def spread(x, rows):
    high, low = split(x)
    high, low = high.astype(F32), low.astype(F32)
    count = x.shape[0]
    for y in range(P_SIZE):
        part = slice(y * 32, y * 32 + 32)
        rows[y * count : y * count + count, :] = jnp.concatenate([high[:, part], low[:, part]], axis=1)
    found = [rows[pl.ds(k, P_SIZE, stride=count), :] for k in range(count)]
    return jnp.concatenate(found, axis=0).astype(BF16)


def stacked(x, width):
    return jnp.concatenate([x[:, i : i + width] for i in range(0, x.shape[1], width)], axis=0)


def unstacked(x, rows):
    return jnp.concatenate([x[i : i + rows] for i in range(0, x.shape[0], rows)], axis=1)


def lanes(rows):
    return lax.broadcasted_iota(jnp.int32, (rows, 128), 1)


FIRST = ("mu", "wide", "small")
NEXT = ("xa", "ey", "ex", "later", "scales")
KEPT = (((2, 256, 128), BF16), ((2, 256, 256), BF16), ((2, 128, 512), BF16), ((2, 192, 256), BF16), ((2, 128, 1408), BF16), ((768, 256), F32))


def first_kernel(q_hbm, mu_hbm, wide_hbm, small_hbm, xa_hbm, ey_hbm, ex_hbm, later_hbm, scales_hbm,
                 m_ref, own_ref, spec_ref, small, xa, ey, ex, later, scales,
                 q, mu, wide, rows, rows32, sem):
    started = []

    def start(source, target):
        copy = pltpu.make_async_copy(source, target, sem.at[len(started)])
        started.append(copy)
        copy.start()
        return copy

    def part(first, last):
        return start(wide_hbm.at[:, first:last, :], wide.at[:, first:last, :])

    now = [start(q_hbm, q), start(small_hbm, small)]
    soon = [part(0, 512), start(mu_hbm, mu)]
    for copy in now:
        copy.wait()
    late = [part(512, 1536), part(1536, 2560)]
    t = {name: View(wide, *place) for name, place in WIDE.items()}
    x = row_times(small_table(small, "sc|"), q[...])
    x = block_times_nt(small_table(small, "sc="), spread(x, rows))
    for copy in soon:
        copy.wait()
    ahead = [
        start(xa_hbm.at[lax.axis_index("gs")], xa),
        start(ey_hbm.at[lax.axis_index("gy")], ey),
        start(ex_hbm.at[lax.axis_index("gc")], ex),
        start(scales_hbm, scales),
        start(later_hbm, later),
    ]
    x = times_table(stacked(x, 128), t["bd"])
    bd32 = View(small, 128, 128, 0, 128)
    y = row_times(small_table(small, "s32|"), q[...])
    y = block_times_nt(small_table(small, "s32="), spread(y, rows32))
    spec_ref[...] = times_table(stacked(y, 128), bd32)
    x = jnp.concatenate([x[i * 64 : i * 64 + 64] / (mu[16:80, :] + mu[i : i + 1, :]) for i in range(16)], axis=0)
    x = times_table(x, t["ty"])
    lane = lanes(16)
    ls, lp, ly = [], [], []
    for i in range(4):
        z = table_times(t["tz"], x[i * 256 : i * 256 + 256])
        for j in range(0, 4, 2):
            one, two = z[j * 32 : j * 32 + 32, 0:128], z[j * 32 + 32 : j * 32 + 64, 0:128]
            ls.append(jnp.where(lane < 64, one[0:16], pltpu.roll(two[0:16], 64, 1)))
            lp.append(jnp.where(lane < 64, pltpu.roll(one[16:32], 64, 1), two[16:32]))
        for j in range(4):
            k = (i * 4 + j) % 8
            one = z[j * 32 + 16 : j * 32 + 32, 128:256]
            ly.append(pltpu.roll(one, 16 * k, 1) if k else one)
    ls, lp = jnp.concatenate(ls, axis=1), jnp.concatenate(lp, axis=1)
    ly = jnp.concatenate([sum(ly[1:8], ly[0]), sum(ly[9:16], ly[8])], axis=1)
    for copy in late:
        copy.wait()
    samples = times_table(ls, t["tx1"])
    coefs = times_table(lp[:, 0:512], t["tx2a"]) + times_table(lp[:, 512:1024], t["tx2b"]) + times_table(ly, t["tx3"])
    x = row_times(small_table(small, "u|"), samples)
    coefs = coefs - times_table(x[16:32], t["kl"])
    own_ref[...] = coefs
    x = (times_table(x[0:8], t["k1"]) + x[8:16]).T
    spilled = jnp.concatenate([x[i * 16 : i * 16 + 16] for i in range(16)], axis=1)
    tile = jnp.zeros((8, 128), F32)
    for i in range(8):
        value = coefs[i % 2 * 8 : i % 2 * 8 + 8]
        shift = (16 * i - 64 - i // 2 * 16) % 128
        tile = jnp.where(lanes(8) // 16 == i, pltpu.roll(value, shift, 1) if shift else value, tile)
    for i in range(16):
        m_ref[i * 24 : i * 24 + 16, :] = spilled
        m_ref[i * 24 + 16 : i * 24 + 24, :] = tile
    for copy in ahead:
        copy.wait()


def unpacked(tile, source, slot):
    parts = []
    for half in range(2):
        shift = (16 * slot - source - 16 * half) % 128
        parts.append(pltpu.roll(tile, shift, 1) if shift else tile)
    return jnp.where(lanes(NL) // 16 == slot, jnp.concatenate(parts, axis=0), 0.0)


def strip_kernel(got_ref, own_ref, xa, ey, ex, later, scales, m_ref, coefs_ref):
    s, c, b = lax.axis_index("gs"), lax.axis_index("gc"), lax.axis_index("gy")
    source = [
        jnp.concatenate([got_ref[(i * 8 + j) * 24 : (i * 8 + j) * 24 + 16, :] for j in range(N_GY)], axis=0)
        for i in range(2)
    ]
    x = table_times(View(later, 0, 64, 1024, 128), jnp.concatenate(source, axis=1))
    lane = lax.broadcasted_iota(jnp.int32, (64, 256), 1)
    x = jnp.concatenate([jnp.where(lane % 8 == k, x, 0.0) for k in range(CELLS)], axis=0)
    x = times_table(x, xa) * scales[0:512, :]
    x = table_times(ey, x)
    x = table_times(ex, x, dot_nt)
    m_ref[...] = jnp.zeros((128, 128), F32)
    lane = lanes(16)
    for f in range(2):
        m_ref[pl.ds(f, 16, stride=8), :] = jnp.where(lane < 80, x[160 + f * 16 : 176 + f * 16], 0.0)
        value = jnp.zeros((16, 128), F32)
        for k in range(CELLS + 2):
            part = pltpu.roll(x[k * 16 : k * 16 + 16], (8 * (k - 10 - f)) % 128, 1)
            value = jnp.where(lane // 8 == k, part, value)
        m_ref[pl.ds(2 + f, 16, stride=8), :] = value

    def tile_of(i, j):
        return got_ref[pl.ds(pl.multiple_of((i * 8 + j) * 24 + 16, 8), 8), :]

    partner = tile_of(1 - c, b)
    outside = jnp.where(c == 0, pltpu.roll(partner, 64, 1), pltpu.roll(partner, 96, 1))
    outside = jnp.where(lanes(8) >= 96, outside, 0.0)
    target = s + 1 - 2 * c

    @pl.when((target >= 0) & (target < 16))
    def _():
        where = pl.ds(pl.multiple_of(target * 8, 8), 8)
        m_ref[where, :] = m_ref[where, :] + outside

    coefs = jnp.where(lane < 64, own_ref[...], 0.0)
    coefs = coefs + jnp.where(c == 0, unpacked(partner, 0, 1), unpacked(partner, 32, 0))
    above = unpacked(tile_of(c, jnp.minimum(b + 1, N_GY - 1)), 64, 3)
    below = unpacked(tile_of(c, jnp.maximum(b - 1, 0)), 96, 2)
    coefs = coefs + jnp.where(b < N_GY - 1, above, 0.0) + jnp.where(b > 0, below, 0.0)
    coefs_ref[...] = coefs


def last_kernel(m_ref, coefs_ref, spec_ref, small, later, scales, out_ref, rows):
    s32, bd32 = small_table(small, "s32|"), View(small, 128, 128, 0, 128)
    got = jnp.sum(m_ref[...].reshape(16, 8, 128), axis=0)
    coefs = coefs_ref[...] + jnp.where(lax.axis_index("gc") == 0, unpacked(got, 96, 0), unpacked(got, 96, 1))
    lz = scales[512:544, 128:256]
    high, low = split(jnp.concatenate([lz * got[i : i + 1] for i in range(4)], axis=1))
    x = row_times(later[0, 64:96, 1024:1072], coefs)
    for i in range(4):
        part = jnp.concatenate([high[:, i * 128 : i * 128 + 128], low[:, i * 128 : i * 128 + 128]], axis=0)
        part = dot(part, later[i // 2, :, 1152 + i % 2 * 128 : 1280 + i % 2 * 128])
        x = x + part[:32] + part[32:]
    x = times_table(x, View(later, 0, 128, 0, 1024))
    x = (stacked(x, 128) + spec_ref[...]) * scales[512:768, 0:128]
    x = row_times(s32, unstacked(x, 32))
    x = times_table(stacked(x, 128), bd32)
    for i in range(8):
        rows[i * 128 : i * 128 + 128, :] = x[i * 32 : i * 32 + 32].T
    x = jnp.concatenate([rows[pl.ds(y, 32, stride=P_SIZE), :] for y in range(P_SIZE)], axis=1)
    out_ref[...] = row_times(s32, x)


def vmem(count):
    return [pl.BlockSpec(memory_space=pltpu.VMEM)] * count


def hbm(count):
    return [pl.BlockSpec(memory_space=pltpu.HBM)] * count


def shape(*dims):
    return jax.ShapeDtypeStruct(dims, F32)


def params(mib):
    return pltpu.CompilerParams(vmem_limit_bytes=mib * 1024 * 1024)


def body(charge):
    t = {k: pltpu.with_memory_space_constraint(jnp.asarray(v), pltpu.HBM) for k, v in packs().items()}
    message, own, spec, small, xa, ey, ex, later, scales = pl.pallas_call(
        first_kernel,
        out_shape=[shape(384, 128), shape(NL, 128), shape(256, 128)] + [jax.ShapeDtypeStruct(*k) for k in KEPT],
        in_specs=hbm(1 + len(FIRST) + len(NEXT)),
        out_specs=vmem(3 + len(KEPT)),
        scratch_shapes=[
            pltpu.VMEM((32, 1024), F32),
            pltpu.VMEM((80, 256), F32),
            pltpu.VMEM((2, 2560, 256), BF16),
            pltpu.VMEM((2048, 64), F32),
            pltpu.VMEM((1024, 64), F32),
            pltpu.SemaphoreType.DMA((11,)),
        ],
        compiler_params=params(24),
        name="first",
    )(pltpu.with_memory_space_constraint(charge, pltpu.HBM), *[t[k] for k in FIRST + NEXT])
    strip = lax.all_to_all(message.reshape(16, 24, 128), ("gc", "gy"), 0, 0).reshape(384, 128)
    message, coefs = pl.pallas_call(
        strip_kernel,
        out_shape=(shape(128, 128), shape(NL, 128)),
        in_specs=vmem(7),
        out_specs=tuple(vmem(2)),
        compiler_params=params(12),
        name="strip",
    )(strip, own, xa, ey, ex, later, scales)
    arrived = lax.all_to_all(message.reshape(16, 8, 128), "gs", 0, 0).reshape(128, 128)
    return pl.pallas_call(
        last_kernel,
        out_shape=shape(32, 1024),
        in_specs=vmem(6),
        out_specs=vmem(1)[0],
        scratch_shapes=[pltpu.VMEM((1024, 32), F32)],
        compiler_params=params(12),
        name="last",
    )(arrived, coefs, spec, small, later, scales)


def solution(mesh):
    strips = jax.sharding.Mesh(mesh.devices.reshape(N_GX // 2, 2, N_GY), ("gs", "gc", "gy"))
    spec = P(("gs", "gc"), "gy")
    return jax.shard_map(body, mesh=strips, in_specs=(spec,), out_specs=spec, check_vma=False)
```

```python
import functools

import jax
import jax.numpy as jnp
import ml_dtypes
import numpy as np
from jax import lax
from jax.experimental import pallas as pl
from jax.experimental.pallas import tpu as pltpu
from jax.sharding import PartitionSpec as P

P_SIZE = 32
W = 16
Q = 4
NL = 16
N_GX = 32
N_GY = 8
CELLS = P_SIZE // Q
BF16 = jnp.bfloat16
F32 = jnp.float32


def sine(length):
    counter = np.arange(length) + 1
    multiple = counter[:, None] * counter[None, :] % (2 * (length + 1))
    return np.sin(np.pi * multiple / (length + 1))


def eigen(length):
    return 2.0 - 2.0 * np.cos(np.pi * (np.arange(length) + 1) / (length + 1))


def interp(fine_start, fine_count, coarse_start, coarse_count, ratio):
    fine_pos = np.arange(fine_count) + fine_start
    coarse_pos = np.arange(coarse_count) + coarse_start
    numerator = 2 * fine_pos - (ratio - 1)
    lower_index = numerator // (2 * ratio)
    weight = ((numerator - 2 * ratio * lower_index) / (2.0 * ratio))[:, None]
    below = (coarse_pos[None, :] == lower_index[:, None]).astype(np.float64)
    above = (coarse_pos[None, :] == lower_index[:, None] + 1).astype(np.float64)
    return below * (1.0 - weight) + above * weight


def legendre(length, count):
    points = (2.0 * np.arange(length) + 1.0) / length - 1.0
    columns = [np.ones_like(points), points]
    for degree in range(2, count):
        columns.append(
            ((2 * degree - 1) * points * columns[-1] - (degree - 1) * columns[-2]) / degree
        )
    result = []
    for column in columns[:count]:
        vector = column
        for _ in range(2):
            for earlier in result:
                vector = vector - np.sum(earlier * vector) * earlier
        result.append(vector / np.sqrt(np.sum(vector * vector)))
    return np.stack(result, axis=1)


def columns_at(table, positions):
    positions = np.asarray(positions)
    inside = (positions >= 0) & (positions < table.shape[1])
    return table[:, np.clip(positions, 0, table.shape[1] - 1)] * inside


def pair(table):
    table = np.asarray(table, np.float64)
    high = table.astype(np.float32).astype(ml_dtypes.bfloat16)
    low = (table - high.astype(np.float64)).astype(np.float32).astype(ml_dtypes.bfloat16)
    return np.stack([high, low], axis=-3)


@functools.lru_cache(None)
def tables():
    t = {}
    n = P_SIZE + 2 * W
    s64, m64 = sine(n), eigen(n)
    s32, m32 = sine(P_SIZE), eigen(P_SIZE)
    s8, m8 = sine(CELLS), eigen(CELLS)
    nx, ny = CELLS * N_GX, CELLS * N_GY
    sx, mx = sine(nx), eigen(nx)
    sy, my = sine(ny), eigen(ny)
    eye = np.eye
    basis = legendre(P_SIZE, NL)
    fine = interp(0, n, 0, n // Q, Q)
    mean = np.kron(eye(n // Q), np.full((1, Q), 1.0 / Q))
    inside = slice(W, W + P_SIZE)
    places = [W - 1, W + P_SIZE, W, W + P_SIZE - 1]
    r = mean @ s64
    bs = basis.T @ s64[inside]
    st = s64[places]
    bl = basis.T @ fine[inside]
    lt = fine[places]
    lanes_x, lanes_y = [0, 16, 64, 80], [32, 48, 96, 112]
    sc = s64[:, inside]
    t["sc"] = pair(sc)
    t["bd"] = pair(np.kron(eye(4), sc.T))
    mu = np.zeros((16 + n, 256))
    mu[:16] = (m64.reshape(16, 4, 1) + m64).reshape(16, 256)
    mu[16:] = m64[:, None]
    t["mu"] = (mu * ((n + 1) / 2.0) ** 3).astype(np.float32)
    ty = np.zeros((4, n, 256))
    for i in range(4):
        ty[i, :, i * 16 : i * 16 + 16] = r.T
        ty[i, :, 64 + i * 16 : 64 + i * 16 + 16] = bs.T
        ty[i, :, 128 + i * 4 : 128 + i * 4 + 4] = st.T
    t["ty"] = pair(ty.reshape(4 * n, 256))
    t["tz"] = pair(np.kron(eye(4), np.concatenate([r, bs], axis=0)))
    t["tx1"] = pair(np.kron(r.T, eye(16)))
    tx2 = np.zeros((n, NL, 128))
    tx3 = np.zeros((n, 4, 128))
    kl = np.zeros((16, 16, 128))
    for i in range(4):
        at_x, at_y = slice(lanes_x[i], lanes_x[i] + NL), slice(lanes_y[i], lanes_y[i] + NL)
        tx2[:, :, at_x] = st[i][:, None, None] * eye(NL)
        kl[:, :, at_x] = lt[i][:, None, None] * bl.T[None]
        tx3[:, i, at_y] = bs.T
        kl[:, :, at_y] = bl.T[:, None, :] * lt[i][None, :, None]
    t["tx2"] = pair(tx2.reshape(n * NL, 128))
    t["tx3"] = pair(tx3.reshape(n * 4, 128))
    t["kl"] = pair(kl.reshape(256, 128))
    first = W // Q
    u1 = np.zeros((CELLS, 16))
    u2 = np.zeros((CELLS, 16))
    for k in range(CELLS):
        u1[:, k + first] += s8[:, k]
        u2[:, k + first - 1] -= s8[:, k] / (Q * Q)
        u2[:, k + first + 1] -= s8[:, k] / (Q * Q)
    t["u"] = pair(np.concatenate([u1, u2, bl], axis=0))
    beside = eye(16, k=1) + eye(16, k=-1)
    k1 = 6.0 * eye(256) - np.kron(beside, eye(16)) - np.kron(eye(16), beside)
    t["k1"] = pair(k1 / (Q * Q))
    t["yb"] = pair(np.concatenate([columns_at(sy, np.arange(16) + b * CELLS - first) for b in range(N_GY)], axis=1))
    xa = [columns_at(sx, np.arange(16) + a * CELLS - first) for a in range(N_GX)]
    xa = [np.concatenate(xa[2 * i : 2 * i + 2], axis=1).T for i in range(N_GX // 2)]
    t["xa"] = pair(np.stack([np.repeat(v, CELLS, axis=0) for v in xa]))
    scale = Q * Q * (2.0 / (nx + 1)) * (2.0 / (ny + 1)) * (2.0 / (CELLS + 1))
    wc = scale / (m8.reshape(CELLS, 1, 1) + my.reshape(1, ny, 1) + mx.reshape(1, 1, nx))
    t["wc"] = wc.reshape(CELLS * ny, nx).astype(np.float32)
    edge = interp(-1, P_SIZE + 2, -1, CELLS + 2, Q)
    ends = edge[[0, P_SIZE + 1]]
    lateral = edge[1 : P_SIZE + 1]
    depth = interp(0, P_SIZE, 0, CELLS, Q)
    around = np.arange(CELLS + 2) - 1
    near = [columns_at(sy, around + b * CELLS).T for b in range(N_GY)]
    near = [np.concatenate([v, ends @ v, np.zeros((4, ny))], axis=0) for v in near]
    ey = np.zeros((N_GY, 16, CELLS, CELLS, ny))
    for k in range(CELLS):
        ey[:, :, k, k, :] = np.stack(near)
    t["ey"] = pair(ey.reshape(N_GY, 128, CELLS * ny))
    near = [columns_at(sx, around + a * CELLS).T for a in range(N_GX)]
    near = np.stack([np.concatenate([v, ends @ v], axis=0) for v in near]).reshape(N_GX // 2, 2, 12, nx)
    t["ex"] = pair(near.transpose(1, 2, 0, 3).reshape(2, 12 * (N_GX // 2), nx))
    t["s32"] = pair(s32)
    t["bd32"] = pair(np.kron(eye(4), s32))
    rm32 = m32.reshape(8, 1, 4, 1) + m32.reshape(1, 32, 1, 1) + m32.reshape(1, 1, 1, 32)
    t["rm32"] = ((2.0 / (P_SIZE + 1)) ** 3 / rm32).reshape(256, 128).astype(np.float32)
    t["sbz"] = pair(s32 @ basis)
    lz = s32 @ depth @ s8
    lane = np.arange(128)
    t["lz"] = lz[:, lane % 8].astype(np.float32)
    sel = np.zeros((4, 128, 128), np.float32)
    for f in range(4):
        for i in range((CELLS + 2) * CELLS):
            sel[f, i, 64 + f * 16 + i // 8] = 1.0
    t["sel"] = sel.reshape(512, 128).astype(ml_dtypes.bfloat16)
    tz2 = np.zeros((128, 32, 32))
    sb, sl = s32 @ basis, s32 @ lateral
    for f, layer in enumerate([0, P_SIZE - 1]):
        near = s32[:, layer]
        for i in range(NL):
            tz2[f * 16 + i] = near[:, None] * sb[None, :, i]
            tz2[32 + f * 16 + i] = near[None, :] * sb[:, None, i]
        for i in range(CELLS + 2):
            tz2[64 + f * 16 + i] = near[:, None] * sl[None, :, i]
            tz2[96 + f * 16 + i] = near[None, :] * sl[:, None, i]
    t["tz2"] = pair(tz2.reshape(128, 1024))
    return t


WIDE = {
    "bd": (0, 128, 0, 256),
    "ty": (128, 256, 0, 256),
    "tz": (384, 128, 0, 256),
    "tx1": (512, 1024, 0, 256),
    "k1": (1536, 256, 0, 256),
    "tx2a": (1792, 512, 0, 128),
    "tx2b": (1792, 512, 128, 128),
    "tx3": (2304, 256, 0, 128),
    "kl": (2304, 256, 128, 128),
}
SMALL = {"sc|": (0, 0, 64, 0, 96), "s32|": (0, 64, 32, 0, 96), "u|": (0, 96, 32, 0, 48), "sc=": (1, 0, 128, 0, 64), "s32=": (1, 0, 64, 64, 64)}


def in_row(table):
    return np.concatenate([table[0], table[1], table[0]], axis=1)


def in_block(table):
    return np.block([[table[0], table[0]], [table[1], np.zeros_like(table[1])]])


@functools.lru_cache(None)
def packs():
    t = tables()
    small = np.zeros((2, 256, 128), ml_dtypes.bfloat16)
    for name, (which, row, rows, lane, width) in SMALL.items():
        form = in_row if name[-1] == "|" else in_block
        small[which, row : row + rows, lane : lane + width] = form(t[name[:-1]])
    small[:, 128:256] = t["bd32"]
    parts = {**t, "tx2a": t["tx2"][:, :512], "tx2b": t["tx2"][:, 512:]}
    wide = np.zeros((2, 2560, 256), ml_dtypes.bfloat16)
    for name, (row, rows, lane, width) in WIDE.items():
        wide[:, row : row + rows, lane : lane + width] = parts[name]
    later = np.zeros((2, 128, 1408), ml_dtypes.bfloat16)
    later[:, :, :1024] = t["tz2"]
    later[:, :64, 1024:1152] = t["yb"]
    later[0, 64:96, 1024:1072] = in_row(t["sbz"])
    later[:, :, 1152:] = t["sel"].reshape(2, 2, 128, 128).transpose(0, 2, 1, 3).reshape(2, 128, 256)
    scales = np.zeros((768, 256), np.float32)
    scales[:512] = t["wc"]
    scales[512:, :128] = t["rm32"]
    scales[512:544, 128:] = t["lz"]
    return {
        "small": small,
        "wide": wide,
        "mu": t["mu"],
        "xa": t["xa"],
        "ey": t["ey"],
        "ex": t["ex"],
        "later": later,
        "scales": scales,
    }


class View:
    def __init__(self, ref, row, rows, lane, width):
        self.ref, self.rows, self.lanes = ref, slice(row, row + rows), slice(lane, lane + width)
        self.shape = (2, rows, width)

    def __getitem__(self, part):
        return self.ref[slice(None) if part is Ellipsis else part, self.rows, self.lanes]


def small_table(ref, name):
    which, row, rows, lane, width = SMALL[name]
    return ref[which, row : row + rows, lane : lane + width]


def split(x):
    high = x.astype(BF16)
    return high, (x - high.astype(F32)).astype(BF16)


def dot(x, y):
    return lax.dot_general(x, y, (((1,), (0,)), ((), ())), preferred_element_type=F32)


def dot_nt(x, y):
    return lax.dot_general(x, y, (((1,), (1,)), ((), ())), preferred_element_type=F32)


def times_table(x, table):
    high, low = split(x)
    rows = x.shape[0]
    if rows > 128:
        return dot(jnp.concatenate([high, low, high], axis=1), jnp.concatenate([table[0], table[0], table[1]], axis=0))
    if rows % 16:
        return dot(high, table[0]) + dot(low, table[0]) + dot(high, table[1])
    both = dot(jnp.concatenate([high, low], axis=0), table[0])
    return both[:rows] + both[rows:] + dot(high, table[1])


def table_times(table, x, product=dot):
    high, low = split(x)
    rows = table.shape[1]
    both = product(table[...].reshape(2 * rows, table.shape[2]), high)
    return both[:rows] + both[rows:] + product(table[0], low)


def row_times(table, x):
    high, low = split(x)
    return dot(table, jnp.concatenate([high, high, low], axis=0))


def block_times_nt(table, x):
    both = dot_nt(table, x)
    rows = table.shape[0] // 2
    return both[:rows] + both[rows:]


def spread(x, rows):
    high, low = split(x)
    high, low = high.astype(F32), low.astype(F32)
    count = x.shape[0]
    for y in range(P_SIZE):
        part = slice(y * 32, y * 32 + 32)
        rows[y * (count + 1) : y * (count + 1) + count, :] = jnp.concatenate([high[:, part], low[:, part]], axis=1)
    found = [rows[pl.ds(k, P_SIZE, stride=count + 1), :] for k in range(count)]
    return jnp.concatenate(found, axis=0).astype(BF16)


def stacked(x, width):
    return jnp.concatenate([x[:, i : i + width] for i in range(0, x.shape[1], width)], axis=0)


def unstacked(x, rows):
    return jnp.concatenate([x[i : i + rows] for i in range(0, x.shape[0], rows)], axis=1)


def lanes(rows):
    return lax.broadcasted_iota(jnp.int32, (rows, 128), 1)


FIRST = ("mu", "wide", "small")
NEXT = ("xa", "ey", "ex", "later", "scales")
KEPT = (((2, 256, 128), BF16), ((2, 256, 256), BF16), ((2, 128, 512), BF16), ((2, 192, 256), BF16), ((2, 128, 1408), BF16), ((768, 256), F32))


def first_kernel(q_hbm, mu_hbm, wide_hbm, small_hbm, xa_hbm, ey_hbm, ex_hbm, later_hbm, scales_hbm,
                 m_ref, own_ref, spec_ref, small, xa, ey, ex, later, scales,
                 q, mu, wide, rows, rows32, sem):
    started = []

    def start(source, target):
        copy = pltpu.make_async_copy(source, target, sem.at[len(started)])
        started.append(copy)
        copy.start()
        return copy

    def part(first, last):
        return start(wide_hbm.at[:, first:last, :], wide.at[:, first:last, :])

    now = [start(q_hbm, q), start(small_hbm, small)]
    soon = [part(0, 512), start(mu_hbm, mu)]
    for copy in now:
        copy.wait()
    late = [part(512, 1536), part(1536, 2560)]
    ahead = [
        start(xa_hbm.at[lax.axis_index("gs")], xa),
        start(ey_hbm.at[lax.axis_index("gy")], ey),
        start(ex_hbm.at[lax.axis_index("gc")], ex),
        start(scales_hbm, scales),
        start(later_hbm, later),
    ]
    t = {name: View(wide, *place) for name, place in WIDE.items()}
    x = row_times(small_table(small, "sc|"), q[...])
    x = block_times_nt(small_table(small, "sc="), spread(x, rows))
    for copy in soon:
        copy.wait()
    x = times_table(stacked(x, 128), t["bd"])
    bd32 = View(small, 128, 128, 0, 128)
    y = row_times(small_table(small, "s32|"), q[...])
    y = block_times_nt(small_table(small, "s32="), spread(y, rows32))
    spec_ref[...] = times_table(stacked(y, 128), bd32)
    x = jnp.concatenate([x[i * 64 : i * 64 + 64] / (mu[16:80, :] + mu[i : i + 1, :]) for i in range(16)], axis=0)
    x = times_table(x, t["ty"])
    lane = lanes(16)
    ls, lp, ly = [], [], []
    for i in range(4):
        z = table_times(t["tz"], x[i * 256 : i * 256 + 256])
        for j in range(0, 4, 2):
            one, two = z[j * 32 : j * 32 + 32, 0:128], z[j * 32 + 32 : j * 32 + 64, 0:128]
            ls.append(jnp.where(lane < 64, one[0:16], pltpu.roll(two[0:16], 64, 1)))
            lp.append(jnp.where(lane < 64, pltpu.roll(one[16:32], 64, 1), two[16:32]))
        for j in range(4):
            k = (i * 4 + j) % 8
            one = z[j * 32 + 16 : j * 32 + 32, 128:256]
            ly.append(pltpu.roll(one, 16 * k, 1) if k else one)
    ls, lp = jnp.concatenate(ls, axis=1), jnp.concatenate(lp, axis=1)
    ly = jnp.concatenate([sum(ly[1:8], ly[0]), sum(ly[9:16], ly[8])], axis=1)
    for copy in late:
        copy.wait()
    samples = times_table(ls, t["tx1"])
    coefs = times_table(lp[:, 0:512], t["tx2a"]) + times_table(lp[:, 512:1024], t["tx2b"]) + times_table(ly, t["tx3"])
    x = row_times(small_table(small, "u|"), samples)
    coefs = coefs - times_table(x[16:32], t["kl"])
    own_ref[...] = coefs
    x = (times_table(x[0:8], t["k1"]) + x[8:16]).T
    spilled = jnp.concatenate([x[i * 16 : i * 16 + 16] for i in range(16)], axis=1)
    tile = jnp.zeros((8, 128), F32)
    for i in range(8):
        value = coefs[i % 2 * 8 : i % 2 * 8 + 8]
        shift = (16 * i - 64 - i // 2 * 16) % 128
        tile = jnp.where(lanes(8) // 16 == i, pltpu.roll(value, shift, 1) if shift else value, tile)
    for i in range(16):
        m_ref[i * 24 : i * 24 + 16, :] = spilled
        m_ref[i * 24 + 16 : i * 24 + 24, :] = tile
    for copy in ahead:
        copy.wait()


def unpacked(tile, source, slot):
    parts = []
    for half in range(2):
        shift = (16 * slot - source - 16 * half) % 128
        parts.append(pltpu.roll(tile, shift, 1) if shift else tile)
    return jnp.where(lanes(NL) // 16 == slot, jnp.concatenate(parts, axis=0), 0.0)


def strip_kernel(got_ref, own_ref, xa, ey, ex, later, scales, m_ref, coefs_ref):
    s, c, b = lax.axis_index("gs"), lax.axis_index("gc"), lax.axis_index("gy")
    source = [
        jnp.concatenate([got_ref[(i * 8 + j) * 24 : (i * 8 + j) * 24 + 16, :] for j in range(N_GY)], axis=0)
        for i in range(2)
    ]
    x = table_times(View(later, 0, 64, 1024, 128), jnp.concatenate(source, axis=1))
    lane = lax.broadcasted_iota(jnp.int32, (64, 256), 1)
    x = jnp.concatenate([jnp.where(lane % 8 == k, x, 0.0) for k in range(CELLS)], axis=0)
    x = times_table(x, xa) * scales[0:512, :]
    x = table_times(ey, x)
    x = table_times(ex, x, dot_nt)
    m_ref[...] = jnp.zeros((128, 128), F32)
    lane = lanes(16)
    for f in range(2):
        m_ref[pl.ds(f, 16, stride=8), :] = jnp.where(lane < 80, x[160 + f * 16 : 176 + f * 16], 0.0)
        value = jnp.zeros((16, 128), F32)
        for k in range(CELLS + 2):
            part = pltpu.roll(x[k * 16 : k * 16 + 16], (8 * (k - 10 - f)) % 128, 1)
            value = jnp.where(lane // 8 == k, part, value)
        m_ref[pl.ds(2 + f, 16, stride=8), :] = value

    def tile_of(i, j):
        return got_ref[pl.ds(pl.multiple_of((i * 8 + j) * 24 + 16, 8), 8), :]

    partner = tile_of(1 - c, b)
    outside = jnp.where(c == 0, pltpu.roll(partner, 64, 1), pltpu.roll(partner, 96, 1))
    outside = jnp.where(lanes(8) >= 96, outside, 0.0)
    target = s + 1 - 2 * c

    @pl.when((target >= 0) & (target < 16))
    def _():
        where = pl.ds(pl.multiple_of(target * 8, 8), 8)
        m_ref[where, :] = m_ref[where, :] + outside

    coefs = jnp.where(lane < 64, own_ref[...], 0.0)
    coefs = coefs + jnp.where(c == 0, unpacked(partner, 0, 1), unpacked(partner, 32, 0))
    above = unpacked(tile_of(c, jnp.minimum(b + 1, N_GY - 1)), 64, 3)
    below = unpacked(tile_of(c, jnp.maximum(b - 1, 0)), 96, 2)
    coefs = coefs + jnp.where(b < N_GY - 1, above, 0.0) + jnp.where(b > 0, below, 0.0)
    coefs_ref[...] = coefs


def last_kernel(m_ref, coefs_ref, spec_ref, small, later, scales, out_ref, rows):
    s32, bd32 = small_table(small, "s32|"), View(small, 128, 128, 0, 128)
    got = jnp.sum(m_ref[...].reshape(16, 8, 128), axis=0)
    coefs = coefs_ref[...] + jnp.where(lax.axis_index("gc") == 0, unpacked(got, 96, 0), unpacked(got, 96, 1))
    lz = scales[512:544, 128:256]
    high, low = split(jnp.concatenate([lz * got[i : i + 1] for i in range(4)], axis=1))
    x = row_times(later[0, 64:96, 1024:1072], coefs)
    for i in range(4):
        part = jnp.concatenate([high[:, i * 128 : i * 128 + 128], low[:, i * 128 : i * 128 + 128]], axis=0)
        part = dot(part, later[i // 2, :, 1152 + i % 2 * 128 : 1280 + i % 2 * 128])
        x = x + part[:32] + part[32:]
    x = times_table(x, View(later, 0, 128, 0, 1024))
    x = (stacked(x, 128) + spec_ref[...]) * scales[512:768, 0:128]
    x = row_times(s32, unstacked(x, 32))
    x = times_table(stacked(x, 128), bd32)
    for i in range(8):
        turned = x[i * 32 : i * 32 + 32].T
        for j in range(4):
            rows[(i * 4 + j) * 33 : (i * 4 + j) * 33 + 32, :] = turned[j * 32 : j * 32 + 32]
    x = jnp.concatenate([rows[pl.ds(y, 32, stride=P_SIZE + 1), :] for y in range(P_SIZE)], axis=1)
    out_ref[...] = row_times(s32, x)


def vmem(count):
    return [pl.BlockSpec(memory_space=pltpu.VMEM)] * count


def hbm(count):
    return [pl.BlockSpec(memory_space=pltpu.HBM)] * count


def shape(*dims):
    return jax.ShapeDtypeStruct(dims, F32)


def params(mib):
    return pltpu.CompilerParams(vmem_limit_bytes=mib * 1024 * 1024)


def body(charge):
    t = {k: pltpu.with_memory_space_constraint(jnp.asarray(v), pltpu.HBM) for k, v in packs().items()}
    message, own, spec, small, xa, ey, ex, later, scales = pl.pallas_call(
        first_kernel,
        out_shape=[shape(384, 128), shape(NL, 128), shape(256, 128)] + [jax.ShapeDtypeStruct(*k) for k in KEPT],
        in_specs=hbm(1 + len(FIRST) + len(NEXT)),
        out_specs=vmem(3 + len(KEPT)),
        scratch_shapes=[
            pltpu.VMEM((32, 1024), F32),
            pltpu.VMEM((80, 256), F32),
            pltpu.VMEM((2, 2560, 256), BF16),
            pltpu.VMEM((2080, 64), F32),
            pltpu.VMEM((1056, 64), F32),
            pltpu.SemaphoreType.DMA((11,)),
        ],
        compiler_params=params(24),
        name="first",
    )(pltpu.with_memory_space_constraint(charge, pltpu.HBM), *[t[k] for k in FIRST + NEXT])
    strip = lax.all_to_all(message.reshape(16, 24, 128), ("gc", "gy"), 0, 0).reshape(384, 128)
    message, coefs = pl.pallas_call(
        strip_kernel,
        out_shape=(shape(128, 128), shape(NL, 128)),
        in_specs=vmem(7),
        out_specs=tuple(vmem(2)),
        compiler_params=params(12),
        name="strip",
    )(strip, own, xa, ey, ex, later, scales)
    arrived = lax.all_to_all(message.reshape(16, 8, 128), "gs", 0, 0).reshape(128, 128)
    return pl.pallas_call(
        last_kernel,
        out_shape=shape(32, 1024),
        in_specs=vmem(6),
        out_specs=vmem(1)[0],
        scratch_shapes=[pltpu.VMEM((1056, 32), F32)],
        compiler_params=params(12),
        name="last",
    )(arrived, coefs, spec, small, later, scales)


def solution(mesh):
    strips = jax.sharding.Mesh(mesh.devices.reshape(N_GX // 2, 2, N_GY), ("gs", "gc", "gy"))
    spec = P(("gs", "gc"), "gy")
    return jax.shard_map(body, mesh=strips, in_specs=(spec,), out_specs=spec, check_vma=False)
```

```python
import functools

import jax
import jax.numpy as jnp
import ml_dtypes
import numpy as np
from jax import lax
from jax.experimental import pallas as pl
from jax.experimental.pallas import tpu as pltpu
from jax.sharding import PartitionSpec as P

P_SIZE = 32
W = 16
Q = 4
NL = 16
N_GX = 32
N_GY = 8
CELLS = P_SIZE // Q
BF16 = jnp.bfloat16
F32 = jnp.float32


def sine(length):
    counter = np.arange(length) + 1
    multiple = counter[:, None] * counter[None, :] % (2 * (length + 1))
    return np.sin(np.pi * multiple / (length + 1))


def eigen(length):
    return 2.0 - 2.0 * np.cos(np.pi * (np.arange(length) + 1) / (length + 1))


def interp(fine_start, fine_count, coarse_start, coarse_count, ratio):
    fine_pos = np.arange(fine_count) + fine_start
    coarse_pos = np.arange(coarse_count) + coarse_start
    numerator = 2 * fine_pos - (ratio - 1)
    lower_index = numerator // (2 * ratio)
    weight = ((numerator - 2 * ratio * lower_index) / (2.0 * ratio))[:, None]
    below = (coarse_pos[None, :] == lower_index[:, None]).astype(np.float64)
    above = (coarse_pos[None, :] == lower_index[:, None] + 1).astype(np.float64)
    return below * (1.0 - weight) + above * weight


def legendre(length, count):
    points = (2.0 * np.arange(length) + 1.0) / length - 1.0
    columns = [np.ones_like(points), points]
    for degree in range(2, count):
        columns.append(
            ((2 * degree - 1) * points * columns[-1] - (degree - 1) * columns[-2]) / degree
        )
    result = []
    for column in columns[:count]:
        vector = column
        for _ in range(2):
            for earlier in result:
                vector = vector - np.sum(earlier * vector) * earlier
        result.append(vector / np.sqrt(np.sum(vector * vector)))
    return np.stack(result, axis=1)


def columns_at(table, positions):
    positions = np.asarray(positions)
    inside = (positions >= 0) & (positions < table.shape[1])
    return table[:, np.clip(positions, 0, table.shape[1] - 1)] * inside


def pair(table):
    table = np.asarray(table, np.float64)
    high = table.astype(np.float32).astype(ml_dtypes.bfloat16)
    low = (table - high.astype(np.float64)).astype(np.float32).astype(ml_dtypes.bfloat16)
    return np.stack([high, low], axis=-3)


@functools.lru_cache(None)
def tables():
    t = {}
    n = P_SIZE + 2 * W
    s64, m64 = sine(n), eigen(n)
    s32, m32 = sine(P_SIZE), eigen(P_SIZE)
    s8, m8 = sine(CELLS), eigen(CELLS)
    nx, ny = CELLS * N_GX, CELLS * N_GY
    sx, mx = sine(nx), eigen(nx)
    sy, my = sine(ny), eigen(ny)
    eye = np.eye
    basis = legendre(P_SIZE, NL)
    fine = interp(0, n, 0, n // Q, Q)
    mean = np.kron(eye(n // Q), np.full((1, Q), 1.0 / Q))
    inside = slice(W, W + P_SIZE)
    places = [W - 1, W + P_SIZE, W, W + P_SIZE - 1]
    r = mean @ s64
    bs = basis.T @ s64[inside]
    st = s64[places]
    bl = basis.T @ fine[inside]
    lt = fine[places]
    lanes_x, lanes_y = [0, 16, 64, 80], [32, 48, 96, 112]
    sc = s64[:, inside]
    t["sc"] = pair(sc)
    t["bd"] = pair(np.kron(eye(4), sc.T))
    mu = np.zeros((16 + n, 256))
    mu[:16] = (m64.reshape(16, 4, 1) + m64).reshape(16, 256)
    mu[16:] = m64[:, None]
    t["mu"] = (mu * ((n + 1) / 2.0) ** 3).astype(np.float32)
    ty = np.zeros((4, n, 256))
    for i in range(4):
        ty[i, :, i * 16 : i * 16 + 16] = r.T
        ty[i, :, 64 + i * 16 : 64 + i * 16 + 16] = bs.T
        ty[i, :, 128 + i * 4 : 128 + i * 4 + 4] = st.T
    t["ty"] = pair(ty.reshape(4 * n, 256))
    t["tz"] = pair(np.kron(eye(4), np.concatenate([r, bs], axis=0)))
    t["tx1"] = pair(np.kron(r.T, eye(16)))
    tx2 = np.zeros((n, NL, 128))
    tx3 = np.zeros((n, 4, 128))
    kl = np.zeros((16, 16, 128))
    for i in range(4):
        at_x, at_y = slice(lanes_x[i], lanes_x[i] + NL), slice(lanes_y[i], lanes_y[i] + NL)
        tx2[:, :, at_x] = st[i][:, None, None] * eye(NL)
        kl[:, :, at_x] = lt[i][:, None, None] * bl.T[None]
        tx3[:, i, at_y] = bs.T
        kl[:, :, at_y] = bl.T[:, None, :] * lt[i][None, :, None]
    t["tx2"] = pair(tx2.reshape(n * NL, 128))
    t["tx3"] = pair(tx3.reshape(n * 4, 128))
    t["kl"] = pair(kl.reshape(256, 128))
    first = W // Q
    u1 = np.zeros((CELLS, 16))
    u2 = np.zeros((CELLS, 16))
    for k in range(CELLS):
        u1[:, k + first] += s8[:, k]
        u2[:, k + first - 1] -= s8[:, k] / (Q * Q)
        u2[:, k + first + 1] -= s8[:, k] / (Q * Q)
    t["u"] = pair(np.concatenate([u1, u2, bl], axis=0))
    beside = eye(16, k=1) + eye(16, k=-1)
    k1 = 6.0 * eye(256) - np.kron(beside, eye(16)) - np.kron(eye(16), beside)
    t["k1"] = pair(k1 / (Q * Q))
    t["yb"] = pair(np.concatenate([columns_at(sy, np.arange(16) + b * CELLS - first) for b in range(N_GY)], axis=1))
    xa = [columns_at(sx, np.arange(16) + a * CELLS - first) for a in range(N_GX)]
    xa = [np.concatenate(xa[2 * i : 2 * i + 2], axis=1).T for i in range(N_GX // 2)]
    t["xa"] = pair(np.stack([np.repeat(v, CELLS, axis=0) for v in xa]))
    scale = Q * Q * (2.0 / (nx + 1)) * (2.0 / (ny + 1)) * (2.0 / (CELLS + 1))
    wc = scale / (m8.reshape(CELLS, 1, 1) + my.reshape(1, ny, 1) + mx.reshape(1, 1, nx))
    t["wc"] = wc.reshape(CELLS * ny, nx).astype(np.float32)
    edge = interp(-1, P_SIZE + 2, -1, CELLS + 2, Q)
    ends = edge[[0, P_SIZE + 1]]
    lateral = edge[1 : P_SIZE + 1]
    depth = interp(0, P_SIZE, 0, CELLS, Q)
    around = np.arange(CELLS + 2) - 1
    near = [columns_at(sy, around + b * CELLS).T for b in range(N_GY)]
    near = [np.concatenate([v, ends @ v, np.zeros((4, ny))], axis=0) for v in near]
    ey = np.zeros((N_GY, 16, CELLS, CELLS, ny))
    for k in range(CELLS):
        ey[:, :, k, k, :] = np.stack(near)
    t["ey"] = pair(ey.reshape(N_GY, 128, CELLS * ny))
    near = [columns_at(sx, around + a * CELLS).T for a in range(N_GX)]
    near = np.stack([np.concatenate([v, ends @ v], axis=0) for v in near]).reshape(N_GX // 2, 2, 12, nx)
    t["ex"] = pair(near.transpose(1, 2, 0, 3).reshape(2, 12 * (N_GX // 2), nx))
    t["s32"] = pair(s32)
    t["bd32"] = pair(np.kron(eye(4), s32))
    rm32 = m32.reshape(8, 1, 4, 1) + m32.reshape(1, 32, 1, 1) + m32.reshape(1, 1, 1, 32)
    t["rm32"] = ((2.0 / (P_SIZE + 1)) ** 3 / rm32).reshape(256, 128).astype(np.float32)
    t["sbz"] = pair(s32 @ basis)
    lz = s32 @ depth @ s8
    lane = np.arange(128)
    t["lz"] = lz[:, lane % 8].astype(np.float32)
    sel = np.zeros((4, 128, 128), np.float32)
    for f in range(4):
        for i in range((CELLS + 2) * CELLS):
            sel[f, i, 64 + f * 16 + i // 8] = 1.0
    t["sel"] = sel.reshape(512, 128).astype(ml_dtypes.bfloat16)
    tz2 = np.zeros((128, 32, 32))
    sb, sl = s32 @ basis, s32 @ lateral
    for f, layer in enumerate([0, P_SIZE - 1]):
        near = s32[:, layer]
        for i in range(NL):
            tz2[f * 16 + i] = near[:, None] * sb[None, :, i]
            tz2[32 + f * 16 + i] = near[None, :] * sb[:, None, i]
        for i in range(CELLS + 2):
            tz2[64 + f * 16 + i] = near[:, None] * sl[None, :, i]
            tz2[96 + f * 16 + i] = near[None, :] * sl[:, None, i]
    t["tz2"] = pair(tz2.reshape(128, 1024))
    return t


WIDE = {
    "bd": (0, 128, 0, 256),
    "ty": (128, 256, 0, 256),
    "tz": (384, 128, 0, 256),
    "tx1": (512, 1024, 0, 256),
    "k1": (1536, 256, 0, 256),
    "tx2a": (1792, 512, 0, 128),
    "tx2b": (1792, 512, 128, 128),
    "tx3": (2304, 256, 0, 128),
    "kl": (2304, 256, 128, 128),
}
SMALL = {"sc|": (0, 0, 64, 0, 96), "s32|": (0, 64, 32, 0, 96), "u|": (0, 96, 32, 0, 48), "sc=": (1, 0, 128, 0, 64), "s32=": (1, 0, 64, 64, 64)}


def in_row(table):
    return np.concatenate([table[0], table[1], table[0]], axis=1)


def in_block(table):
    return np.block([[table[0], table[0]], [table[1], np.zeros_like(table[1])]])


@functools.lru_cache(None)
def packs():
    t = tables()
    small = np.zeros((2, 256, 128), ml_dtypes.bfloat16)
    for name, (which, row, rows, lane, width) in SMALL.items():
        form = in_row if name[-1] == "|" else in_block
        small[which, row : row + rows, lane : lane + width] = form(t[name[:-1]])
    small[:, 128:256] = t["bd32"]
    parts = {**t, "tx2a": t["tx2"][:, :512], "tx2b": t["tx2"][:, 512:]}
    wide = np.zeros((2, 2560, 256), ml_dtypes.bfloat16)
    for name, (row, rows, lane, width) in WIDE.items():
        wide[:, row : row + rows, lane : lane + width] = parts[name]
    later = np.zeros((2, 128, 1408), ml_dtypes.bfloat16)
    later[:, :, :1024] = t["tz2"]
    later[:, :64, 1024:1152] = t["yb"]
    later[0, 64:96, 1024:1072] = in_row(t["sbz"])
    later[:, :, 1152:] = t["sel"].reshape(2, 2, 128, 128).transpose(0, 2, 1, 3).reshape(2, 128, 256)
    scales = np.zeros((768, 256), np.float32)
    scales[:512] = t["wc"]
    scales[512:, :128] = t["rm32"]
    scales[512:544, 128:] = t["lz"]
    return {
        "small": small,
        "wide": wide,
        "mu": t["mu"],
        "xa": t["xa"],
        "ey": t["ey"],
        "ex": t["ex"],
        "later": later,
        "scales": scales,
    }


class View:
    def __init__(self, ref, row, rows, lane, width):
        self.ref, self.rows, self.lanes = ref, slice(row, row + rows), slice(lane, lane + width)
        self.shape = (2, rows, width)

    def __getitem__(self, part):
        return self.ref[slice(None) if part is Ellipsis else part, self.rows, self.lanes]


def small_table(ref, name):
    which, row, rows, lane, width = SMALL[name]
    return ref[which, row : row + rows, lane : lane + width]


def split(x):
    high = x.astype(BF16)
    return high, (x - high.astype(F32)).astype(BF16)


def dot(x, y):
    return lax.dot_general(x, y, (((1,), (0,)), ((), ())), preferred_element_type=F32)


def dot_nt(x, y):
    return lax.dot_general(x, y, (((1,), (1,)), ((), ())), preferred_element_type=F32)


def times_table(x, table):
    high, low = split(x)
    rows = x.shape[0]
    if rows > 128:
        return dot(jnp.concatenate([high, low, high], axis=1), jnp.concatenate([table[0], table[0], table[1]], axis=0))
    if rows % 16:
        return dot(high, table[0]) + dot(low, table[0]) + dot(high, table[1])
    both = dot(jnp.concatenate([high, low], axis=0), table[0])
    return both[:rows] + both[rows:] + dot(high, table[1])


def table_times(table, x, product=dot):
    high, low = split(x)
    rows = table.shape[1]
    both = product(table[...].reshape(2 * rows, table.shape[2]), high)
    return both[:rows] + both[rows:] + product(table[0], low)


def row_times(table, x):
    high, low = split(x)
    return dot(table, jnp.concatenate([high, high, low], axis=0))


def block_times_nt(table, x):
    both = dot_nt(table, x)
    rows = table.shape[0] // 2
    return both[:rows] + both[rows:]


def spread(x, rows):
    high, low = split(x)
    high, low = high.astype(F32), low.astype(F32)
    count = x.shape[0]
    for y in range(P_SIZE):
        part = slice(y * 32, y * 32 + 32)
        rows[y * (count + 1) : y * (count + 1) + count, :] = jnp.concatenate([high[:, part], low[:, part]], axis=1)
    found = [rows[pl.ds(k, P_SIZE, stride=count + 1), :] for k in range(count)]
    return jnp.concatenate(found, axis=0).astype(BF16)


def stacked(x, width):
    return jnp.concatenate([x[:, i : i + width] for i in range(0, x.shape[1], width)], axis=0)


def unstacked(x, rows):
    return jnp.concatenate([x[i : i + rows] for i in range(0, x.shape[0], rows)], axis=1)


def lanes(rows):
    return lax.broadcasted_iota(jnp.int32, (rows, 128), 1)


FIRST = ("mu", "wide", "small")
NEXT = ("xa", "ey", "ex", "later", "scales")
KEPT = (((2, 256, 128), BF16), ((2, 256, 256), BF16), ((2, 128, 512), BF16), ((2, 192, 256), BF16), ((2, 128, 1408), BF16), ((768, 256), F32))


def first_kernel(q_hbm, mu_hbm, wide_hbm, small_hbm, xa_hbm, ey_hbm, ex_hbm, later_hbm, scales_hbm,
                 m_ref, own_ref, spec_ref, small, xa, ey, ex, later, scales,
                 q, mu, wide, rows, rows32, sem):
    started = []

    def start(source, target):
        copy = pltpu.make_async_copy(source, target, sem.at[len(started)])
        started.append(copy)
        copy.start()
        return copy

    def part(first, last):
        return start(wide_hbm.at[:, first:last, :], wide.at[:, first:last, :])

    now = [start(q_hbm, q), start(small_hbm, small)]
    soon = [part(0, 512), start(mu_hbm, mu)]
    for copy in now:
        copy.wait()
    late = [part(512, 1536), part(1536, 2560)]
    ahead = [
        start(scales_hbm, scales),
        start(later_hbm, later),
        start(xa_hbm.at[lax.axis_index("gs")], xa),
        start(ey_hbm.at[lax.axis_index("gy")], ey),
        start(ex_hbm.at[lax.axis_index("gc")], ex),
    ]
    t = {name: View(wide, *place) for name, place in WIDE.items()}
    x = row_times(small_table(small, "sc|"), q[...])
    x = block_times_nt(small_table(small, "sc="), spread(x, rows))
    for copy in soon:
        copy.wait()
    x = times_table(stacked(x, 128), t["bd"])
    bd32 = View(small, 128, 128, 0, 128)
    y = row_times(small_table(small, "s32|"), q[...])
    y = block_times_nt(small_table(small, "s32="), spread(y, rows32))
    spec_ref[...] = times_table(stacked(y, 128), bd32)
    x = jnp.concatenate([x[i * 64 : i * 64 + 64] / (mu[16:80, :] + mu[i : i + 1, :]) for i in range(16)], axis=0)
    x = times_table(x, t["ty"])
    lane = lanes(16)
    ls, lp, ly = [], [], []
    for i in range(4):
        z = table_times(t["tz"], x[i * 256 : i * 256 + 256])
        for j in range(0, 4, 2):
            one, two = z[j * 32 : j * 32 + 32, 0:128], z[j * 32 + 32 : j * 32 + 64, 0:128]
            ls.append(jnp.where(lane < 64, one[0:16], pltpu.roll(two[0:16], 64, 1)))
            lp.append(jnp.where(lane < 64, pltpu.roll(one[16:32], 64, 1), two[16:32]))
        for j in range(4):
            k = (i * 4 + j) % 8
            one = z[j * 32 + 16 : j * 32 + 32, 128:256]
            ly.append(pltpu.roll(one, 16 * k, 1) if k else one)
    ls, lp = jnp.concatenate(ls, axis=1), jnp.concatenate(lp, axis=1)
    ly = jnp.concatenate([sum(ly[1:8], ly[0]), sum(ly[9:16], ly[8])], axis=1)
    for copy in late:
        copy.wait()
    samples = times_table(ls, t["tx1"])
    coefs = times_table(lp[:, 0:512], t["tx2a"]) + times_table(lp[:, 512:1024], t["tx2b"]) + times_table(ly, t["tx3"])
    x = row_times(small_table(small, "u|"), samples)
    coefs = coefs - times_table(x[16:32], t["kl"])
    own_ref[...] = coefs
    x = (times_table(x[0:8], t["k1"]) + x[8:16]).T
    spilled = jnp.concatenate([x[i * 16 : i * 16 + 16] for i in range(16)], axis=1)
    tile = jnp.zeros((8, 128), F32)
    for i in range(8):
        value = coefs[i % 2 * 8 : i % 2 * 8 + 8]
        shift = (16 * i - 64 - i // 2 * 16) % 128
        tile = jnp.where(lanes(8) // 16 == i, pltpu.roll(value, shift, 1) if shift else value, tile)
    for i in range(16):
        m_ref[i * 24 : i * 24 + 16, :] = spilled
        m_ref[i * 24 + 16 : i * 24 + 24, :] = tile
    for copy in ahead:
        copy.wait()


def unpacked(tile, source, slot):
    parts = []
    for half in range(2):
        shift = (16 * slot - source - 16 * half) % 128
        parts.append(pltpu.roll(tile, shift, 1) if shift else tile)
    return jnp.where(lanes(NL) // 16 == slot, jnp.concatenate(parts, axis=0), 0.0)


def strip_kernel(got_ref, own_ref, xa, ey, ex, later, scales, m_ref, coefs_ref):
    s, c, b = lax.axis_index("gs"), lax.axis_index("gc"), lax.axis_index("gy")
    source = [
        jnp.concatenate([got_ref[(i * 8 + j) * 24 : (i * 8 + j) * 24 + 16, :] for j in range(N_GY)], axis=0)
        for i in range(2)
    ]
    x = table_times(View(later, 0, 64, 1024, 128), jnp.concatenate(source, axis=1))
    lane = lax.broadcasted_iota(jnp.int32, (64, 256), 1)
    x = jnp.concatenate([jnp.where(lane % 8 == k, x, 0.0) for k in range(CELLS)], axis=0)
    x = times_table(x, xa) * scales[0:512, :]
    x = table_times(ey, x)
    x = table_times(ex, x, dot_nt)

    def tile_of(i, j):
        return got_ref[pl.ds(pl.multiple_of((i * 8 + j) * 24 + 16, 8), 8), :]

    partner = tile_of(1 - c, b)
    outside = jnp.where(c == 0, pltpu.roll(partner, 64, 1), pltpu.roll(partner, 96, 1))
    outside = jnp.where(lanes(8) >= 96, outside, 0.0)
    fifth = outside[7:8]
    for j in range(3):
        fifth = fifth + pltpu.roll(outside, 32 * j + 32, 1)[4 + j : 5 + j]
    hit = lax.broadcasted_iota(jnp.int32, (16, 128), 0) == s + 1 - 2 * c
    lane = lanes(16)
    for f in range(2):
        value = jnp.where(lane < 80, x[160 + f * 16 : 176 + f * 16], 0.0)
        m_ref[pl.ds(f, 16, stride=5), :] = value + jnp.where(hit, outside[f : f + 1], 0.0)
        value = jnp.zeros((16, 128), F32)
        for k in range(CELLS + 2):
            part = pltpu.roll(x[k * 16 : k * 16 + 16], (8 * (k - 10 - f)) % 128, 1)
            value = jnp.where(lane // 8 == k, part, value)
        m_ref[pl.ds(2 + f, 16, stride=5), :] = value + jnp.where(hit, outside[2 + f : 3 + f], 0.0)
    m_ref[pl.ds(4, 16, stride=5), :] = jnp.where(hit, fifth, 0.0)
    coefs = jnp.where(lane < 64, own_ref[...], 0.0)
    coefs = coefs + jnp.where(c == 0, unpacked(partner, 0, 1), unpacked(partner, 32, 0))
    above = unpacked(tile_of(c, jnp.minimum(b + 1, N_GY - 1)), 64, 3)
    below = unpacked(tile_of(c, jnp.maximum(b - 1, 0)), 96, 2)
    coefs = coefs + jnp.where(b < N_GY - 1, above, 0.0) + jnp.where(b > 0, below, 0.0)
    coefs_ref[...] = coefs


def last_kernel(m_ref, coefs_ref, spec_ref, small, later, scales, out_ref, rows):
    s32, bd32 = small_table(small, "s32|"), View(small, 128, 128, 0, 128)
    got = [jnp.sum(m_ref[pl.ds(i, 16, stride=5), :], axis=0, keepdims=True) for i in range(5)]
    tile = got[:4] + [pltpu.roll(got[4], 96 - 32 * j, 1) if j < 3 else got[4] for j in range(4)]
    tile = jnp.concatenate(tile, axis=0)
    coefs = coefs_ref[...] + jnp.where(lax.axis_index("gc") == 0, unpacked(tile, 96, 0), unpacked(tile, 96, 1))
    lz = scales[512:544, 128:256]
    high, low = split(jnp.concatenate([lz * got[i] for i in range(4)], axis=1))
    x = row_times(later[0, 64:96, 1024:1072], coefs)
    for i in range(4):
        part = jnp.concatenate([high[:, i * 128 : i * 128 + 128], low[:, i * 128 : i * 128 + 128]], axis=0)
        part = dot(part, later[i // 2, :, 1152 + i % 2 * 128 : 1280 + i % 2 * 128])
        x = x + part[:32] + part[32:]
    x = times_table(x, View(later, 0, 128, 0, 1024))
    x = (stacked(x, 128) + spec_ref[...]) * scales[512:768, 0:128]
    x = row_times(s32, unstacked(x, 32))
    x = times_table(stacked(x, 128), bd32)
    for i in range(8):
        turned = x[i * 32 : i * 32 + 32].T
        for j in range(4):
            rows[(i * 4 + j) * 33 : (i * 4 + j) * 33 + 32, :] = turned[j * 32 : j * 32 + 32]
    x = jnp.concatenate([rows[pl.ds(y, 32, stride=P_SIZE + 1), :] for y in range(P_SIZE)], axis=1)
    out_ref[...] = row_times(s32, x)


def vmem(count):
    return [pl.BlockSpec(memory_space=pltpu.VMEM)] * count


def hbm(count):
    return [pl.BlockSpec(memory_space=pltpu.HBM)] * count


def shape(*dims):
    return jax.ShapeDtypeStruct(dims, F32)


def params(mib):
    return pltpu.CompilerParams(vmem_limit_bytes=mib * 1024 * 1024)


def body(charge):
    t = {k: pltpu.with_memory_space_constraint(jnp.asarray(v), pltpu.HBM) for k, v in packs().items()}
    message, own, spec, small, xa, ey, ex, later, scales = pl.pallas_call(
        first_kernel,
        out_shape=[shape(384, 128), shape(NL, 128), shape(256, 128)] + [jax.ShapeDtypeStruct(*k) for k in KEPT],
        in_specs=hbm(1 + len(FIRST) + len(NEXT)),
        out_specs=vmem(3 + len(KEPT)),
        scratch_shapes=[
            pltpu.VMEM((32, 1024), F32),
            pltpu.VMEM((80, 256), F32),
            pltpu.VMEM((2, 2560, 256), BF16),
            pltpu.VMEM((2080, 64), F32),
            pltpu.VMEM((1056, 64), F32),
            pltpu.SemaphoreType.DMA((11,)),
        ],
        compiler_params=params(24),
        name="first",
    )(pltpu.with_memory_space_constraint(charge, pltpu.HBM), *[t[k] for k in FIRST + NEXT])
    strip = lax.all_to_all(message.reshape(16, 24, 128), ("gc", "gy"), 0, 0).reshape(384, 128)
    message, coefs = pl.pallas_call(
        strip_kernel,
        out_shape=(shape(80, 128), shape(NL, 128)),
        in_specs=vmem(7),
        out_specs=tuple(vmem(2)),
        compiler_params=params(12),
        name="strip",
    )(strip, own, xa, ey, ex, later, scales)
    arrived = lax.all_to_all(message.reshape(16, 1, 640), "gs", 0, 0).reshape(80, 128)
    return pl.pallas_call(
        last_kernel,
        out_shape=shape(32, 1024),
        in_specs=vmem(6),
        out_specs=vmem(1)[0],
        scratch_shapes=[pltpu.VMEM((1056, 32), F32)],
        compiler_params=params(12),
        name="last",
    )(arrived, coefs, spec, small, later, scales)


def solution(mesh):
    strips = jax.sharding.Mesh(mesh.devices.reshape(N_GX // 2, 2, N_GY), ("gs", "gc", "gy"))
    spec = P(("gs", "gc"), "gy")
    return jax.shard_map(body, mesh=strips, in_specs=(spec,), out_specs=spec, check_vma=False)
```

```python
import functools

import jax
import jax.numpy as jnp
import ml_dtypes
import numpy as np
from jax import lax
from jax.experimental import pallas as pl
from jax.experimental.pallas import tpu as pltpu
from jax.sharding import PartitionSpec as P

P_SIZE = 32
W = 16
Q = 4
NL = 16
N_GX = 32
N_GY = 8
CELLS = P_SIZE // Q
BF16 = jnp.bfloat16
F32 = jnp.float32


def sine(length):
    counter = np.arange(length) + 1
    multiple = counter[:, None] * counter[None, :] % (2 * (length + 1))
    return np.sin(np.pi * multiple / (length + 1))


def eigen(length):
    return 2.0 - 2.0 * np.cos(np.pi * (np.arange(length) + 1) / (length + 1))


def interp(fine_start, fine_count, coarse_start, coarse_count, ratio):
    fine_pos = np.arange(fine_count) + fine_start
    coarse_pos = np.arange(coarse_count) + coarse_start
    numerator = 2 * fine_pos - (ratio - 1)
    lower_index = numerator // (2 * ratio)
    weight = ((numerator - 2 * ratio * lower_index) / (2.0 * ratio))[:, None]
    below = (coarse_pos[None, :] == lower_index[:, None]).astype(np.float64)
    above = (coarse_pos[None, :] == lower_index[:, None] + 1).astype(np.float64)
    return below * (1.0 - weight) + above * weight


def legendre(length, count):
    points = (2.0 * np.arange(length) + 1.0) / length - 1.0
    columns = [np.ones_like(points), points]
    for degree in range(2, count):
        columns.append(
            ((2 * degree - 1) * points * columns[-1] - (degree - 1) * columns[-2]) / degree
        )
    result = []
    for column in columns[:count]:
        vector = column
        for _ in range(2):
            for earlier in result:
                vector = vector - np.sum(earlier * vector) * earlier
        result.append(vector / np.sqrt(np.sum(vector * vector)))
    return np.stack(result, axis=1)


def columns_at(table, positions):
    positions = np.asarray(positions)
    inside = (positions >= 0) & (positions < table.shape[1])
    return table[:, np.clip(positions, 0, table.shape[1] - 1)] * inside


def pair(table):
    table = np.asarray(table, np.float64)
    high = table.astype(np.float32).astype(ml_dtypes.bfloat16)
    low = (table - high.astype(np.float64)).astype(np.float32).astype(ml_dtypes.bfloat16)
    return np.stack([high, low], axis=-3)


@functools.lru_cache(None)
def tables():
    t = {}
    n = P_SIZE + 2 * W
    s64, m64 = sine(n), eigen(n)
    s32, m32 = sine(P_SIZE), eigen(P_SIZE)
    s8, m8 = sine(CELLS), eigen(CELLS)
    nx, ny = CELLS * N_GX, CELLS * N_GY
    sx, mx = sine(nx), eigen(nx)
    sy, my = sine(ny), eigen(ny)
    eye = np.eye
    basis = legendre(P_SIZE, NL)
    fine = interp(0, n, 0, n // Q, Q)
    mean = np.kron(eye(n // Q), np.full((1, Q), 1.0 / Q))
    inside = slice(W, W + P_SIZE)
    places = [W - 1, W + P_SIZE, W, W + P_SIZE - 1]
    r = mean @ s64
    bs = basis.T @ s64[inside]
    st = s64[places]
    bl = basis.T @ fine[inside]
    lt = fine[places]
    lanes_x, lanes_y = [0, 16, 64, 80], [32, 48, 96, 112]
    sc = s64[:, inside]
    t["sc"] = pair(sc)
    t["bd"] = pair(np.kron(eye(4), sc.T))
    mu = np.zeros((16 + n, 256))
    mu[:16] = (m64.reshape(16, 4, 1) + m64).reshape(16, 256)
    mu[16:] = m64[:, None]
    t["mu"] = (mu * ((n + 1) / 2.0) ** 3).astype(np.float32)
    ty = np.zeros((4, n, 256))
    for i in range(4):
        ty[i, :, i * 16 : i * 16 + 16] = r.T
        ty[i, :, 64 + i * 16 : 64 + i * 16 + 16] = bs.T
        ty[i, :, 128 + i * 4 : 128 + i * 4 + 4] = st.T
    t["ty"] = pair(ty.reshape(4 * n, 256))
    t["tz"] = pair(np.kron(eye(4), np.concatenate([r, bs], axis=0)))
    t["tx1"] = pair(np.kron(r.T, eye(16)))
    tx2 = np.zeros((n, NL, 128))
    tx3 = np.zeros((n, 4, 128))
    kl = np.zeros((16, 16, 128))
    for i in range(4):
        at_x, at_y = slice(lanes_x[i], lanes_x[i] + NL), slice(lanes_y[i], lanes_y[i] + NL)
        tx2[:, :, at_x] = st[i][:, None, None] * eye(NL)
        kl[:, :, at_x] = lt[i][:, None, None] * bl.T[None]
        tx3[:, i, at_y] = bs.T
        kl[:, :, at_y] = bl.T[:, None, :] * lt[i][None, :, None]
    t["tx2"] = pair(tx2.reshape(n * NL, 128))
    t["tx3"] = pair(tx3.reshape(n * 4, 128))
    t["kl"] = pair(kl.reshape(256, 128))
    first = W // Q
    u1 = np.zeros((CELLS, 16))
    u2 = np.zeros((CELLS, 16))
    for k in range(CELLS):
        u1[:, k + first] += s8[:, k]
        u2[:, k + first - 1] -= s8[:, k] / (Q * Q)
        u2[:, k + first + 1] -= s8[:, k] / (Q * Q)
    t["u"] = pair(np.concatenate([u1, u2, bl], axis=0))
    beside = eye(16, k=1) + eye(16, k=-1)
    k1 = 6.0 * eye(256) - np.kron(beside, eye(16)) - np.kron(eye(16), beside)
    t["k1"] = pair(k1 / (Q * Q))
    t["yb"] = pair(np.concatenate([columns_at(sy, np.arange(16) + b * CELLS - first) for b in range(N_GY)], axis=1))
    xa = [columns_at(sx, np.arange(16) + a * CELLS - first) for a in range(N_GX)]
    xa = [np.concatenate(xa[2 * i : 2 * i + 2], axis=1).T for i in range(N_GX // 2)]
    t["xa"] = pair(np.stack([np.repeat(v, CELLS, axis=0) for v in xa]))
    scale = Q * Q * (2.0 / (nx + 1)) * (2.0 / (ny + 1)) * (2.0 / (CELLS + 1))
    wc = scale / (m8.reshape(CELLS, 1, 1) + my.reshape(1, ny, 1) + mx.reshape(1, 1, nx))
    t["wc"] = wc.reshape(CELLS * ny, nx).astype(np.float32)
    edge = interp(-1, P_SIZE + 2, -1, CELLS + 2, Q)
    ends = edge[[0, P_SIZE + 1]]
    lateral = edge[1 : P_SIZE + 1]
    depth = interp(0, P_SIZE, 0, CELLS, Q)
    around = np.arange(CELLS + 2) - 1
    near = [columns_at(sy, around + b * CELLS).T for b in range(N_GY)]
    near = [np.concatenate([v, ends @ v, np.zeros((4, ny))], axis=0) for v in near]
    ey = np.zeros((N_GY, 16, CELLS, CELLS, ny))
    for k in range(CELLS):
        ey[:, :, k, k, :] = np.stack(near)
    t["ey"] = pair(ey.reshape(N_GY, 128, CELLS * ny))
    near = [columns_at(sx, around + a * CELLS).T for a in range(N_GX)]
    near = np.stack([np.concatenate([v, ends @ v], axis=0) for v in near]).reshape(N_GX // 2, 2, 12, nx)
    t["ex"] = pair(near.transpose(1, 2, 0, 3).reshape(2, 12 * (N_GX // 2), nx))
    t["s32"] = pair(s32)
    t["bd32"] = pair(np.kron(eye(4), s32))
    rm32 = m32.reshape(8, 1, 4, 1) + m32.reshape(1, 32, 1, 1) + m32.reshape(1, 1, 1, 32)
    t["rm32"] = ((2.0 / (P_SIZE + 1)) ** 3 / rm32).reshape(256, 128).astype(np.float32)
    t["sbz"] = pair(s32 @ basis)
    lz = s32 @ depth @ s8
    lane = np.arange(128)
    t["lz"] = lz[:, lane % 8].astype(np.float32)
    sel = np.zeros((4, 128, 128), np.float32)
    for f in range(4):
        for i in range((CELLS + 2) * CELLS):
            sel[f, i, 64 + f * 16 + i // 8] = 1.0
    t["sel"] = sel.reshape(512, 128).astype(ml_dtypes.bfloat16)
    tz2 = np.zeros((128, 32, 32))
    sb, sl = s32 @ basis, s32 @ lateral
    for f, layer in enumerate([0, P_SIZE - 1]):
        near = s32[:, layer]
        for i in range(NL):
            tz2[f * 16 + i] = near[:, None] * sb[None, :, i]
            tz2[32 + f * 16 + i] = near[None, :] * sb[:, None, i]
        for i in range(CELLS + 2):
            tz2[64 + f * 16 + i] = near[:, None] * sl[None, :, i]
            tz2[96 + f * 16 + i] = near[None, :] * sl[:, None, i]
    t["tz2"] = pair(tz2.reshape(128, 1024))
    return t


WIDE = {
    "bd": (0, 128, 0, 256),
    "ty": (128, 256, 0, 256),
    "tz": (384, 128, 0, 256),
    "tx1": (512, 1024, 0, 256),
    "k1": (1536, 256, 0, 256),
    "tx2a": (1792, 512, 0, 128),
    "tx2b": (1792, 512, 128, 128),
    "tx3": (2304, 256, 0, 128),
    "kl": (2304, 256, 128, 128),
}
SMALL = {"sc|": (0, 0, 64, 0, 96), "s32|": (0, 64, 32, 0, 96), "u|": (0, 96, 32, 0, 48), "sc=": (1, 0, 64, 0, 96), "s32=": (1, 64, 32, 0, 96)}


def in_row(table):
    return np.concatenate([table[0], table[1], table[0]], axis=1)


def in_block(table):
    return np.concatenate([table[0], table[0], table[1]], axis=1)


@functools.lru_cache(None)
def packs():
    t = tables()
    small = np.zeros((2, 256, 128), ml_dtypes.bfloat16)
    for name, (which, row, rows, lane, width) in SMALL.items():
        form = in_row if name[-1] == "|" else in_block
        small[which, row : row + rows, lane : lane + width] = form(t[name[:-1]])
    small[:, 128:256] = t["bd32"]
    parts = {**t, "tx2a": t["tx2"][:, :512], "tx2b": t["tx2"][:, 512:]}
    wide = np.zeros((2, 2560, 256), ml_dtypes.bfloat16)
    for name, (row, rows, lane, width) in WIDE.items():
        wide[:, row : row + rows, lane : lane + width] = parts[name]
    later = np.zeros((2, 128, 1408), ml_dtypes.bfloat16)
    later[:, :, :1024] = t["tz2"]
    later[:, :64, 1024:1152] = t["yb"]
    later[0, 64:96, 1024:1072] = in_row(t["sbz"])
    later[:, :, 1152:] = t["sel"].reshape(2, 2, 128, 128).transpose(0, 2, 1, 3).reshape(2, 128, 256)
    scales = np.zeros((768, 256), np.float32)
    scales[:512] = t["wc"]
    scales[512:, :128] = t["rm32"]
    scales[512:544, 128:] = t["lz"]
    return {
        "small": small,
        "wide": wide,
        "mu": t["mu"],
        "xa": t["xa"],
        "ey": t["ey"],
        "ex": t["ex"],
        "later": later,
        "scales": scales,
    }


class View:
    def __init__(self, ref, row, rows, lane, width):
        self.ref, self.rows, self.lanes = ref, slice(row, row + rows), slice(lane, lane + width)
        self.shape = (2, rows, width)

    def __getitem__(self, part):
        return self.ref[slice(None) if part is Ellipsis else part, self.rows, self.lanes]


def small_table(ref, name):
    which, row, rows, lane, width = SMALL[name]
    return ref[which, row : row + rows, lane : lane + width]


def split(x):
    high = x.astype(BF16)
    return high, (x - high.astype(F32)).astype(BF16)


def dot(x, y):
    return lax.dot_general(x, y, (((1,), (0,)), ((), ())), preferred_element_type=F32)


def dot_nt(x, y):
    return lax.dot_general(x, y, (((1,), (1,)), ((), ())), preferred_element_type=F32)


def times_table(x, table):
    high, low = split(x)
    rows = x.shape[0]
    if rows > 128:
        return dot(jnp.concatenate([high, low, high], axis=1), jnp.concatenate([table[0], table[0], table[1]], axis=0))
    if rows % 16:
        return dot(high, table[0]) + dot(low, table[0]) + dot(high, table[1])
    both = dot(jnp.concatenate([high, low], axis=0), table[0])
    return both[:rows] + both[rows:] + dot(high, table[1])


def table_times(table, x, product=dot):
    high, low = split(x)
    rows = table.shape[1]
    both = product(table[...].reshape(2 * rows, table.shape[2]), high)
    return both[:rows] + both[rows:] + product(table[0], low)


def row_times(table, x):
    high, low = split(x)
    return dot(table, jnp.concatenate([high, high, low], axis=0))


def block_times_nt(table, x):
    return dot_nt(table, x)


def spread(x, rows):
    high, low = split(x)
    high, low = high.astype(F32), low.astype(F32)
    count = x.shape[0]
    for y in range(P_SIZE):
        part = slice(y * 32, y * 32 + 32)
        rows[y * (count + 1) : y * (count + 1) + count, :] = jnp.concatenate([high[:, part], low[:, part], high[:, part]], axis=1)
    found = [rows[pl.ds(k, P_SIZE, stride=count + 1), :] for k in range(count)]
    return jnp.concatenate(found, axis=0).astype(BF16)


def stacked(x, width):
    return jnp.concatenate([x[:, i : i + width] for i in range(0, x.shape[1], width)], axis=0)


def unstacked(x, rows):
    return jnp.concatenate([x[i : i + rows] for i in range(0, x.shape[0], rows)], axis=1)


def lanes(rows):
    return lax.broadcasted_iota(jnp.int32, (rows, 128), 1)


FIRST = ("mu", "wide", "small")
NEXT = ("xa", "ey", "ex", "later", "scales")
KEPT = (((2, 256, 128), BF16), ((2, 256, 256), BF16), ((2, 128, 512), BF16), ((2, 192, 256), BF16), ((2, 128, 1408), BF16), ((768, 256), F32))


def first_kernel(q_hbm, mu_hbm, wide_hbm, small_hbm, xa_hbm, ey_hbm, ex_hbm, later_hbm, scales_hbm,
                 m_ref, own_ref, spec_ref, small, xa, ey, ex, later, scales,
                 q, mu, wide, rows, rows32, sem):
    started = []

    def start(source, target):
        copy = pltpu.make_async_copy(source, target, sem.at[len(started)])
        started.append(copy)
        copy.start()
        return copy

    def part(first, last):
        return start(wide_hbm.at[:, first:last, :], wide.at[:, first:last, :])

    now = [start(q_hbm, q), start(small_hbm, small)]
    soon = [part(0, 512), start(mu_hbm, mu)]
    for copy in now:
        copy.wait()
    late = [part(512, 1536), part(1536, 2560)]
    ahead = [
        start(scales_hbm, scales),
        start(later_hbm, later),
        start(xa_hbm.at[lax.axis_index("gs")], xa),
        start(ey_hbm.at[lax.axis_index("gy")], ey),
        start(ex_hbm.at[lax.axis_index("gc")], ex),
    ]
    t = {name: View(wide, *place) for name, place in WIDE.items()}
    x = row_times(small_table(small, "sc|"), q[...])
    x = block_times_nt(small_table(small, "sc="), spread(x, rows))
    for copy in soon:
        copy.wait()
    x = times_table(stacked(x, 128), t["bd"])
    bd32 = View(small, 128, 128, 0, 128)
    y = row_times(small_table(small, "s32|"), q[...])
    y = block_times_nt(small_table(small, "s32="), spread(y, rows32))
    spec_ref[...] = times_table(stacked(y, 128), bd32)
    x = jnp.concatenate([x[i * 64 : i * 64 + 64] / (mu[16:80, :] + mu[i : i + 1, :]) for i in range(16)], axis=0)
    x = times_table(x, t["ty"])
    lane = lanes(16)
    ls, lp, ly = [], [], []
    for i in range(4):
        z = table_times(t["tz"], x[i * 256 : i * 256 + 256])
        for j in range(0, 4, 2):
            one, two = z[j * 32 : j * 32 + 32, 0:128], z[j * 32 + 32 : j * 32 + 64, 0:128]
            ls.append(jnp.where(lane < 64, one[0:16], pltpu.roll(two[0:16], 64, 1)))
            lp.append(jnp.where(lane < 64, pltpu.roll(one[16:32], 64, 1), two[16:32]))
        for j in range(4):
            k = (i * 4 + j) % 8
            one = z[j * 32 + 16 : j * 32 + 32, 128:256]
            ly.append(pltpu.roll(one, 16 * k, 1) if k else one)
    ls, lp = jnp.concatenate(ls, axis=1), jnp.concatenate(lp, axis=1)
    ly = jnp.concatenate([sum(ly[1:8], ly[0]), sum(ly[9:16], ly[8])], axis=1)
    for copy in late:
        copy.wait()
    samples = times_table(ls, t["tx1"])
    coefs = times_table(lp[:, 0:512], t["tx2a"]) + times_table(lp[:, 512:1024], t["tx2b"]) + times_table(ly, t["tx3"])
    x = row_times(small_table(small, "u|"), samples)
    coefs = coefs - times_table(x[16:32], t["kl"])
    own_ref[...] = coefs
    x = (times_table(x[0:8], t["k1"]) + x[8:16]).T
    spilled = jnp.concatenate([x[i * 16 : i * 16 + 16] for i in range(16)], axis=1)
    tile = jnp.zeros((8, 128), F32)
    for i in range(8):
        value = coefs[i % 2 * 8 : i % 2 * 8 + 8]
        shift = (16 * i - 64 - i // 2 * 16) % 128
        tile = jnp.where(lanes(8) // 16 == i, pltpu.roll(value, shift, 1) if shift else value, tile)
    for i in range(16):
        m_ref[i * 24 : i * 24 + 16, :] = spilled
        m_ref[i * 24 + 16 : i * 24 + 24, :] = tile
    for copy in ahead:
        copy.wait()


def unpacked(tile, source, slot):
    parts = []
    for half in range(2):
        shift = (16 * slot - source - 16 * half) % 128
        parts.append(pltpu.roll(tile, shift, 1) if shift else tile)
    return jnp.where(lanes(NL) // 16 == slot, jnp.concatenate(parts, axis=0), 0.0)


def strip_kernel(got_ref, own_ref, xa, ey, ex, later, scales, m_ref, coefs_ref):
    s, c, b = lax.axis_index("gs"), lax.axis_index("gc"), lax.axis_index("gy")
    source = [
        jnp.concatenate([got_ref[(i * 8 + j) * 24 : (i * 8 + j) * 24 + 16, :] for j in range(N_GY)], axis=0)
        for i in range(2)
    ]
    x = table_times(View(later, 0, 64, 1024, 128), jnp.concatenate(source, axis=1))
    lane = lax.broadcasted_iota(jnp.int32, (64, 256), 1)
    x = jnp.concatenate([jnp.where(lane % 8 == k, x, 0.0) for k in range(CELLS)], axis=0)
    x = times_table(x, xa) * scales[0:512, :]
    x = table_times(ey, x)
    x = table_times(ex, x, dot_nt)

    def tile_of(i, j):
        return got_ref[pl.ds(pl.multiple_of((i * 8 + j) * 24 + 16, 8), 8), :]

    partner = tile_of(1 - c, b)
    outside = jnp.where(c == 0, pltpu.roll(partner, 64, 1), pltpu.roll(partner, 96, 1))
    outside = jnp.where(lanes(8) >= 96, outside, 0.0)
    fifth = outside[7:8]
    for j in range(3):
        fifth = fifth + pltpu.roll(outside, 32 * j + 32, 1)[4 + j : 5 + j]
    hit = lax.broadcasted_iota(jnp.int32, (16, 128), 0) == s + 1 - 2 * c
    lane = lanes(16)
    for f in range(2):
        value = jnp.where(lane < 80, x[160 + f * 16 : 176 + f * 16], 0.0)
        m_ref[pl.ds(f, 16, stride=5), :] = value + jnp.where(hit, outside[f : f + 1], 0.0)
        value = jnp.zeros((16, 128), F32)
        for k in range(CELLS + 2):
            part = pltpu.roll(x[k * 16 : k * 16 + 16], (8 * (k - 10 - f)) % 128, 1)
            value = jnp.where(lane // 8 == k, part, value)
        m_ref[pl.ds(2 + f, 16, stride=5), :] = value + jnp.where(hit, outside[2 + f : 3 + f], 0.0)
    m_ref[pl.ds(4, 16, stride=5), :] = jnp.where(hit, fifth, 0.0)
    coefs = jnp.where(lane < 64, own_ref[...], 0.0)
    coefs = coefs + jnp.where(c == 0, unpacked(partner, 0, 1), unpacked(partner, 32, 0))
    above = unpacked(tile_of(c, jnp.minimum(b + 1, N_GY - 1)), 64, 3)
    below = unpacked(tile_of(c, jnp.maximum(b - 1, 0)), 96, 2)
    coefs = coefs + jnp.where(b < N_GY - 1, above, 0.0) + jnp.where(b > 0, below, 0.0)
    coefs_ref[...] = coefs


def last_kernel(m_ref, coefs_ref, spec_ref, small, later, scales, out_ref, rows, done, sem):
    s32, bd32 = small_table(small, "s32|"), View(small, 128, 128, 0, 128)
    got = [jnp.sum(m_ref[pl.ds(i, 16, stride=5), :], axis=0, keepdims=True) for i in range(5)]
    tile = got[:4] + [pltpu.roll(got[4], 96 - 32 * j, 1) if j < 3 else got[4] for j in range(4)]
    tile = jnp.concatenate(tile, axis=0)
    coefs = coefs_ref[...] + jnp.where(lax.axis_index("gc") == 0, unpacked(tile, 96, 0), unpacked(tile, 96, 1))
    lz = scales[512:544, 128:256]
    high, low = split(jnp.concatenate([lz * got[i] for i in range(4)], axis=1))
    x = row_times(later[0, 64:96, 1024:1072], coefs)
    for i in range(4):
        part = jnp.concatenate([high[:, i * 128 : i * 128 + 128], low[:, i * 128 : i * 128 + 128]], axis=0)
        part = dot(part, later[i // 2, :, 1152 + i % 2 * 128 : 1280 + i % 2 * 128])
        x = x + part[:32] + part[32:]
    x = times_table(x, View(later, 0, 128, 0, 1024))
    x = (stacked(x, 128) + spec_ref[...]) * scales[512:768, 0:128]
    x = row_times(s32, unstacked(x, 32))
    x = times_table(stacked(x, 128), bd32)
    for i in range(8):
        turned = x[i * 32 : i * 32 + 32].T
        for j in range(4):
            rows[(i * 4 + j) * 33 : (i * 4 + j) * 33 + 32, :] = turned[j * 32 : j * 32 + 32]
    x = jnp.concatenate([rows[pl.ds(y, 32, stride=P_SIZE + 1), :] for y in range(P_SIZE)], axis=1)
    copies = []
    for i in range(4):
        done[:, i * 256 : i * 256 + 256] = row_times(s32, x[:, i * 256 : i * 256 + 256])
        copies.append(pltpu.make_async_copy(done.at[:, i * 256 : i * 256 + 256], out_ref.at[:, i * 256 : i * 256 + 256], sem.at[i]))
        copies[-1].start()
    for copy in copies:
        copy.wait()


def vmem(count):
    return [pl.BlockSpec(memory_space=pltpu.VMEM)] * count


def hbm(count):
    return [pl.BlockSpec(memory_space=pltpu.HBM)] * count


def shape(*dims):
    return jax.ShapeDtypeStruct(dims, F32)


def params(mib):
    return pltpu.CompilerParams(vmem_limit_bytes=mib * 1024 * 1024)


def body(charge):
    t = {k: pltpu.with_memory_space_constraint(jnp.asarray(v), pltpu.HBM) for k, v in packs().items()}
    message, own, spec, small, xa, ey, ex, later, scales = pl.pallas_call(
        first_kernel,
        out_shape=[shape(384, 128), shape(NL, 128), shape(256, 128)] + [jax.ShapeDtypeStruct(*k) for k in KEPT],
        in_specs=hbm(1 + len(FIRST) + len(NEXT)),
        out_specs=vmem(3 + len(KEPT)),
        scratch_shapes=[
            pltpu.VMEM((32, 1024), F32),
            pltpu.VMEM((80, 256), F32),
            pltpu.VMEM((2, 2560, 256), BF16),
            pltpu.VMEM((2080, 96), F32),
            pltpu.VMEM((1056, 96), F32),
            pltpu.SemaphoreType.DMA((11,)),
        ],
        compiler_params=params(24),
        name="first",
    )(pltpu.with_memory_space_constraint(charge, pltpu.HBM), *[t[k] for k in FIRST + NEXT])
    strip = lax.all_to_all(message.reshape(16, 24, 128), ("gc", "gy"), 0, 0).reshape(384, 128)
    message, coefs = pl.pallas_call(
        strip_kernel,
        out_shape=(shape(80, 128), shape(NL, 128)),
        in_specs=vmem(7),
        out_specs=tuple(vmem(2)),
        compiler_params=params(12),
        name="strip",
    )(strip, own, xa, ey, ex, later, scales)
    arrived = lax.all_to_all(message.reshape(16, 1, 640), "gs", 0, 0).reshape(80, 128)
    return pl.pallas_call(
        last_kernel,
        out_shape=shape(32, 1024),
        in_specs=vmem(6),
        out_specs=hbm(1)[0],
        scratch_shapes=[pltpu.VMEM((1056, 32), F32), pltpu.VMEM((32, 1024), F32), pltpu.SemaphoreType.DMA((4,))],
        compiler_params=params(12),
        name="last",
    )(arrived, coefs, spec, small, later, scales)


def solution(mesh):
    strips = jax.sharding.Mesh(mesh.devices.reshape(N_GX // 2, 2, N_GY), ("gs", "gc", "gy"))
    spec = P(("gs", "gc"), "gy")
    return jax.shard_map(body, mesh=strips, in_specs=(spec,), out_specs=spec, check_vma=False)
```

```python
import functools

import jax
import jax.numpy as jnp
import ml_dtypes
import numpy as np
from jax import lax
from jax.experimental import pallas as pl
from jax.experimental.pallas import tpu as pltpu
from jax.sharding import PartitionSpec as P

P_SIZE = 32
W = 16
Q = 4
NL = 16
N_GX = 32
N_GY = 8
CELLS = P_SIZE // Q
BF16 = jnp.bfloat16
F32 = jnp.float32


def sine(length):
    counter = np.arange(length) + 1
    multiple = counter[:, None] * counter[None, :] % (2 * (length + 1))
    return np.sin(np.pi * multiple / (length + 1))


def eigen(length):
    return 2.0 - 2.0 * np.cos(np.pi * (np.arange(length) + 1) / (length + 1))


def interp(fine_start, fine_count, coarse_start, coarse_count, ratio):
    fine_pos = np.arange(fine_count) + fine_start
    coarse_pos = np.arange(coarse_count) + coarse_start
    numerator = 2 * fine_pos - (ratio - 1)
    lower_index = numerator // (2 * ratio)
    weight = ((numerator - 2 * ratio * lower_index) / (2.0 * ratio))[:, None]
    below = (coarse_pos[None, :] == lower_index[:, None]).astype(np.float64)
    above = (coarse_pos[None, :] == lower_index[:, None] + 1).astype(np.float64)
    return below * (1.0 - weight) + above * weight


def legendre(length, count):
    points = (2.0 * np.arange(length) + 1.0) / length - 1.0
    columns = [np.ones_like(points), points]
    for degree in range(2, count):
        columns.append(
            ((2 * degree - 1) * points * columns[-1] - (degree - 1) * columns[-2]) / degree
        )
    result = []
    for column in columns[:count]:
        vector = column
        for _ in range(2):
            for earlier in result:
                vector = vector - np.sum(earlier * vector) * earlier
        result.append(vector / np.sqrt(np.sum(vector * vector)))
    return np.stack(result, axis=1)


def columns_at(table, positions):
    positions = np.asarray(positions)
    inside = (positions >= 0) & (positions < table.shape[1])
    return table[:, np.clip(positions, 0, table.shape[1] - 1)] * inside


def pair(table):
    table = np.asarray(table, np.float64)
    high = table.astype(np.float32).astype(ml_dtypes.bfloat16)
    low = (table - high.astype(np.float64)).astype(np.float32).astype(ml_dtypes.bfloat16)
    return np.stack([high, low], axis=-3)


@functools.lru_cache(None)
def tables():
    t = {}
    n = P_SIZE + 2 * W
    s64, m64 = sine(n), eigen(n)
    s32, m32 = sine(P_SIZE), eigen(P_SIZE)
    s8, m8 = sine(CELLS), eigen(CELLS)
    nx, ny = CELLS * N_GX, CELLS * N_GY
    sx, mx = sine(nx), eigen(nx)
    sy, my = sine(ny), eigen(ny)
    eye = np.eye
    basis = legendre(P_SIZE, NL)
    fine = interp(0, n, 0, n // Q, Q)
    mean = np.kron(eye(n // Q), np.full((1, Q), 1.0 / Q))
    inside = slice(W, W + P_SIZE)
    places = [W - 1, W + P_SIZE, W, W + P_SIZE - 1]
    r = mean @ s64
    bs = basis.T @ s64[inside]
    st = s64[places]
    bl = basis.T @ fine[inside]
    lt = fine[places]
    lanes_x, lanes_y = [0, 16, 64, 80], [32, 48, 96, 112]
    sc = s64[:, inside]
    t["sc"] = pair(sc)
    t["bd"] = pair(np.kron(eye(4), sc.T))
    mu = np.zeros((16 + n, 256))
    mu[:16] = (m64.reshape(16, 4, 1) + m64).reshape(16, 256)
    mu[16:] = m64[:, None]
    t["mu"] = (mu * ((n + 1) / 2.0) ** 3).astype(np.float32)
    ty = np.zeros((4, n, 256))
    for i in range(4):
        ty[i, :, i * 16 : i * 16 + 16] = r.T
        ty[i, :, 64 + i * 16 : 64 + i * 16 + 16] = bs.T
        ty[i, :, 128 + i * 4 : 128 + i * 4 + 4] = st.T
    t["ty"] = pair(ty.reshape(4 * n, 256))
    t["tz"] = pair(np.kron(eye(4), np.concatenate([r, bs], axis=0)))
    t["tx1"] = pair(np.kron(r.T, eye(16)))
    tx2 = np.zeros((n, NL, 128))
    tx3 = np.zeros((n, 4, 128))
    kl = np.zeros((16, 16, 128))
    for i in range(4):
        at_x, at_y = slice(lanes_x[i], lanes_x[i] + NL), slice(lanes_y[i], lanes_y[i] + NL)
        tx2[:, :, at_x] = st[i][:, None, None] * eye(NL)
        kl[:, :, at_x] = lt[i][:, None, None] * bl.T[None]
        tx3[:, i, at_y] = bs.T
        kl[:, :, at_y] = bl.T[:, None, :] * lt[i][None, :, None]
    t["tx2"] = pair(tx2.reshape(n * NL, 128))
    t["tx3"] = pair(tx3.reshape(n * 4, 128))
    t["kl"] = pair(kl.reshape(256, 128))
    first = W // Q
    u1 = np.zeros((CELLS, 16))
    u2 = np.zeros((CELLS, 16))
    for k in range(CELLS):
        u1[:, k + first] += s8[:, k]
        u2[:, k + first - 1] -= s8[:, k] / (Q * Q)
        u2[:, k + first + 1] -= s8[:, k] / (Q * Q)
    t["u"] = pair(np.concatenate([u1, u2, bl], axis=0))
    beside = eye(16, k=1) + eye(16, k=-1)
    k1 = 6.0 * eye(256) - np.kron(beside, eye(16)) - np.kron(eye(16), beside)
    t["k1"] = pair(k1 / (Q * Q))
    t["yb"] = pair(np.concatenate([columns_at(sy, np.arange(16) + b * CELLS - first) for b in range(N_GY)], axis=1))
    xa = [columns_at(sx, np.arange(16) + a * CELLS - first) for a in range(N_GX)]
    xa = [np.concatenate(xa[2 * i : 2 * i + 2], axis=1).T for i in range(N_GX // 2)]
    t["xa"] = pair(np.stack([np.repeat(v, CELLS, axis=0) for v in xa]))
    scale = Q * Q * (2.0 / (nx + 1)) * (2.0 / (ny + 1)) * (2.0 / (CELLS + 1))
    wc = scale / (m8.reshape(CELLS, 1, 1) + my.reshape(1, ny, 1) + mx.reshape(1, 1, nx))
    t["wc"] = wc.reshape(CELLS * ny, nx).astype(np.float32)
    edge = interp(-1, P_SIZE + 2, -1, CELLS + 2, Q)
    ends = edge[[0, P_SIZE + 1]]
    lateral = edge[1 : P_SIZE + 1]
    depth = interp(0, P_SIZE, 0, CELLS, Q)
    around = np.arange(CELLS + 2) - 1
    near = [columns_at(sy, around + b * CELLS).T for b in range(N_GY)]
    near = [np.concatenate([v, ends @ v, np.zeros((4, ny))], axis=0) for v in near]
    ey = np.zeros((N_GY, 16, CELLS, CELLS, ny))
    for k in range(CELLS):
        ey[:, :, k, k, :] = np.stack(near)
    t["ey"] = pair(ey.reshape(N_GY, 128, CELLS * ny))
    near = [columns_at(sx, around + a * CELLS).T for a in range(N_GX)]
    near = np.stack([np.concatenate([v, ends @ v], axis=0) for v in near]).reshape(N_GX // 2, 2, 12, nx)
    t["ex"] = pair(near.transpose(1, 2, 0, 3).reshape(2, 12 * (N_GX // 2), nx))
    t["s32"] = pair(s32)
    t["bd32"] = pair(np.kron(eye(4), s32))
    rm32 = m32.reshape(8, 1, 4, 1) + m32.reshape(1, 32, 1, 1) + m32.reshape(1, 1, 1, 32)
    t["rm32"] = ((2.0 / (P_SIZE + 1)) ** 3 / rm32).reshape(256, 128).astype(np.float32)
    t["sbz"] = pair(s32 @ basis)
    lz = s32 @ depth @ s8
    lane = np.arange(128)
    t["lz"] = lz[:, lane % 8].astype(np.float32)
    sel = np.zeros((4, 128, 128), np.float32)
    for f in range(4):
        for i in range((CELLS + 2) * CELLS):
            sel[f, i, 64 + f * 16 + i // 8] = 1.0
    t["sel"] = sel.reshape(512, 128).astype(ml_dtypes.bfloat16)
    tz2 = np.zeros((128, 32, 32))
    sb, sl = s32 @ basis, s32 @ lateral
    for f, layer in enumerate([0, P_SIZE - 1]):
        near = s32[:, layer]
        for i in range(NL):
            tz2[f * 16 + i] = near[:, None] * sb[None, :, i]
            tz2[32 + f * 16 + i] = near[None, :] * sb[:, None, i]
        for i in range(CELLS + 2):
            tz2[64 + f * 16 + i] = near[:, None] * sl[None, :, i]
            tz2[96 + f * 16 + i] = near[None, :] * sl[:, None, i]
    t["tz2"] = pair(tz2.reshape(128, 1024))
    return t


WIDE = {
    "bd": (0, 128, 0, 256),
    "ty": (128, 256, 0, 256),
    "tz": (384, 128, 0, 256),
    "tx1": (512, 1024, 0, 256),
    "k1": (1536, 256, 0, 256),
    "tx2a": (1792, 512, 0, 128),
    "tx2b": (1792, 512, 128, 128),
    "tx3": (2304, 256, 0, 128),
    "kl": (2304, 256, 128, 128),
}
SMALL = {"sc|": (0, 0, 64, 0, 96), "s32|": (0, 64, 32, 0, 96), "u|": (0, 96, 32, 0, 48), "sc=": (1, 0, 64, 0, 96), "s32=": (1, 64, 32, 0, 96)}


def in_row(table):
    return np.concatenate([table[0], table[1], table[0]], axis=1)


def in_block(table):
    return np.concatenate([table[0], table[0], table[1]], axis=1)


@functools.lru_cache(None)
def packs():
    t = tables()
    small = np.zeros((2, 256, 128), ml_dtypes.bfloat16)
    for name, (which, row, rows, lane, width) in SMALL.items():
        form = in_row if name[-1] == "|" else in_block
        small[which, row : row + rows, lane : lane + width] = form(t[name[:-1]])
    small[:, 128:256] = t["bd32"]
    parts = {**t, "tx2a": t["tx2"][:, :512], "tx2b": t["tx2"][:, 512:]}
    wide = np.zeros((2, 2560, 256), ml_dtypes.bfloat16)
    for name, (row, rows, lane, width) in WIDE.items():
        wide[:, row : row + rows, lane : lane + width] = parts[name]
    later = np.zeros((2, 128, 1408), ml_dtypes.bfloat16)
    later[:, :, :1024] = t["tz2"]
    later[:, :64, 1024:1152] = t["yb"]
    later[0, 64:96, 1024:1072] = in_row(t["sbz"])
    later[:, :, 1152:] = t["sel"].reshape(2, 2, 128, 128).transpose(0, 2, 1, 3).reshape(2, 128, 256)
    scales = np.zeros((768, 256), np.float32)
    scales[:512] = t["wc"]
    scales[512:, :128] = t["rm32"]
    scales[512:544, 128:] = t["lz"]
    return {
        "small": small,
        "wide": wide,
        "mu": t["mu"],
        "xa": t["xa"],
        "ey": t["ey"],
        "ex": t["ex"],
        "later": later,
        "scales": scales,
    }


class View:
    def __init__(self, ref, row, rows, lane, width):
        self.ref, self.rows, self.lanes = ref, slice(row, row + rows), slice(lane, lane + width)
        self.shape = (2, rows, width)

    def __getitem__(self, part):
        return self.ref[slice(None) if part is Ellipsis else part, self.rows, self.lanes]


def small_table(ref, name):
    which, row, rows, lane, width = SMALL[name]
    return ref[which, row : row + rows, lane : lane + width]


def split(x):
    high = x.astype(BF16)
    return high, (x - high.astype(F32)).astype(BF16)


def dot(x, y):
    return lax.dot_general(x, y, (((1,), (0,)), ((), ())), preferred_element_type=F32)


def dot_nt(x, y):
    return lax.dot_general(x, y, (((1,), (1,)), ((), ())), preferred_element_type=F32)


def times_table(x, table):
    high, low = split(x)
    rows = x.shape[0]
    if rows > 128:
        return dot(jnp.concatenate([high, low, high], axis=1), jnp.concatenate([table[0], table[0], table[1]], axis=0))
    if rows % 16:
        return dot(high, table[0]) + dot(low, table[0]) + dot(high, table[1])
    both = dot(jnp.concatenate([high, low], axis=0), table[0])
    return both[:rows] + both[rows:] + dot(high, table[1])


def table_times(table, x, product=dot):
    high, low = split(x)
    rows = table.shape[1]
    both = product(table[...].reshape(2 * rows, table.shape[2]), high)
    return both[:rows] + both[rows:] + product(table[0], low)


def row_times(table, x):
    high, low = split(x)
    return dot(table, jnp.concatenate([high, high, low], axis=0))


def block_times_nt(table, x):
    return dot_nt(table, x)


def spread(x, rows):
    high, low = split(x)
    high, low = high.astype(F32), low.astype(F32)
    count = x.shape[0]
    for y in range(P_SIZE):
        part = slice(y * 32, y * 32 + 32)
        rows[y * (count + 1) : y * (count + 1) + count, :] = jnp.concatenate([high[:, part], low[:, part], high[:, part]], axis=1)
    found = [rows[pl.ds(k, P_SIZE, stride=count + 1), :] for k in range(count)]
    return jnp.concatenate(found, axis=0).astype(BF16)


def stacked(x, width):
    return jnp.concatenate([x[:, i : i + width] for i in range(0, x.shape[1], width)], axis=0)


def unstacked(x, rows):
    return jnp.concatenate([x[i : i + rows] for i in range(0, x.shape[0], rows)], axis=1)


def lanes(rows):
    return lax.broadcasted_iota(jnp.int32, (rows, 128), 1)


FIRST = ("mu", "wide", "small")
NEXT = ("xa", "ey", "ex", "later", "scales")
KEPT = (((2, 256, 128), BF16), ((2, 256, 256), BF16), ((2, 128, 512), BF16), ((2, 192, 256), BF16), ((2, 128, 1408), BF16), ((768, 256), F32))


def first_kernel(q_hbm, mu_hbm, wide_hbm, small_hbm, xa_hbm, ey_hbm, ex_hbm, later_hbm, scales_hbm,
                 m_ref, own_ref, spec_ref, small, xa, ey, ex, later, scales,
                 q, mu, wide, rows, rows32, sem):
    started = []

    def start(source, target):
        copy = pltpu.make_async_copy(source, target, sem.at[len(started)])
        started.append(copy)
        copy.start()
        return copy

    def part(first, last):
        return start(wide_hbm.at[:, first:last, :], wide.at[:, first:last, :])

    now = [start(q_hbm, q), start(small_hbm, small)]
    soon = [part(0, 512), start(mu_hbm, mu)]
    for copy in now:
        copy.wait()
    ahead = [
        start(scales_hbm, scales),
        start(later_hbm, later),
        start(xa_hbm.at[lax.axis_index("gs")], xa),
        start(ey_hbm.at[lax.axis_index("gy")], ey),
        start(ex_hbm.at[lax.axis_index("gc")], ex),
    ]
    late = [part(512, 1536), part(1536, 2560)]
    t = {name: View(wide, *place) for name, place in WIDE.items()}
    x = row_times(small_table(small, "sc|"), q[...])
    x = block_times_nt(small_table(small, "sc="), spread(x, rows))
    for copy in soon:
        copy.wait()
    x = times_table(stacked(x, 128), t["bd"])
    bd32 = View(small, 128, 128, 0, 128)
    y = row_times(small_table(small, "s32|"), q[...])
    y = block_times_nt(small_table(small, "s32="), spread(y, rows32))
    spec_ref[...] = times_table(stacked(y, 128), bd32)
    x = jnp.concatenate([x[i * 64 : i * 64 + 64] / (mu[16:80, :] + mu[i : i + 1, :]) for i in range(16)], axis=0)
    x = times_table(x, t["ty"])
    lane = lanes(16)
    ls, lp, ly = [], [], []
    for i in range(4):
        z = table_times(t["tz"], x[i * 256 : i * 256 + 256])
        for j in range(0, 4, 2):
            one, two = z[j * 32 : j * 32 + 32, 0:128], z[j * 32 + 32 : j * 32 + 64, 0:128]
            ls.append(jnp.where(lane < 64, one[0:16], pltpu.roll(two[0:16], 64, 1)))
            lp.append(jnp.where(lane < 64, pltpu.roll(one[16:32], 64, 1), two[16:32]))
        for j in range(4):
            k = (i * 4 + j) % 8
            one = z[j * 32 + 16 : j * 32 + 32, 128:256]
            ly.append(pltpu.roll(one, 16 * k, 1) if k else one)
    ls, lp = jnp.concatenate(ls, axis=1), jnp.concatenate(lp, axis=1)
    ly = jnp.concatenate([sum(ly[1:8], ly[0]), sum(ly[9:16], ly[8])], axis=1)
    for copy in late:
        copy.wait()
    samples = times_table(ls, t["tx1"])
    coefs = times_table(lp[:, 0:512], t["tx2a"]) + times_table(lp[:, 512:1024], t["tx2b"]) + times_table(ly, t["tx3"])
    x = row_times(small_table(small, "u|"), samples)
    coefs = coefs - times_table(x[16:32], t["kl"])
    own_ref[...] = coefs
    x = (times_table(x[0:8], t["k1"]) + x[8:16]).T
    spilled = jnp.concatenate([x[i * 16 : i * 16 + 16] for i in range(16)], axis=1)
    tile = jnp.zeros((8, 128), F32)
    for i in range(8):
        value = coefs[i % 2 * 8 : i % 2 * 8 + 8]
        shift = (16 * i - 64 - i // 2 * 16) % 128
        tile = jnp.where(lanes(8) // 16 == i, pltpu.roll(value, shift, 1) if shift else value, tile)
    for i in range(16):
        m_ref[i * 24 : i * 24 + 16, :] = spilled
        m_ref[i * 24 + 16 : i * 24 + 24, :] = tile
    for copy in ahead:
        copy.wait()


def unpacked(tile, source, slot):
    parts = []
    for half in range(2):
        shift = (16 * slot - source - 16 * half) % 128
        parts.append(pltpu.roll(tile, shift, 1) if shift else tile)
    return jnp.where(lanes(NL) // 16 == slot, jnp.concatenate(parts, axis=0), 0.0)


def strip_kernel(got_ref, own_ref, xa, ey, ex, later, scales, m_ref, coefs_ref):
    s, c, b = lax.axis_index("gs"), lax.axis_index("gc"), lax.axis_index("gy")
    source = [
        jnp.concatenate([got_ref[(i * 8 + j) * 24 : (i * 8 + j) * 24 + 16, :] for j in range(N_GY)], axis=0)
        for i in range(2)
    ]
    x = table_times(View(later, 0, 64, 1024, 128), jnp.concatenate(source, axis=1))
    lane = lax.broadcasted_iota(jnp.int32, (64, 256), 1)
    x = jnp.concatenate([jnp.where(lane % 8 == k, x, 0.0) for k in range(CELLS)], axis=0)
    x = times_table(x, xa) * scales[0:512, :]
    x = table_times(ey, x)
    x = table_times(ex, x, dot_nt)

    def tile_of(i, j):
        return got_ref[pl.ds(pl.multiple_of((i * 8 + j) * 24 + 16, 8), 8), :]

    partner = tile_of(1 - c, b)
    outside = jnp.where(c == 0, pltpu.roll(partner, 64, 1), pltpu.roll(partner, 96, 1))
    outside = jnp.where(lanes(8) >= 96, outside, 0.0)
    fifth = outside[7:8]
    for j in range(3):
        fifth = fifth + pltpu.roll(outside, 32 * j + 32, 1)[4 + j : 5 + j]
    hit = lax.broadcasted_iota(jnp.int32, (16, 128), 0) == s + 1 - 2 * c
    lane = lanes(16)
    for f in range(2):
        value = jnp.where(lane < 80, x[160 + f * 16 : 176 + f * 16], 0.0)
        m_ref[pl.ds(f, 16, stride=5), :] = value + jnp.where(hit, outside[f : f + 1], 0.0)
        value = jnp.zeros((16, 128), F32)
        for k in range(CELLS + 2):
            part = pltpu.roll(x[k * 16 : k * 16 + 16], (8 * (k - 10 - f)) % 128, 1)
            value = jnp.where(lane // 8 == k, part, value)
        m_ref[pl.ds(2 + f, 16, stride=5), :] = value + jnp.where(hit, outside[2 + f : 3 + f], 0.0)
    m_ref[pl.ds(4, 16, stride=5), :] = jnp.where(hit, fifth, 0.0)
    coefs = jnp.where(lane < 64, own_ref[...], 0.0)
    coefs = coefs + jnp.where(c == 0, unpacked(partner, 0, 1), unpacked(partner, 32, 0))
    above = unpacked(tile_of(c, jnp.minimum(b + 1, N_GY - 1)), 64, 3)
    below = unpacked(tile_of(c, jnp.maximum(b - 1, 0)), 96, 2)
    coefs = coefs + jnp.where(b < N_GY - 1, above, 0.0) + jnp.where(b > 0, below, 0.0)
    coefs_ref[...] = coefs


def last_kernel(m_ref, coefs_ref, spec_ref, small, later, scales, out_ref, rows):
    s32, bd32 = small_table(small, "s32|"), View(small, 128, 128, 0, 128)
    got = [jnp.sum(m_ref[pl.ds(i, 16, stride=5), :], axis=0, keepdims=True) for i in range(5)]
    tile = got[:4] + [pltpu.roll(got[4], 96 - 32 * j, 1) if j < 3 else got[4] for j in range(4)]
    tile = jnp.concatenate(tile, axis=0)
    coefs = coefs_ref[...] + jnp.where(lax.axis_index("gc") == 0, unpacked(tile, 96, 0), unpacked(tile, 96, 1))
    lz = scales[512:544, 128:256]
    high, low = split(jnp.concatenate([lz * got[i] for i in range(4)], axis=1))
    x = row_times(later[0, 64:96, 1024:1072], coefs)
    for i in range(4):
        part = jnp.concatenate([high[:, i * 128 : i * 128 + 128], low[:, i * 128 : i * 128 + 128]], axis=0)
        part = dot(part, later[i // 2, :, 1152 + i % 2 * 128 : 1280 + i % 2 * 128])
        x = x + part[:32] + part[32:]
    x = times_table(x, View(later, 0, 128, 0, 1024))
    x = (stacked(x, 128) + spec_ref[...]) * scales[512:768, 0:128]
    x = row_times(s32, unstacked(x, 32))
    x = times_table(stacked(x, 128), bd32)
    for i in range(8):
        turned = x[i * 32 : i * 32 + 32].T
        for j in range(4):
            rows[(i * 4 + j) * 33 : (i * 4 + j) * 33 + 32, :] = turned[j * 32 : j * 32 + 32]
    x = jnp.concatenate([rows[pl.ds(y, 32, stride=P_SIZE + 1), :] for y in range(P_SIZE)], axis=1)
    out_ref[...] = row_times(s32, x)


def vmem(count):
    return [pl.BlockSpec(memory_space=pltpu.VMEM)] * count


def hbm(count):
    return [pl.BlockSpec(memory_space=pltpu.HBM)] * count


def shape(*dims):
    return jax.ShapeDtypeStruct(dims, F32)


def params(mib):
    return pltpu.CompilerParams(vmem_limit_bytes=mib * 1024 * 1024)


def body(charge):
    t = {k: pltpu.with_memory_space_constraint(jnp.asarray(v), pltpu.HBM) for k, v in packs().items()}
    message, own, spec, small, xa, ey, ex, later, scales = pl.pallas_call(
        first_kernel,
        out_shape=[shape(384, 128), shape(NL, 128), shape(256, 128)] + [jax.ShapeDtypeStruct(*k) for k in KEPT],
        in_specs=hbm(1 + len(FIRST) + len(NEXT)),
        out_specs=vmem(3 + len(KEPT)),
        scratch_shapes=[
            pltpu.VMEM((32, 1024), F32),
            pltpu.VMEM((80, 256), F32),
            pltpu.VMEM((2, 2560, 256), BF16),
            pltpu.VMEM((2080, 96), F32),
            pltpu.VMEM((1056, 96), F32),
            pltpu.SemaphoreType.DMA((11,)),
        ],
        compiler_params=params(24),
        name="first",
    )(pltpu.with_memory_space_constraint(charge, pltpu.HBM), *[t[k] for k in FIRST + NEXT])
    strip = lax.all_to_all(message.reshape(16, 24, 128), ("gc", "gy"), 0, 0).reshape(384, 128)
    message, coefs = pl.pallas_call(
        strip_kernel,
        out_shape=(shape(80, 128), shape(NL, 128)),
        in_specs=vmem(7),
        out_specs=tuple(vmem(2)),
        compiler_params=params(12),
        name="strip",
    )(strip, own, xa, ey, ex, later, scales)
    arrived = lax.all_to_all(message.reshape(16, 1, 640), "gs", 0, 0).reshape(80, 128)
    return pl.pallas_call(
        last_kernel,
        out_shape=shape(32, 1024),
        in_specs=vmem(6),
        out_specs=vmem(1)[0],
        scratch_shapes=[pltpu.VMEM((1056, 32), F32)],
        compiler_params=params(12),
        name="last",
    )(arrived, coefs, spec, small, later, scales)


def solution(mesh):
    strips = jax.sharding.Mesh(mesh.devices.reshape(N_GX // 2, 2, N_GY), ("gs", "gc", "gy"))
    spec = P(("gs", "gc"), "gy")
    return jax.shard_map(body, mesh=strips, in_specs=(spec,), out_specs=spec, check_vma=False)
```
